32 devices in a mesh: front: 4 (over y, core), blk: 8 (over z, x).
Axes of the slice: x: 2, y: 2, z: 4, core: 2. Of those that a mesh axis runs over, the one named last changes fastest.
Arguments:
- front: float32 [12288, 3072], P('front', 'blk'), may hold values from -8 to 96, as said below
- parent_group: int32 [4, 8, 6, 1], P('front', 'blk'), may hold values from 0 to 3; in each aligned block of 6 rows (0 to 5, 6 to 11, ..., all dimensions but the last counted through in order) at most 2 rows name the same one
- row_block: int32 [4, 8, 6], P('front', 'blk'), may hold values from 0 to 7
- parent_base: float32 [4096, 3072], P('front', 'blk'), may hold values from -6 to 6
Outputs:
- factored: float32 [12288, 3072], P('front', 'blk')
- assembled: float32 [4096, 3072], P('front', 'blk')
The draws below stay inside these ranges and needn't reach their ends.
Inputs may be any that keep to these rules, and one draw needn't show every extreme that they name: `parent_group`: in the 6 blocks of one device no group is named more than 2 times. `front`: diagonal entries at indices pivotal at some tick lie between 48 and 96; every other entry lies within 8 of zero.
All inputs are finite; a program needn't handle non-finite values.
Results may differ from the reference program's by a relative error of at most 0.003.
Values may be sent and summed in bfloat16 or wider, within the bound.
No kernel may reach another device: no remote copies, remote signals or barrier semaphores. Data moves between devices by JAX's collectives and lax.ppermute only.
A program may use at most 128 MiB of HBM per device.

```python
import math
import jax
import jax.numpy as jnp
import numpy as np
from jax import lax

SLAB = 384
P_SIZE = 256
ROOT_P = 16
TICKS = 5
NEWTON = 2
RB = 128
NB = 6
CAP = 2
ASM_BLOCKS = 8
GROUPS = 4
SLABS = 8
F = 3072
ASM_ROWS = 1024


def draw_front(key, part):
    first, second = jax.random.split(jax.random.fold_in(key, 11))
    spread = jnp.clip(jax.random.normal(first, (GROUPS, F, F), jnp.float32), -6.0, 6.0)
    index = jnp.arange(F)
    pivotal = (index % SLAB < P_SIZE) & (index // SLAB < TICKS)
    factor = jnp.exp(jax.random.uniform(second, (GROUPS, F), jnp.float32, 0.0, math.log(2.0)))
    diagonal = 3.0 * ROOT_P * factor
    select = (index[:, None] == index[None, :]) & pivotal[None, :]
    matrix = jnp.where(select[None, :, :], diagonal[:, None, :], spread)
    return matrix.reshape(GROUPS * F, F).astype(jnp.float32)


def set_ends(array, own_key, low, largest):
    dims = array.shape
    spot = [jax.random.randint(jax.random.fold_in(own_key, axis), (), 0, dims[axis]) for axis in range(len(dims))]
    array = array.at[tuple(spot)].set(low)
    longest = dims.index(max(dims))
    spot[longest] = (spot[longest] + 1) % dims[longest]
    return array.at[tuple(spot)].set(largest)


def block_scale(stream_key, shape, cuts, smallest, largest):
    loudness, own = 1.0, jax.random.fold_in(stream_key, 6)
    for position, shards_of in cuts:
        draws = jnp.exp(jax.random.uniform(jax.random.fold_in(own, position), (shards_of,), jnp.float32, smallest / len(cuts), largest / len(cuts)))
        loudness = loudness * jnp.repeat(draws, shape[position] // shards_of).reshape([-1 if axis == position else 1 for axis in range(len(shape))])
    return loudness


def routed_block(own_key, own, number, rows, number_of, top, most, skew):
    sequence = jax.random.permutation(own_key, number_of)
    crowded, common = portions_of(number_of, rows * top, most, skew, True), portions_of(number_of, rows * top, most, skew, False)
    places = jnp.arange(number_of)

    def named(tallies, offset_by):
        used = int((tallies > 0).sum())
        fixed = max(1, used // 4)
        passed = fixed + (places - fixed + offset_by * (used - fixed)) % max(1, number_of - fixed)
        return jnp.zeros((number_of,), jnp.int32).at[sequence[jnp.where(places < fixed, places, passed)]].set(jnp.asarray(tallies, jnp.int32))

    tallies = jnp.where(number % 4 == 0, named(crowded, number // 4), named(common, number - number // 4 - 1))
    mixed = jax.random.permutation(jax.random.fold_in(own, 3), number_of)
    donor, sink = mixed[0:number_of // 2 * 2:2], mixed[1:number_of // 2 * 2:2]
    room = jnp.minimum(tallies[donor] - 1, most - tallies[sink]) // 2
    room = jnp.where((donor == sequence[0]) | (sink == sequence[0]) | (tallies[sink] == 0), 0, jnp.maximum(room, 0))
    passed = jax.random.randint(jax.random.fold_in(own, 4), (number_of // 2,), 0, 1 << 20) % (room + 1)
    tallies = tallies.at[donor].add(-passed).at[sink].add(passed)
    members = jnp.searchsorted(jnp.cumsum(tallies), jnp.arange(rows * top), side="right").astype(jnp.int32)
    listing = members.reshape(top, rows).T
    listing = listing[jax.random.permutation(jax.random.fold_in(own, 1), rows)]
    offset_by = jax.random.randint(jax.random.fold_in(own, 2), (rows, 1), 0, top)
    return jnp.take_along_axis(listing, (jnp.arange(top)[None, :] + offset_by) % top, axis=1)


def portions_of(count, total, limit, lean, full):
    weights = [(1 << 20) // math.isqrt(standing ** lean) + 1 for standing in range(1, count + 1)]
    largest = limit if full else min(limit, max(-(-total // count), total * weights[0] // sum(weights)))
    least = 1 if total - largest >= count - 1 else 0
    holding, spare = [largest] + [least] * (count - 1), total - largest - least * (count - 1)
    while spare > 0:
        free = [i for i in range(1, count) if holding[i] < largest] or [i for i in range(1, count) if holding[i] < limit]
        pool, remaining = sum([weights[i] for i in free]), spare
        for i in free:
            more = min(limit - holding[i], max(1, remaining * weights[i] // pool), spare)
            holding[i] = holding[i] + more
            spare = spare - more
    return np.array(holding)


def noise(key, shape, deviation, most, shards=(), kind=jnp.bfloat16):
    result = deviation * jax.random.normal(key, shape, jnp.float32)
    if shards:
        result = result * block_scale(key, shape, shards, -0.22, 0.18)
    return jnp.clip(result, -most, most).astype(kind)


def setup_inputs(seed: int = 0) -> dict:
    key_list = jax.random.split(jax.random.key(seed), 5)
    front = draw_front(jax.random.fold_in(key_list[4], 71), 0)
    parent_group_keys = jax.random.split(jax.random.fold_in(key_list[1], 1), GROUPS * SLABS * NB // NB)
    parent_group_turns = jax.random.permutation(jax.random.fold_in(key_list[1], 3), GROUPS * SLABS * NB // NB)
    parent_group = jax.vmap(lambda own, number: routed_block(jax.random.fold_in(key_list[1], 2), own, number, NB, GROUPS, 1, CAP, 2))(parent_group_keys, parent_group_turns).reshape((GROUPS, SLABS, NB, 1))
    row_block = set_ends(jax.random.randint(key_list[2], (GROUPS, SLABS, NB), 0, ASM_BLOCKS), jax.random.fold_in(key_list[2], 1), 0, ASM_BLOCKS - 1).astype(jnp.int32)
    parent_base = noise(key_list[3], (GROUPS * ASM_ROWS, F), 1.0, 6.0, ((0, 4), (1, 8)), jnp.float32)
    return {"front": front, "parent_group": parent_group, "row_block": row_block, "parent_base": parent_base}


def newton_inverse(block):
    inverse = jnp.diag(1.0 / jnp.diagonal(block))
    ident = jnp.eye(block.shape[0], dtype=block.dtype)
    for step in range(NEWTON):
        inverse = jnp.dot(inverse, 2.0 * ident - jnp.dot(block, inverse, precision=lax.Precision.HIGHEST), precision=lax.Precision.HIGHEST)
    return inverse


def factor_front(matrix):
    order = matrix.shape[0]
    index = jnp.arange(order)
    pivotal = index % SLAB < P_SIZE
    for tick in range(TICKS):
        start = tick * SLAB
        live = jnp.logical_not(pivotal & (index // SLAB <= tick))
        inverse = newton_inverse(matrix[start:start + P_SIZE, start:start + P_SIZE])
        mult = jnp.dot(matrix[:, start:start + P_SIZE], inverse, precision=lax.Precision.HIGHEST)
        mult = mult * live[:, None].astype(matrix.dtype)
        panel = mult.astype(jnp.bfloat16)
        urows = matrix[start:start + P_SIZE, :].astype(jnp.bfloat16)
        change = jnp.dot(panel, urows, preferred_element_type=jnp.float32)
        matrix = matrix - change * live[None, :].astype(matrix.dtype)
        matrix = matrix.at[:, start:start + P_SIZE].set(jnp.where(live[:, None], mult, matrix[:, start:start + P_SIZE]))
    return matrix


def reference(front, parent_group, row_block, parent_base):
    fronts = front.reshape(GROUPS, F, F)
    factored = lax.map(factor_front, fronts)
    index = jnp.arange(F)
    keep = jnp.logical_not((index % SLAB < P_SIZE) & (index // SLAB < TICKS))
    tail = factored[:, F - NB * RB:, :] * keep[None, None, :].astype(factored.dtype)
    cont = lax.optimization_barrier(tail.astype(jnp.bfloat16)).astype(jnp.float32)
    cont = cont.reshape(GROUPS, NB, RB, SLABS, SLAB)
    dest = parent_group[..., 0]
    to_group = dest[..., None] == jnp.arange(GROUPS, dtype=jnp.int32)
    to_block = row_block[..., None] == jnp.arange(ASM_BLOCKS, dtype=jnp.int32)
    route = (to_group[..., :, None] & to_block[..., None, :]).astype(jnp.float32)
    added = jnp.einsum("gbipo,girbc->porbc", route, cont)
    base = parent_base.reshape(GROUPS, ASM_BLOCKS, RB, SLABS, SLAB)
    assembled = (base + added).reshape(GROUPS * ASM_ROWS, F)
    return factored.reshape(GROUPS * F, F), assembled
```

```python
import functools

import jax
import jax.numpy as jnp
from jax import lax
from jax.experimental import pallas as pl
from jax.experimental.pallas import tpu as pltpu
from jax.sharding import PartitionSpec as P

P_SIZE = 256
TICKS = 5
NEWTON = 2
RB = 128
NB = 6
CAP = 2
ASM_BLOCKS = 8
ROW_TILE = 128
HIGH = lax.Precision.HIGHEST
ANY = pl.BlockSpec(memory_space=pl.ANY)
SMEM = pl.BlockSpec(memory_space=pltpu.SMEM)
VMEM = pl.BlockSpec(memory_space=pltpu.VMEM)


def after(values, done):
    return lax.optimization_barrier((values, done))[0]


def permute(value, pairs):
    return lax.ppermute(value, "blk", pairs)


def start_halves(own, member):
    half = own.shape[0] // 2
    moved = permute(own[half:], [(4, 5)])
    return jnp.where(member == 5, moved, own[:half])


def relay(segments, member):
    across = [(m, m ^ 1) for m in range(8)]
    near = [(m, m ^ 2) for m in range(8)]
    distant = [(m, m + 4) for m in range(4)]
    level = member // 2
    a, b, c = segments
    rest = jnp.concatenate([b, c], axis=0)

    first = permute(a, distant)
    half_a = start_halves(a, member)
    half_n = start_halves(rest, member)
    cur_a = jnp.where(member < 4, a, first)

    b1, ha, hn = after((b, half_a, half_n), first)
    cur_a = after(cur_a, half_a)
    far_a = permute(cur_a, near)
    over_a = permute(cur_a, across)
    back_a = permute(ha, [(4, 0), (5, 1)])
    first_b = permute(b1, distant)
    back_n = permute(hn, [(4, 0), (5, 1)])
    ha = jnp.where(level == 0, back_a, half_a)
    hn = jnp.where(level == 0, back_n, half_n)
    cur_b = jnp.where(member < 4, b, first_b)

    c1, cur_b, ha, hn, fa = after((c, cur_b, ha, hn, far_a), (far_a, over_a, first_b))
    spread = [(0, 2), (1, 3), (4, 6), (5, 7)]
    far_b = permute(cur_b, near)
    first_c = permute(c1, distant)
    overfar_a = permute(fa, across)
    spread_a = permute(ha, spread)
    over_b = permute(cur_b, across)
    spread_n = permute(hn, spread)
    ha = jnp.where(level % 2 == 1, spread_a, ha)
    hn = jnp.where(level % 2 == 1, spread_n, hn)
    cur_c = jnp.where(member < 4, c, first_c)

    cur_c, ha, hn, fb = after((cur_c, ha, hn, far_b), (far_b, first_c, overfar_a))
    overha = permute(ha, across)
    far_c = permute(cur_c, near)
    overfar_b = permute(fb, across)
    overhn = permute(hn, across)
    over_c = permute(cur_c, across)

    fc = after(far_c, (overfar_b, over_c))
    overfar_c = permute(fc, across)
    return (
        (cur_a, far_a, over_a, overfar_a, ha, overha),
        (cur_b, far_b, over_b, overfar_b, hn, overhn),
        (cur_c, far_c, over_c, overfar_c, hn, overhn),
    )


def fetch_relayed(member, refs, target, sems, first_row, total_rows, rows):
    cur, far, over, overfar, half, overhalf = refs
    x = lax.rem(member, 2)
    even = lax.rem(lax.div(member, 2), 2) == 0
    places = (
        (cur, jnp.where(even, x, 2 + x)),
        (far, jnp.where(even, 2 + x, x)),
        (over, jnp.where(even, 1 - x, 3 - x)),
        (overfar, jnp.where(even, 3 - x, 1 - x)),
    )
    copies = [
        pltpu.make_async_copy(ref, target.at[slab], sems.at[i]) for i, (ref, slab) in enumerate(places)
    ]
    for copy in copies:
        copy.start()
    split = total_rows // 2
    low = max(0, min(rows, split - first_row))
    pieces = []
    if low:
        pieces.append((0, first_row, 0, low))
    if rows - low:
        pieces.append((1, first_row + low - split, low, rows - low))
    for which in (0, 1):
        mine, other = (half, overhalf) if which == 0 else (overhalf, half)

        @pl.when(x == which)
        def _(mine=mine, other=other):
            for number, (part, source, to, count) in enumerate(pieces):
                ref = mine if part == 0 else other
                pltpu.make_async_copy(
                    ref.at[pl.ds(source, count)],
                    target.at[TICKS - 1, pl.ds(to, count)],
                    sems.at[4 + number],
                ).start()

    def wait():
        for copy in copies:
            copy.wait()
        for number, (part, source, to, count) in enumerate(pieces):
            pltpu.make_async_copy(
                half.at[pl.ds(source, count)],
                target.at[TICKS - 1, pl.ds(to, count)],
                sems.at[4 + number],
            ).wait()

    return wait


def fetch_gathered(member, refs, target, sems, first_row, total_rows, rows):
    copy = pltpu.make_async_copy(refs[0], target, sems.at[0])
    copy.start()
    return copy.wait


def diagonal_inverse(block):
    size = block.shape[0]
    row = lax.broadcasted_iota(jnp.int32, (size, size), 0)
    col = lax.broadcasted_iota(jnp.int32, (size, size), 1)
    on = row == col
    kept = jnp.where(on, block, 0.0)
    down = 1.0 / jnp.sum(kept, axis=1, keepdims=True)
    right = 1.0 / jnp.sum(kept, axis=0, keepdims=True)
    twice = jnp.where(on, 2.0, 0.0)
    inverse = down * (twice - block * right)
    for step in range(NEWTON - 1):
        inner = twice - jnp.dot(block, inverse, precision=HIGH, preferred_element_type=jnp.float32)
        inverse = jnp.dot(inverse, inner, precision=HIGH, preferred_element_type=jnp.float32)
    return inverse


def pivot_kernel(fetch, n_bufs, width, member_ref, front, *rest):
    bufs = rest[:n_bufs]
    out, w_out, raw, mat, own, inv, sems, own_sems = rest[n_bufs:]
    member = member_ref[0]
    p, rows = P_SIZE, TICKS * P_SIZE
    loads = [
        pltpu.make_async_copy(
            front.at[pl.ds(t * width, p), :], own.at[pl.ds(t * p, p), :], own_sems.at[t]
        )
        for t in range(TICKS)
    ]
    for load in loads:
        load.start()
    wait = fetch(member, bufs, raw, sems, 0, rows, rows)
    wait()
    for load in loads:
        load.wait()
    for s in range(TICKS):
        mat[s] = raw[s].astype(jnp.float32)
    for t in range(TICKS):
        lo, below = t * p, (t + 1) * p
        x = diagonal_inverse(mat[t, lo:below, :])
        inv[t] = x
        if below < rows:
            mult = jnp.dot(mat[t, below:, :], x, precision=HIGH, preferred_element_type=jnp.float32)
            panel = mult.astype(jnp.bfloat16)
            for s in range(t + 1, TICKS):
                mat[s, below:, :] = mat[s, below:, :] - jnp.dot(
                    panel, mat[s, lo:below, :].astype(jnp.bfloat16), preferred_element_type=jnp.float32
                )
            urows = own[lo:below, :].astype(jnp.bfloat16)
            own[below:, p:] = own[below:, p:] - jnp.dot(
                panel, urows[:, p:], preferred_element_type=jnp.float32
            )

            @pl.when((member >= TICKS) | (member > t))
            def _():
                own[below:, :p] = own[below:, :p] - jnp.dot(
                    panel, urows[:, :p], preferred_element_type=jnp.float32
                )

            @pl.when(member == t)
            def _():
                own[below:, :p] = jnp.dot(
                    own[below:, :p], x, precision=HIGH, preferred_element_type=jnp.float32
                )

    stores = [
        pltpu.make_async_copy(
            own.at[pl.ds(t * p, p), :], out.at[pl.ds(t * width, p), :], own_sems.at[t]
        )
        for t in range(TICKS)
    ]
    for store in stores:
        store.start()
    row = lax.broadcasted_iota(jnp.int32, (p, width), 0)
    col = lax.broadcasted_iota(jnp.int32, (p, width), 1)
    owner = (member < TICKS) & (col < p)
    for t in reversed(range(TICKS)):
        lo, hi = t * p, (t + 1) * p
        unit = jnp.where((row == col) & (member == t), -1.0, 0.0)
        side = jnp.where(owner, unit, own[lo:hi, :])
        for s in range(t + 1, TICKS):
            side = side - jnp.dot(
                mat[s, lo:hi, :].astype(jnp.bfloat16),
                w_out[s * p : (s + 1) * p, :],
                preferred_element_type=jnp.float32,
            )
        w_out[lo:hi, :] = jnp.dot(
            inv[t], side, precision=HIGH, preferred_element_type=jnp.float32
        ).astype(jnp.bfloat16)
    for store in stores:
        store.wait()


def pivot_rows(fetch, member, front, bufs):
    order, width = front.shape
    p, rows = P_SIZE, TICKS * P_SIZE
    return pl.pallas_call(
        functools.partial(pivot_kernel, fetch, len(bufs), width),
        name="pivot_rows",
        out_shape=(
            jax.ShapeDtypeStruct((order, width), jnp.float32),
            jax.ShapeDtypeStruct((rows, width), jnp.bfloat16),
        ),
        in_specs=[SMEM, ANY] + [ANY] * len(bufs),
        out_specs=(ANY, VMEM),
        scratch_shapes=[
            pltpu.VMEM((TICKS, rows, p), jnp.bfloat16),
            pltpu.VMEM((TICKS, rows, p), jnp.float32),
            pltpu.VMEM((rows, width), jnp.float32),
            pltpu.VMEM((TICKS, p, p), jnp.float32),
            pltpu.SemaphoreType.DMA((6,)),
            pltpu.SemaphoreType.DMA((TICKS,)),
        ],
    )(member, front, *bufs)


def other_kernel(fetch, n_bufs, ranges, first_row, total_rows, tail, member_ref, w, front, out_in, *rest):
    bufs = rest[:n_bufs]
    if tail:
        out, cont, raw, base, sems, base_sems = rest[n_bufs:]
    else:
        out, raw, base, sems, base_sems = rest[n_bufs:]
    member = member_ref[0]
    rows, width = base.shape
    loads = [
        pltpu.make_async_copy(front.at[pl.ds(src, n), :], base.at[pl.ds(dst, n), :], base_sems.at[i])
        for i, (src, dst, n) in enumerate(ranges)
    ]
    for load in loads:
        load.start()
    wait = fetch(member, bufs, raw, sems, first_row, total_rows, rows)
    wait()
    for load in loads:
        load.wait()
    keep = (member >= TICKS) | (lax.broadcasted_iota(jnp.int32, (ROW_TILE, width), 1) >= P_SIZE)

    def tile(i, carry):
        at = pl.ds(pl.multiple_of(i * ROW_TILE, ROW_TILE), ROW_TILE)
        total = jnp.where(keep, base[at, :], 0.0)
        for s in range(TICKS):
            total = total - jnp.dot(
                raw[s, at, :], w[s * P_SIZE : (s + 1) * P_SIZE, :], preferred_element_type=jnp.float32
            )
        base[at, :] = total
        if tail:
            cont[at, :] = jnp.where(keep, total, 0.0).astype(jnp.bfloat16)
        return carry

    lax.fori_loop(0, rows // ROW_TILE, tile, 0)
    stores = [
        pltpu.make_async_copy(base.at[pl.ds(dst, n), :], out.at[pl.ds(src, n), :], base_sems.at[i])
        for i, (src, dst, n) in enumerate(ranges)
    ]
    for store in stores:
        store.start()
    for store in stores:
        store.wait()


def other_rows(fetch, member, w, front, out, bufs, ranges, first_row, total_rows, tail):
    order, width = front.shape
    rows = sum(n for _, _, n in ranges)
    shapes = [jax.ShapeDtypeStruct((order, width), jnp.float32)]
    specs = [ANY]
    if tail:
        shapes.append(jax.ShapeDtypeStruct((rows, width), jnp.bfloat16))
        specs.append(VMEM)
    return pl.pallas_call(
        functools.partial(other_kernel, fetch, len(bufs), ranges, first_row, total_rows, tail),
        name="tail_rows" if tail else "middle_rows",
        out_shape=tuple(shapes),
        in_specs=[SMEM, VMEM, ANY, ANY] + [ANY] * len(bufs),
        out_specs=tuple(specs),
        input_output_aliases={3: 0},
        scratch_shapes=[
            pltpu.VMEM((TICKS, rows, P_SIZE), jnp.bfloat16),
            pltpu.VMEM((rows, width), jnp.float32),
            pltpu.SemaphoreType.DMA((6,)),
            pltpu.SemaphoreType.DMA((len(ranges),)),
        ],
    )(member, w, front, out, *bufs)


def assemble(cont, parent_group, row_block, parent_base):
    width = parent_base.shape[1]
    groups = lax.axis_size("front")
    cont = cont.reshape(NB, RB, width)
    dest = parent_group.reshape(NB)
    target_block = row_block.reshape(NB)
    offset_hot = (target_block[:, None] == jnp.arange(ASM_BLOCKS, dtype=jnp.int32)[None, :]).astype(
        jnp.bfloat16
    )
    number = jnp.arange(NB)
    earlier = (dest[None, :] == dest[:, None]) & (number[None, :] < number[:, None])
    slot = jnp.sum(earlier.astype(jnp.int32), axis=1)
    pick = (dest[None, None, :] == jnp.arange(groups, dtype=jnp.int32)[:, None, None]) & (
        slot[None, None, :] == jnp.arange(CAP, dtype=jnp.int32)[None, :, None]
    )
    pick = pick.astype(jnp.bfloat16)
    outgoing = jnp.einsum("gci,irk->gcrk", pick, cont, preferred_element_type=jnp.float32).astype(
        jnp.bfloat16
    )
    address = jnp.einsum(
        "gci,ia->gca", pick, offset_hot, preferred_element_type=jnp.float32
    ).astype(jnp.bfloat16)
    incoming = lax.all_to_all(outgoing, "front", split_axis=0, concat_axis=0, tiled=True)
    received_address = lax.all_to_all(address, "front", split_axis=0, concat_axis=0, tiled=True)
    added = jnp.einsum(
        "gca,gcrk->ark", received_address, incoming, preferred_element_type=jnp.float32
    )
    return parent_base + added.reshape(ASM_BLOCKS * RB, width)


def local(front, parent_group, row_block, parent_base):
    order, width = front.shape
    member = lax.axis_index("blk")
    holder = member.reshape(1).astype(jnp.int32)
    p, top = P_SIZE, TICKS * width
    tail_n = NB * RB
    tail_at = order - tail_n
    slabs = front[:top].reshape(TICKS, width, width)
    own_p = slabs[:, :p, :p].reshape(TICKS * p, p).astype(jnp.bfloat16)
    own_t = front[tail_at:, :p].astype(jnp.bfloat16)
    own_m = jnp.concatenate(
        [slabs[:, p:, :p].reshape(TICKS * (width - p), p), front[top:tail_at, :p]], axis=0
    ).astype(jnp.bfloat16)
    middle = [(t * width + p, t * (width - p), width - p) for t in range(TICKS)]
    if tail_at > top:
        middle.append((top, TICKS * (width - p), tail_at - top))
    segments = (own_p, own_t, own_m)
    if lax.axis_size("blk") == 8:
        fetch = fetch_relayed
        sets = relay(segments, member)
    else:
        fetch = fetch_gathered
        sets = tuple((lax.all_gather(s, "blk")[:TICKS],) for s in segments)
    rest = own_t.shape[0] + own_m.shape[0]
    out, w = pivot_rows(fetch, holder, front, sets[0])
    out, cont = other_rows(
        fetch, holder, w, front, out, sets[1], [(tail_at, 0, tail_n)], 0, rest, True
    )
    assembled = assemble(cont, parent_group, row_block, parent_base)
    (factored,) = other_rows(fetch, holder, w, front, out, sets[2], middle, tail_n, rest, False)
    return (factored, assembled)


def solution(mesh):
    placed = (
        P("front", "blk"),
        P("front", "blk", None, None),
        P("front", "blk", None),
        P("front", "blk"),
    )
    return jax.shard_map(
        local,
        mesh=mesh,
        in_specs=placed,
        out_specs=(P("front", "blk"), P("front", "blk")),
        check_vma=False,
    )
```

```python
import functools

import jax
import jax.numpy as jnp
from jax import lax
from jax.experimental import pallas as pl
from jax.experimental.pallas import tpu as pltpu
from jax.sharding import PartitionSpec as P


P_SIZE = 256
TICKS = 5
NEWTON = 2
RB = 128
NB = 6
CAP = 2
ASM_BLOCKS = 8
ROW_TILE = 128
HIGH = lax.Precision.HIGHEST
ANY = pl.BlockSpec(memory_space=pl.ANY)
SMEM = pl.BlockSpec(memory_space=pltpu.SMEM)
VMEM = pl.BlockSpec(memory_space=pltpu.VMEM)


def permute(value, pairs):
    return lax.ppermute(value, "blk", pairs)


def relay(segments, member):
    across = [(m, m ^ 1) for m in range(8)]
    near = [(m, m ^ 2) for m in range(8)]
    distant = [(m, m + 4) for m in range(4)]
    beside, back = [(4, 5)], [(4, 0), (5, 1)]
    spread = [(0, 2), (1, 3), (4, 6), (5, 7)]
    level = member // 2

    def slabs(own):
        cur = jnp.where(member < 4, own, permute(own, distant))
        far = permute(cur, near)
        over = permute(cur, across)
        return cur, far, over, permute(far, across)

    def halves(own):
        n = own.shape[0] // 2
        half = jnp.where(member == 5, permute(own[n:], beside), own[:n])
        half = jnp.where(level == 0, permute(half, back), half)
        half = jnp.where(level % 2 == 1, permute(half, spread), half)
        return half, permute(half, across)

    a, b, c = segments
    early = halves(jnp.concatenate([a, b], axis=0))
    late = halves(c)
    return slabs(a) + early, slabs(b) + early, slabs(c) + late


def fetch_relayed(member, refs, target, sems, first_row, total_rows, rows):
    cur, far, over, overfar, half, overhalf = refs
    x = lax.rem(member, 2)
    even = lax.rem(lax.div(member, 2), 2) == 0
    places = (
        (cur, jnp.where(even, x, 2 + x)),
        (far, jnp.where(even, 2 + x, x)),
        (over, jnp.where(even, 1 - x, 3 - x)),
        (overfar, jnp.where(even, 3 - x, 1 - x)),
    )
    copies = [
        pltpu.make_async_copy(ref, target.at[slab], sems.at[i]) for i, (ref, slab) in enumerate(places)
    ]
    for copy in copies:
        copy.start()
    split = total_rows // 2
    low = max(0, min(rows, split - first_row))
    pieces = []
    if low:
        pieces.append((0, first_row, 0, low))
    if rows - low:
        pieces.append((1, first_row + low - split, low, rows - low))
    for which in (0, 1):
        mine, other = (half, overhalf) if which == 0 else (overhalf, half)

        @pl.when(x == which)
        def _(mine=mine, other=other):
            for number, (part, source, to, count) in enumerate(pieces):
                ref = mine if part == 0 else other
                pltpu.make_async_copy(
                    ref.at[pl.ds(source, count)],
                    target.at[TICKS - 1, pl.ds(to, count)],
                    sems.at[4 + number],
                ).start()

    def wait():
        for copy in copies:
            copy.wait()
        for number, (part, source, to, count) in enumerate(pieces):
            pltpu.make_async_copy(
                half.at[pl.ds(source, count)],
                target.at[TICKS - 1, pl.ds(to, count)],
                sems.at[4 + number],
            ).wait()

    return wait


def fetch_gathered(member, refs, target, sems, first_row, total_rows, rows):
    copy = pltpu.make_async_copy(refs[0], target, sems.at[0])
    copy.start()
    return copy.wait


def diagonal_inverse(block):
    size = block.shape[0]
    row = lax.broadcasted_iota(jnp.int32, (size, size), 0)
    col = lax.broadcasted_iota(jnp.int32, (size, size), 1)
    on = row == col
    kept = jnp.where(on, block, 0.0)
    down = 1.0 / jnp.sum(kept, axis=1, keepdims=True)
    right = 1.0 / jnp.sum(kept, axis=0, keepdims=True)
    twice = jnp.where(on, 2.0, 0.0)
    inverse = down * (twice - block * right)
    for _ in range(NEWTON - 1):
        inner = twice - jnp.dot(block, inverse, precision=HIGH, preferred_element_type=jnp.float32)
        inverse = jnp.dot(inverse, inner, precision=HIGH, preferred_element_type=jnp.float32)
    return inverse


def pivot_kernel(fetch, n_bufs, width, total_rows, member_ref, front, *rest):
    bufs = rest[:n_bufs]
    out, w_out, raw, mat, own, inv, sems, own_sems = rest[n_bufs:]
    member = member_ref[0]
    p, rows = P_SIZE, TICKS * P_SIZE
    loads = [
        pltpu.make_async_copy(
            front.at[pl.ds(t * width, p), :], own.at[pl.ds(t * p, p), :], own_sems.at[t]
        )
        for t in range(TICKS)
    ]
    for load in loads:
        load.start()
    wait = fetch(member, bufs, raw, sems, 0, total_rows, rows)
    wait()
    for load in loads:
        load.wait()
    for s in range(TICKS):
        mat[s] = raw[s].astype(jnp.float32)
    for t in range(TICKS):
        lo, below = t * p, (t + 1) * p
        x = diagonal_inverse(mat[t, lo:below, :])
        inv[t] = x
        if below < rows:
            mult = jnp.dot(mat[t, below:, :], x, precision=HIGH, preferred_element_type=jnp.float32)
            panel = mult.astype(jnp.bfloat16)
            for s in range(t + 1, TICKS):
                mat[s, below:, :] = mat[s, below:, :] - jnp.dot(
                    panel, mat[s, lo:below, :].astype(jnp.bfloat16), preferred_element_type=jnp.float32
                )
            urows = own[lo:below, :].astype(jnp.bfloat16)
            own[below:, p:] = own[below:, p:] - jnp.dot(
                panel, urows[:, p:], preferred_element_type=jnp.float32
            )

            @pl.when((member >= TICKS) | (member > t))
            def _():
                own[below:, :p] = own[below:, :p] - jnp.dot(
                    panel, urows[:, :p], preferred_element_type=jnp.float32
                )

            @pl.when(member == t)
            def _():
                own[below:, :p] = jnp.dot(
                    own[below:, :p], x, precision=HIGH, preferred_element_type=jnp.float32
                )

    stores = [
        pltpu.make_async_copy(
            own.at[pl.ds(t * p, p), :], out.at[pl.ds(t * width, p), :], own_sems.at[t]
        )
        for t in range(TICKS)
    ]
    for store in stores:
        store.start()
    row = lax.broadcasted_iota(jnp.int32, (p, width), 0)
    col = lax.broadcasted_iota(jnp.int32, (p, width), 1)
    owner = (member < TICKS) & (col < p)
    for t in reversed(range(TICKS)):
        lo, hi = t * p, (t + 1) * p
        unit = jnp.where((row == col) & (member == t), -1.0, 0.0)
        side = jnp.where(owner, unit, own[lo:hi, :])
        for s in range(t + 1, TICKS):
            side = side - jnp.dot(
                mat[s, lo:hi, :].astype(jnp.bfloat16),
                w_out[s * p : (s + 1) * p, :],
                preferred_element_type=jnp.float32,
            )
        w_out[lo:hi, :] = jnp.dot(
            inv[t], side, precision=HIGH, preferred_element_type=jnp.float32
        ).astype(jnp.bfloat16)
    for store in stores:
        store.wait()


def pivot_rows(fetch, member, front, bufs, total_rows):
    order, width = front.shape
    p, rows = P_SIZE, TICKS * P_SIZE
    return pl.pallas_call(
        functools.partial(pivot_kernel, fetch, len(bufs), width, total_rows),
        name="pivot_rows",
        out_shape=(
            jax.ShapeDtypeStruct((order, width), jnp.float32),
            jax.ShapeDtypeStruct((rows, width), jnp.bfloat16),
        ),
        in_specs=[SMEM, ANY] + [ANY] * len(bufs),
        out_specs=(ANY, VMEM),
        scratch_shapes=[
            pltpu.VMEM((TICKS, rows, p), jnp.bfloat16),
            pltpu.VMEM((TICKS, rows, p), jnp.float32),
            pltpu.VMEM((rows, width), jnp.float32),
            pltpu.VMEM((TICKS, p, p), jnp.float32),
            pltpu.SemaphoreType.DMA((6,)),
            pltpu.SemaphoreType.DMA((TICKS,)),
        ],
    )(member, front, *bufs)


def other_kernel(fetch, n_bufs, ranges, first_row, total_rows, tail, member_ref, w, front, out_in, *rest):
    bufs = rest[:n_bufs]
    if tail:
        out, cont, raw, base, sems, base_sems = rest[n_bufs:]
    else:
        out, raw, base, sems, base_sems = rest[n_bufs:]
    member = member_ref[0]
    rows, width = base.shape
    loads = [
        pltpu.make_async_copy(front.at[pl.ds(src, n), :], base.at[pl.ds(dst, n), :], base_sems.at[i])
        for i, (src, dst, n) in enumerate(ranges)
    ]
    for load in loads:
        load.start()
    wait = fetch(member, bufs, raw, sems, first_row, total_rows, rows)
    wait()
    for load in loads:
        load.wait()
    keep = (member >= TICKS) | (lax.broadcasted_iota(jnp.int32, (ROW_TILE, width), 1) >= P_SIZE)

    def tile(i, carry):
        at = pl.ds(pl.multiple_of(i * ROW_TILE, ROW_TILE), ROW_TILE)
        total = jnp.where(keep, base[at, :], 0.0)
        for s in range(TICKS):
            total = total - jnp.dot(
                raw[s, at, :], w[s * P_SIZE : (s + 1) * P_SIZE, :], preferred_element_type=jnp.float32
            )
        base[at, :] = total
        if tail:
            cont[at, :] = jnp.where(keep, total, 0.0).astype(jnp.bfloat16)
        return carry

    lax.fori_loop(0, rows // ROW_TILE, tile, 0)
    stores = [
        pltpu.make_async_copy(base.at[pl.ds(dst, n), :], out.at[pl.ds(src, n), :], base_sems.at[i])
        for i, (src, dst, n) in enumerate(ranges)
    ]
    for store in stores:
        store.start()
    for store in stores:
        store.wait()


def other_rows(fetch, member, w, front, out, bufs, ranges, first_row, total_rows, tail):
    order, width = front.shape
    rows = sum(n for _, _, n in ranges)
    shapes = [jax.ShapeDtypeStruct((order, width), jnp.float32)]
    specs = [ANY]
    if tail:
        shapes.append(jax.ShapeDtypeStruct((rows, width), jnp.bfloat16))
        specs.append(VMEM)
    return pl.pallas_call(
        functools.partial(other_kernel, fetch, len(bufs), ranges, first_row, total_rows, tail),
        name="tail_rows" if tail else "middle_rows",
        out_shape=tuple(shapes),
        in_specs=[SMEM, VMEM, ANY, ANY] + [ANY] * len(bufs),
        out_specs=tuple(specs),
        input_output_aliases={3: 0},
        scratch_shapes=[
            pltpu.VMEM((TICKS, rows, P_SIZE), jnp.bfloat16),
            pltpu.VMEM((rows, width), jnp.float32),
            pltpu.SemaphoreType.DMA((6,)),
            pltpu.SemaphoreType.DMA((len(ranges),)),
        ],
    )(member, w, front, out, *bufs)


def assemble(cont, parent_group, row_block, parent_base):
    width = parent_base.shape[1]
    groups = lax.axis_size("front")
    cont = cont.reshape(NB, RB, width)
    dest = parent_group.reshape(NB)
    target_block = row_block.reshape(NB)
    offset_hot = (target_block[:, None] == jnp.arange(ASM_BLOCKS, dtype=jnp.int32)[None, :]).astype(
        jnp.bfloat16
    )
    number = jnp.arange(NB)
    earlier = (dest[None, :] == dest[:, None]) & (number[None, :] < number[:, None])
    slot = jnp.sum(earlier.astype(jnp.int32), axis=1)
    pick = (dest[None, None, :] == jnp.arange(groups, dtype=jnp.int32)[:, None, None]) & (
        slot[None, None, :] == jnp.arange(CAP, dtype=jnp.int32)[None, :, None]
    )
    pick = pick.astype(jnp.bfloat16)
    outgoing = jnp.einsum("gci,irk->gcrk", pick, cont, preferred_element_type=jnp.float32).astype(
        jnp.bfloat16
    )
    address = jnp.einsum(
        "gci,ia->gca", pick, offset_hot, preferred_element_type=jnp.float32
    ).astype(jnp.bfloat16)
    incoming = lax.all_to_all(outgoing, "front", split_axis=0, concat_axis=0, tiled=True)
    received_address = lax.all_to_all(address, "front", split_axis=0, concat_axis=0, tiled=True)
    added = jnp.einsum(
        "gca,gcrk->ark", received_address, incoming, preferred_element_type=jnp.float32
    )
    return parent_base + added.reshape(ASM_BLOCKS * RB, width)


def local(front, parent_group, row_block, parent_base):
    order, width = front.shape
    member = lax.axis_index("blk")
    holder = member.reshape(1).astype(jnp.int32)
    p, top = P_SIZE, TICKS * width
    tail_n = NB * RB
    tail_at = order - tail_n
    slabs = front[:top].reshape(TICKS, width, width)
    own_p = slabs[:, :p, :p].reshape(TICKS * p, p).astype(jnp.bfloat16)
    own_t = front[tail_at:, :p].astype(jnp.bfloat16)
    own_m = jnp.concatenate(
        [slabs[:, p:, :p].reshape(TICKS * (width - p), p), front[top:tail_at, :p]], axis=0
    ).astype(jnp.bfloat16)
    middle = [(t * width + p, t * (width - p), width - p) for t in range(TICKS)]
    if tail_at > top:
        middle.append((top, TICKS * (width - p), tail_at - top))
    segments = (own_p, own_t, own_m)
    if lax.axis_size("blk") == 8:
        fetch = fetch_relayed
        sets = relay(segments, member)
    else:
        fetch = fetch_gathered
        sets = tuple((lax.all_gather(s, "blk")[:TICKS],) for s in segments)
    early, late = TICKS * p + tail_n, own_m.shape[0]
    out, w = pivot_rows(fetch, holder, front, sets[0], early)
    out, cont = other_rows(
        fetch, holder, w, front, out, sets[1], [(tail_at, 0, tail_n)], TICKS * p, early, True
    )
    assembled = assemble(cont, parent_group, row_block, parent_base)
    (factored,) = other_rows(fetch, holder, w, front, out, sets[2], middle, 0, late, False)
    return (factored, assembled)


def solution(mesh):
    placed = (
        P("front", "blk"),
        P("front", "blk", None, None),
        P("front", "blk", None),
        P("front", "blk"),
    )
    return jax.shard_map(
        local,
        mesh=mesh,
        in_specs=placed,
        out_specs=(P("front", "blk"), P("front", "blk")),
        check_vma=False,
    )
```

```python
import functools

import jax
import jax.numpy as jnp
from jax import lax
from jax.experimental import pallas as pl
from jax.experimental.pallas import tpu as pltpu
from jax.sharding import PartitionSpec as P


P_SIZE = 256
TICKS = 5
NEWTON = 2
RB = 128
NB = 6
CAP = 2
HIGH = lax.Precision.HIGHEST
ANY = pl.BlockSpec(memory_space=pl.ANY)
SMEM = pl.BlockSpec(memory_space=pltpu.SMEM)
VMEM = pl.BlockSpec(memory_space=pltpu.VMEM)


def permute(value, pairs):
    return lax.ppermute(value, "blk", pairs)


def relay(parts, member):
    across = [(m, m ^ 1) for m in range(8)]
    near = [(m, m ^ 2) for m in range(8)]
    distant = [(m, m + 4) for m in range(4)]
    pairs = [(0, 1), (1, 0), (2, 3), (3, 2)]
    beside, back = [(4, 5)], [(4, 0), (5, 1)]
    spread = [(0, 2), (1, 3), (4, 6), (5, 7)]
    level = member // 2
    a, b, c, e_low, e_high = parts

    def slabs(own):
        cur = jnp.where(member < 4, own, permute(own, distant))
        far = permute(cur, near)
        over = permute(cur, across)
        return cur, far, over, permute(far, across)

    def both_slabs(own):
        both = jnp.stack([own, permute(own, pairs)])
        cur = jnp.where(member < 4, both, permute(both, distant))
        return cur, permute(cur, near)

    def halves(low, high):
        half = jnp.where(member == 5, permute(high, beside), low)
        half = jnp.where(level == 0, permute(half, back), half)
        half = jnp.where(level % 2 == 1, permute(half, spread), half)
        return half, permute(half, across)

    early = halves(e_low, e_high)
    n = c.shape[0] // 2
    late = halves(c[:n], c[n:])
    return (slabs(a), early), (both_slabs(b), early), (slabs(c), late)


def placed_slabs(member, refs):
    x = lax.rem(member, 2)
    even = lax.rem(lax.div(member, 2), 2) == 0
    near, far = jnp.where(even, x, 2 + x), jnp.where(even, 2 + x, x)
    over, overfar = jnp.where(even, 1 - x, 3 - x), jnp.where(even, 3 - x, 1 - x)
    if len(refs) == 2:
        return ((refs[0].at[0], near), (refs[1].at[0], far), (refs[0].at[1], over), (refs[1].at[1], overfar))
    return tuple(zip(refs, (near, far, over, overfar)))


def start_first(member, refs, target, sems):
    if len(refs) == 1:
        copies = [pltpu.make_async_copy(refs[0].at[pl.ds(0, TICKS - 1)], target.at[pl.ds(0, TICKS - 1)], sems.at[0])]
    else:
        copies = [
            pltpu.make_async_copy(ref, target.at[slab], sems.at[i])
            for i, (ref, slab) in enumerate(placed_slabs(member, refs))
        ]
    for copy in copies:
        copy.start()
    return copies


def start_last(member, refs, target, sems, first_row, rows):
    if len(refs) == 1:
        copies = [pltpu.make_async_copy(refs[0].at[TICKS - 1], target, sems.at[0])]
        copies[0].start()
        return copies
    half, overhalf = refs
    x = lax.rem(member, 2)
    split = half.shape[0]
    low = max(0, min(rows, split - first_row))
    pieces = []
    if low:
        pieces.append((0, first_row, 0, low))
    if rows - low:
        pieces.append((1, first_row + low - split, low, rows - low))

    def copy(ref, number):
        _, source, to, count = pieces[number]
        return pltpu.make_async_copy(
            ref.at[pl.ds(source, count)], target.at[pl.ds(to, count)], sems.at[number]
        )

    for which in (0, 1):

        @pl.when(x == which)
        def _(which=which):
            for number, piece in enumerate(pieces):
                copy(half if piece[0] == which else overhalf, number).start()

    return [copy(half, number) for number in range(len(pieces))]


def wait_all(copies):
    for copy in copies:
        copy.wait()


def pack_kernel(pieces, front, *rest):
    outs, (held, sems) = rest[: len(pieces)], rest[len(pieces) :]
    copies, at = [], 0
    for ranges in pieces:
        for start, count in ranges:
            copies.append(
                pltpu.make_async_copy(
                    front.at[pl.ds(start, count), pl.ds(0, P_SIZE)], held.at[pl.ds(at, count), :], sems.at[len(copies)]
                )
            )
            copies[-1].start()
            at += count
    at, number = 0, 0
    for ranges, out in zip(pieces, outs):
        to = 0
        for _, count in ranges:
            copies[number].wait()
            out[pl.ds(to, count), :] = held[pl.ds(at, count), :].astype(jnp.bfloat16)
            at, to, number = at + count, to + count, number + 1


def pack(front, pieces):
    sizes = [sum(n for _, n in ranges) for ranges in pieces]
    return pl.pallas_call(
        functools.partial(pack_kernel, pieces),
        out_shape=tuple(jax.ShapeDtypeStruct((n, P_SIZE), jnp.bfloat16) for n in sizes),
        in_specs=[ANY],
        out_specs=(VMEM,) * len(sizes),
        scratch_shapes=[
            pltpu.VMEM((sum(sizes), P_SIZE), jnp.float32),
            pltpu.SemaphoreType.DMA((sum(len(r) for r in pieces),)),
        ],
    )(front)


def diagonal_inverse(block):
    size = block.shape[0]
    row = lax.broadcasted_iota(jnp.int32, (size, size), 0)
    col = lax.broadcasted_iota(jnp.int32, (size, size), 1)
    on = row == col
    kept = jnp.where(on, block, 0.0)
    down = 1.0 / jnp.sum(kept, axis=1, keepdims=True)
    right = 1.0 / jnp.sum(kept, axis=0, keepdims=True)
    twice = jnp.where(on, 2.0, 0.0)
    inverse = down * (twice - block * right)
    for _ in range(NEWTON - 1):
        inner = twice - jnp.dot(block, inverse, precision=HIGH, preferred_element_type=jnp.float32)
        inverse = jnp.dot(inverse, inner, precision=HIGH, preferred_element_type=jnp.float32)
    return inverse


def minus_dot(value, left, right):
    return value - jnp.dot(left, right, preferred_element_type=jnp.float32)


def pivot_kernel(n_bufs, width, member_ref, front, *rest):
    bufs = rest[:n_bufs]
    out, low_up, inv, own, raw, mat, sems, own_sems = rest[n_bufs:]
    member = member_ref[0]
    p = P_SIZE
    copies = start_first(member, bufs, raw, sems)
    loads = [
        pltpu.make_async_copy(
            front.at[pl.ds(t * width, p), :], own.at[pl.ds(t * p, p), :], own_sems.at[t]
        )
        for t in range(TICKS)
    ]
    for load in loads:
        load.start()
    wait_all(copies)
    for s in range(TICKS - 1):
        mat[s] = raw[s].astype(jnp.float32)
    wait_all(loads)
    for t in range(TICKS - 1):
        lo, below = t * p, (t + 1) * p
        x = diagonal_inverse(mat[t, lo:below, :])
        inv[t] = x
        mult = jnp.dot(mat[t, below:, :], x, precision=HIGH, preferred_element_type=jnp.float32)
        panel = mult.astype(jnp.bfloat16)
        low_up[t, below:, :] = panel
        for s in range(t + 1, TICKS - 1):
            urows = mat[s, lo:below, :].astype(jnp.bfloat16)
            low_up[s, lo:below, :] = urows
            mat[s, below:, :] = minus_dot(mat[s, below:, :], panel, urows)
        urows = own[lo:below, :].astype(jnp.bfloat16)
        own[below:, p:] = minus_dot(own[below:, p:], panel, urows[:, p:])

        @pl.when((member >= TICKS) | (member > t))
        def _():
            own[below:, :p] = minus_dot(own[below:, :p], panel, urows[:, :p])

        @pl.when(member == t)
        def _():
            own[below:, :p] = jnp.dot(
                own[below:, :p], x, precision=HIGH, preferred_element_type=jnp.float32
            )

    stores = [
        pltpu.make_async_copy(
            own.at[pl.ds(t * p, p), :], out.at[pl.ds(t * width, p), :], own_sems.at[t]
        )
        for t in range(TICKS)
    ]
    for store in stores:
        store.start()
    wait_all(stores)


def pivot_rows(member, front, bufs):
    order, width = front.shape
    p, rows = P_SIZE, TICKS * P_SIZE
    return pl.pallas_call(
        functools.partial(pivot_kernel, len(bufs), width),
        name="pivot_rows",
        out_shape=(
            jax.ShapeDtypeStruct((order, width), jnp.float32),
            jax.ShapeDtypeStruct((TICKS - 1, rows, p), jnp.bfloat16),
            jax.ShapeDtypeStruct((TICKS - 1, p, p), jnp.float32),
            jax.ShapeDtypeStruct((rows, width), jnp.float32),
        ),
        in_specs=[SMEM, ANY] + [ANY] * len(bufs),
        out_specs=(ANY, VMEM, VMEM, VMEM),
        scratch_shapes=[
            pltpu.VMEM((TICKS - 1, rows, p), jnp.bfloat16),
            pltpu.VMEM((TICKS - 1, rows, p), jnp.float32),
            pltpu.SemaphoreType.DMA((4,)),
            pltpu.SemaphoreType.DMA((TICKS,)),
        ],
    )(member, front, *bufs)


def solve_kernel(n_bufs, member_ref, low_up, inv, own, *rest):
    bufs = rest[:n_bufs]
    w_out, raw, mat, sems = rest[n_bufs:]
    member = member_ref[0]
    p, rows, width = P_SIZE, own.shape[0], own.shape[1]
    copies = start_last(member, bufs, raw, sems, 0, rows)
    wait_all(copies)
    mat[...] = raw[...].astype(jnp.float32)
    last = TICKS - 1
    for t in range(last):
        lo, below = t * p, (t + 1) * p
        mat[below:, :] = minus_dot(mat[below:, :], low_up[t, below:, :], mat[lo:below, :].astype(jnp.bfloat16))
    x_last = diagonal_inverse(mat[last * p :, :])
    row = lax.broadcasted_iota(jnp.int32, (p, width), 0)
    col = lax.broadcasted_iota(jnp.int32, (p, width), 1)
    owner = (member < TICKS) & (col < p)
    for t in reversed(range(TICKS)):
        lo, hi = t * p, (t + 1) * p
        unit = jnp.where((row == col) & (member == t), -1.0, 0.0)
        side = jnp.where(owner, unit, own[lo:hi, :])
        for s in range(t + 1, TICKS):
            urows = mat[lo:hi, :].astype(jnp.bfloat16) if s == last else low_up[s, lo:hi, :]
            side = minus_dot(side, urows, w_out[s * p : (s + 1) * p, :])
        x = x_last if t == last else inv[t]
        w_out[lo:hi, :] = jnp.dot(x, side, precision=HIGH, preferred_element_type=jnp.float32).astype(
            jnp.bfloat16
        )


def solve(member, low_up, inv, own, bufs):
    rows, width = own.shape
    return pl.pallas_call(
        functools.partial(solve_kernel, len(bufs)),
        name="solve",
        out_shape=jax.ShapeDtypeStruct((rows, width), jnp.bfloat16),
        in_specs=[SMEM, VMEM, VMEM, VMEM] + [ANY] * len(bufs),
        out_specs=VMEM,
        scratch_shapes=[
            pltpu.VMEM((rows, P_SIZE), jnp.bfloat16),
            pltpu.VMEM((rows, P_SIZE), jnp.float32),
            pltpu.SemaphoreType.DMA((2,)),
        ],
    )(member, low_up, inv, own, *bufs)


def other_kernel(counts, ranges, first_row, tail, member_ref, dest_ref, slot_ref, w, front, out_in, *rest):
    firsts, lasts = rest[: counts[0]], rest[counts[0] : sum(counts)]
    if tail:
        out, outgoing, raw, base, sems, last_sems, base_sems = rest[sum(counts) :]
    else:
        out, raw, base, sems, last_sems, base_sems = rest[sum(counts) :]
    member = member_ref[0]
    rows, width = base.shape
    copies = start_first(member, firsts, raw, sems)
    copies += start_last(member, lasts, raw.at[TICKS - 1], last_sems, first_row, rows)
    loads = [
        pltpu.make_async_copy(front.at[pl.ds(src, n), :], base.at[pl.ds(dst, n), :], base_sems.at[i])
        for i, (src, dst, n) in enumerate(ranges)
    ]
    for load in loads:
        load.start()
    wait_all(copies)
    wait_all(loads)
    keep = (member >= TICKS) | (lax.broadcasted_iota(jnp.int32, (RB, width), 1) >= P_SIZE)

    def tile(i, carry):
        at = pl.ds(pl.multiple_of(i * RB, RB), RB)
        total = jnp.where(keep, base[at, :], 0.0)
        for s in range(TICKS):
            total = minus_dot(total, raw[s, at, :], w[s * P_SIZE : (s + 1) * P_SIZE, :])
        base[at, :] = total
        if tail:
            outgoing[dest_ref[i], slot_ref[i]] = jnp.where(keep, total, 0.0).astype(jnp.bfloat16)
        return carry

    lax.fori_loop(0, rows // RB, tile, 0)
    stores = [
        pltpu.make_async_copy(base.at[pl.ds(dst, n), :], out.at[pl.ds(src, n), :], base_sems.at[i])
        for i, (src, dst, n) in enumerate(ranges)
    ]
    for store in stores:
        store.start()
    wait_all(stores)


def other_rows(member, dest, slot, w, front, out, bufs, ranges, first_row, groups=0):
    order, width = front.shape
    rows = sum(n for _, _, n in ranges)
    shapes = [jax.ShapeDtypeStruct((order, width), jnp.float32)]
    specs = [ANY]
    if groups:
        shapes.append(jax.ShapeDtypeStruct((groups, CAP, RB, width), jnp.bfloat16))
        specs.append(VMEM)
    counts = tuple(len(b) for b in bufs)
    return pl.pallas_call(
        functools.partial(other_kernel, counts, ranges, first_row, bool(groups)),
        name="tail_rows" if groups else "middle_rows",
        out_shape=tuple(shapes),
        in_specs=[SMEM, SMEM, SMEM, VMEM, ANY, ANY] + [ANY] * sum(counts),
        out_specs=tuple(specs),
        input_output_aliases={5: 0},
        scratch_shapes=[
            pltpu.VMEM((TICKS, rows, P_SIZE), jnp.bfloat16),
            pltpu.VMEM((rows, width), jnp.float32),
            pltpu.SemaphoreType.DMA((4,)),
            pltpu.SemaphoreType.DMA((2,)),
            pltpu.SemaphoreType.DMA((len(ranges),)),
        ],
    )(member, dest, slot, w, front, out, *bufs[0], *bufs[1])


def routes(parent_group, row_block):
    groups = lax.axis_size("front")
    dest = parent_group.reshape(NB)
    target = row_block.reshape(NB)
    number = jnp.arange(NB)
    earlier = (dest[None, :] == dest[:, None]) & (number[None, :] < number[:, None])
    slot = jnp.sum(earlier.astype(jnp.int32), axis=1)
    pick = (dest[None, None, :] == jnp.arange(groups, dtype=jnp.int32)[:, None, None]) & (
        slot[None, None, :] == jnp.arange(CAP, dtype=jnp.int32)[None, :, None]
    )
    address = jnp.sum(jnp.where(pick, target[None, None, :] + 1, 0), axis=2) - 1
    received = lax.all_to_all(address, "front", split_axis=0, concat_axis=0, tiled=True)
    return dest, slot, received.reshape(groups * CAP)


def add_kernel(address_ref, incoming, base, out):
    out[...] = base[...]
    for i in range(incoming.shape[0]):
        to = address_ref[i]

        @pl.when(to >= 0)
        def _(i=i, to=to):
            at = pl.ds(pl.multiple_of(to * RB, RB), RB)
            out[at, :] = out[at, :] + incoming[i].astype(jnp.float32)


def add_blocks(address, incoming, parent_base):
    groups, cap, rows, width = incoming.shape
    return pl.pallas_call(
        add_kernel,
        name="add_blocks",
        out_shape=jax.ShapeDtypeStruct(parent_base.shape, parent_base.dtype),
        in_specs=[SMEM, VMEM, VMEM],
        out_specs=VMEM,
    )(address, incoming.reshape(groups * cap, rows, width), parent_base)


def local(front, parent_group, row_block, parent_base):
    order, width = front.shape
    member = lax.axis_index("blk")
    holder = member.reshape(1).astype(jnp.int32)
    p, top = P_SIZE, TICKS * width
    tail_n = NB * RB
    tail_at = order - tail_n
    pivot_ranges = [(t * width, p) for t in range(TICKS)]
    tail_ranges = [(tail_at, tail_n)]
    middle_ranges = [(t * width + p, width - p) for t in range(TICKS)]
    if tail_at > top:
        middle_ranges.append((top, tail_at - top))
    middle, at = [], 0
    for start, count in middle_ranges:
        middle.append((start, at, count))
        at += count
    (own_p,) = pack(front, [pivot_ranges])
    if lax.axis_size("blk") == 8:
        own_t, e_high, own_m = pack(front, [tail_ranges, pivot_ranges[TICKS - 1 :] + tail_ranges, middle_ranges])
        sets = relay((own_p, own_t, own_m, own_p[: (TICKS - 1) * p], e_high), member)
    else:
        own_t, own_m = pack(front, [tail_ranges, middle_ranges])
        sets = tuple(((lax.all_gather(s, "blk")[:TICKS],),) * 2 for s in (own_p, own_t, own_m))
    dest, slot, address = routes(parent_group, row_block)
    out, low_up, inv, own = pivot_rows(holder, front, sets[0][0])
    w = solve(holder, low_up, inv, own, sets[0][1])
    out, outgoing = other_rows(
        holder, dest, slot, w, front, out, sets[1], [(tail_at, 0, tail_n)], TICKS * p, lax.axis_size("front")
    )
    incoming = lax.all_to_all(outgoing, "front", split_axis=0, concat_axis=0, tiled=True)
    (factored,) = other_rows(holder, dest, slot, w, front, out, sets[2], middle, 0)
    assembled = add_blocks(address, incoming, parent_base)
    return (factored, assembled)


def solution(mesh):
    placed = (
        P("front", "blk"),
        P("front", "blk", None, None),
        P("front", "blk", None),
        P("front", "blk"),
    )
    return jax.shard_map(
        local,
        mesh=mesh,
        in_specs=placed,
        out_specs=(P("front", "blk"), P("front", "blk")),
        check_vma=False,
    )
```

```python
import functools

import jax
import jax.numpy as jnp
from jax import lax
from jax.experimental import pallas as pl
from jax.experimental.pallas import tpu as pltpu
from jax.sharding import PartitionSpec as P


P_SIZE = 256
TICKS = 5
NEWTON = 2
RB = 128
NB = 6
CAP = 2
HIGH = lax.Precision.HIGHEST
ANY = pl.BlockSpec(memory_space=pl.ANY)
SMEM = pl.BlockSpec(memory_space=pltpu.SMEM)
VMEM = pl.BlockSpec(memory_space=pltpu.VMEM)


def permute(value, pairs):
    return lax.ppermute(value, "blk", pairs)


def relay(parts, member):
    across = [(m, m ^ 1) for m in range(8)]
    near = [(m, m ^ 2) for m in range(8)]
    distant = [(m, m + 4) for m in range(4)]
    beside, back = [(4, 5)], [(4, 0), (5, 1)]
    spread = [(0, 2), (1, 3), (4, 6), (5, 7)]
    level = member // 2
    a, b, c, e_low, e_high = parts

    def slabs(own):
        cur = jnp.where(member < 4, own, permute(own, distant))
        far = permute(cur, near)
        over = permute(cur, across)
        return cur, far, over, permute(far, across)

    def halves(low, high):
        half = jnp.where(member == 5, permute(high, beside), low)
        half = jnp.where(level == 0, permute(half, back), half)
        half = jnp.where(level % 2 == 1, permute(half, spread), half)
        return half, permute(half, across)

    early = halves(e_low, e_high)
    n = c.shape[0] // 2
    late = halves(c[:n], c[n:])
    return (slabs(a), early), (slabs(b), early), (slabs(c), late)


def placed_slabs(member, refs):
    x = lax.rem(member, 2)
    even = lax.rem(lax.div(member, 2), 2) == 0
    near, far = jnp.where(even, x, 2 + x), jnp.where(even, 2 + x, x)
    over, overfar = jnp.where(even, 1 - x, 3 - x), jnp.where(even, 3 - x, 1 - x)
    return tuple(zip(refs, (near, far, over, overfar)))


def start_first(member, refs, target, sems):
    if len(refs) == 1:
        copies = [pltpu.make_async_copy(refs[0].at[pl.ds(0, TICKS - 1)], target.at[pl.ds(0, TICKS - 1)], sems.at[0])]
    else:
        copies = [
            pltpu.make_async_copy(ref, target.at[slab], sems.at[i])
            for i, (ref, slab) in enumerate(placed_slabs(member, refs))
        ]
    for copy in copies:
        copy.start()
    return copies


def start_last(member, refs, target, sems, first_row, rows):
    if len(refs) == 1:
        copies = [pltpu.make_async_copy(refs[0].at[TICKS - 1], target, sems.at[0])]
        copies[0].start()
        return copies
    half, overhalf = refs
    x = lax.rem(member, 2)
    split = half.shape[0]
    low = max(0, min(rows, split - first_row))
    pieces = []
    if low:
        pieces.append((0, first_row, 0, low))
    if rows - low:
        pieces.append((1, first_row + low - split, low, rows - low))

    def copy(ref, number):
        _, source, to, count = pieces[number]
        return pltpu.make_async_copy(
            ref.at[pl.ds(source, count)], target.at[pl.ds(to, count)], sems.at[number]
        )

    for which in (0, 1):

        @pl.when(x == which)
        def _(which=which):
            for number, piece in enumerate(pieces):
                copy(half if piece[0] == which else overhalf, number).start()

    return [copy(half, number) for number in range(len(pieces))]


def wait_all(copies):
    for copy in copies:
        copy.wait()


def pack_kernel(pieces, front, *rest):
    outs, (held, sems) = rest[: len(pieces)], rest[len(pieces) :]
    copies, at = [], 0
    for ranges in pieces:
        for start, count in ranges:
            copies.append(
                pltpu.make_async_copy(
                    front.at[pl.ds(start, count), pl.ds(0, P_SIZE)], held.at[pl.ds(at, count), :], sems.at[len(copies)]
                )
            )
            copies[-1].start()
            at += count
    at, number = 0, 0
    for ranges, out in zip(pieces, outs):
        to = 0
        for _, count in ranges:
            copies[number].wait()
            out[pl.ds(to, count), :] = held[pl.ds(at, count), :].astype(jnp.bfloat16)
            at, to, number = at + count, to + count, number + 1


def pack(front, pieces):
    sizes = [sum(n for _, n in ranges) for ranges in pieces]
    return pl.pallas_call(
        functools.partial(pack_kernel, pieces),
        out_shape=tuple(jax.ShapeDtypeStruct((n, P_SIZE), jnp.bfloat16) for n in sizes),
        in_specs=[ANY],
        out_specs=(VMEM,) * len(sizes),
        scratch_shapes=[
            pltpu.VMEM((sum(sizes), P_SIZE), jnp.float32),
            pltpu.SemaphoreType.DMA((sum(len(r) for r in pieces),)),
        ],
    )(front)


def diagonal_inverse(block):
    size = block.shape[0]
    row = lax.broadcasted_iota(jnp.int32, (size, size), 0)
    col = lax.broadcasted_iota(jnp.int32, (size, size), 1)
    on = row == col
    kept = jnp.where(on, block, 0.0)
    down = 1.0 / jnp.sum(kept, axis=1, keepdims=True)
    right = 1.0 / jnp.sum(kept, axis=0, keepdims=True)
    twice = jnp.where(on, 2.0, 0.0)
    inverse = down * (twice - block * right)
    for _ in range(NEWTON - 1):
        inner = twice - jnp.dot(block, inverse, precision=HIGH, preferred_element_type=jnp.float32)
        inverse = jnp.dot(inverse, inner, precision=HIGH, preferred_element_type=jnp.float32)
    return inverse


def minus_dot(value, left, right):
    return value - jnp.dot(left, right, preferred_element_type=jnp.float32)


def minus_dot(value, left, right):
    return value - jnp.dot(left, right, preferred_element_type=jnp.float32)


def pivot_kernel(counts, width, member_ref, front, *rest):
    firsts, lasts = rest[: counts[0]], rest[counts[0] : sum(counts)]
    out, w_out, raw, mat, own, inv, sems, last_sems, own_sems = rest[sum(counts) :]
    member = member_ref[0]
    p, rows = P_SIZE, TICKS * P_SIZE
    copies = start_first(member, firsts, raw, sems)
    copies += start_last(member, lasts, raw.at[TICKS - 1], last_sems, 0, rows)
    loads = [
        pltpu.make_async_copy(
            front.at[pl.ds(t * width, p), :], own.at[pl.ds(t * p, p), :], own_sems.at[t]
        )
        for t in range(TICKS)
    ]
    for load in loads:
        load.start()
    wait_all(copies)
    for s in range(TICKS):
        mat[s] = raw[s].astype(jnp.float32)
    wait_all(loads)
    for t in range(TICKS):
        lo, below = t * p, (t + 1) * p
        x = diagonal_inverse(mat[t, lo:below, :])
        inv[t] = x
        if below < rows:
            mult = jnp.dot(mat[t, below:, :], x, precision=HIGH, preferred_element_type=jnp.float32)
            panel = mult.astype(jnp.bfloat16)
            for s in range(t + 1, TICKS):
                mat[s, below:, :] = minus_dot(
                    mat[s, below:, :], panel, mat[s, lo:below, :].astype(jnp.bfloat16)
                )
            urows = own[lo:below, :].astype(jnp.bfloat16)
            own[below:, p:] = minus_dot(own[below:, p:], panel, urows[:, p:])

            @pl.when((member >= TICKS) | (member > t))
            def _():
                own[below:, :p] = minus_dot(own[below:, :p], panel, urows[:, :p])

            @pl.when(member == t)
            def _():
                own[below:, :p] = jnp.dot(
                    own[below:, :p], x, precision=HIGH, preferred_element_type=jnp.float32
                )

    stores = [
        pltpu.make_async_copy(
            own.at[pl.ds(t * p, p), :], out.at[pl.ds(t * width, p), :], own_sems.at[t]
        )
        for t in range(TICKS)
    ]
    for store in stores:
        store.start()
    row = lax.broadcasted_iota(jnp.int32, (p, width), 0)
    col = lax.broadcasted_iota(jnp.int32, (p, width), 1)
    owner = (member < TICKS) & (col < p)
    for t in reversed(range(TICKS)):
        lo, hi = t * p, (t + 1) * p
        unit = jnp.where((row == col) & (member == t), -1.0, 0.0)
        side = jnp.where(owner, unit, own[lo:hi, :])
        for s in range(t + 1, TICKS):
            side = minus_dot(side, mat[s, lo:hi, :].astype(jnp.bfloat16), w_out[s * p : (s + 1) * p, :])
        w_out[lo:hi, :] = jnp.dot(
            inv[t], side, precision=HIGH, preferred_element_type=jnp.float32
        ).astype(jnp.bfloat16)
    wait_all(stores)


def pivot_rows(member, front, bufs):
    order, width = front.shape
    p, rows = P_SIZE, TICKS * P_SIZE
    counts = tuple(len(b) for b in bufs)
    return pl.pallas_call(
        functools.partial(pivot_kernel, counts, width),
        name="pivot_rows",
        out_shape=(
            jax.ShapeDtypeStruct((order, width), jnp.float32),
            jax.ShapeDtypeStruct((rows, width), jnp.bfloat16),
        ),
        in_specs=[SMEM, ANY] + [ANY] * sum(counts),
        out_specs=(ANY, VMEM),
        scratch_shapes=[
            pltpu.VMEM((TICKS, rows, p), jnp.bfloat16),
            pltpu.VMEM((TICKS, rows, p), jnp.float32),
            pltpu.VMEM((rows, width), jnp.float32),
            pltpu.VMEM((TICKS, p, p), jnp.float32),
            pltpu.SemaphoreType.DMA((4,)),
            pltpu.SemaphoreType.DMA((2,)),
            pltpu.SemaphoreType.DMA((TICKS,)),
        ],
    )(member, front, *bufs[0], *bufs[1])


def other_kernel(counts, ranges, first_row, tail, member_ref, dest_ref, slot_ref, w, front, out_in, *rest):
    firsts, lasts = rest[: counts[0]], rest[counts[0] : sum(counts)]
    if tail:
        out, outgoing, raw, base, sems, last_sems, base_sems = rest[sum(counts) :]
    else:
        out, raw, base, sems, last_sems, base_sems = rest[sum(counts) :]
    member = member_ref[0]
    rows, width = base.shape
    copies = start_first(member, firsts, raw, sems)
    copies += start_last(member, lasts, raw.at[TICKS - 1], last_sems, first_row, rows)
    loads = [
        pltpu.make_async_copy(front.at[pl.ds(src, n), :], base.at[pl.ds(dst, n), :], base_sems.at[i])
        for i, (src, dst, n) in enumerate(ranges)
    ]
    for load in loads:
        load.start()
    wait_all(copies)
    wait_all(loads)
    keep = (member >= TICKS) | (lax.broadcasted_iota(jnp.int32, (RB, width), 1) >= P_SIZE)

    def tile(i, carry):
        at = pl.ds(pl.multiple_of(i * RB, RB), RB)
        total = jnp.where(keep, base[at, :], 0.0)
        for s in range(TICKS):
            total = minus_dot(total, raw[s, at, :], w[s * P_SIZE : (s + 1) * P_SIZE, :])
        base[at, :] = total
        if tail:
            outgoing[dest_ref[i], slot_ref[i]] = jnp.where(keep, total, 0.0).astype(jnp.bfloat16)
        return carry

    lax.fori_loop(0, rows // RB, tile, 0)
    stores = [
        pltpu.make_async_copy(base.at[pl.ds(dst, n), :], out.at[pl.ds(src, n), :], base_sems.at[i])
        for i, (src, dst, n) in enumerate(ranges)
    ]
    for store in stores:
        store.start()
    wait_all(stores)


def other_rows(member, dest, slot, w, front, out, bufs, ranges, first_row, groups=0):
    order, width = front.shape
    rows = sum(n for _, _, n in ranges)
    shapes = [jax.ShapeDtypeStruct((order, width), jnp.float32)]
    specs = [ANY]
    if groups:
        shapes.append(jax.ShapeDtypeStruct((groups, CAP, RB, width), jnp.bfloat16))
        specs.append(VMEM)
    counts = tuple(len(b) for b in bufs)
    return pl.pallas_call(
        functools.partial(other_kernel, counts, ranges, first_row, bool(groups)),
        name="tail_rows" if groups else "middle_rows",
        out_shape=tuple(shapes),
        in_specs=[SMEM, SMEM, SMEM, VMEM, ANY, ANY] + [ANY] * sum(counts),
        out_specs=tuple(specs),
        input_output_aliases={5: 0},
        scratch_shapes=[
            pltpu.VMEM((TICKS, rows, P_SIZE), jnp.bfloat16),
            pltpu.VMEM((rows, width), jnp.float32),
            pltpu.SemaphoreType.DMA((4,)),
            pltpu.SemaphoreType.DMA((2,)),
            pltpu.SemaphoreType.DMA((len(ranges),)),
        ],
    )(member, dest, slot, w, front, out, *bufs[0], *bufs[1])


def routes(parent_group, row_block):
    groups = lax.axis_size("front")
    dest = parent_group.reshape(NB)
    target = row_block.reshape(NB)
    number = jnp.arange(NB)
    earlier = (dest[None, :] == dest[:, None]) & (number[None, :] < number[:, None])
    slot = jnp.sum(earlier.astype(jnp.int32), axis=1)
    pick = (dest[None, None, :] == jnp.arange(groups, dtype=jnp.int32)[:, None, None]) & (
        slot[None, None, :] == jnp.arange(CAP, dtype=jnp.int32)[None, :, None]
    )
    address = jnp.sum(jnp.where(pick, target[None, None, :] + 1, 0), axis=2) - 1
    received = lax.all_to_all(address, "front", split_axis=0, concat_axis=0, tiled=True)
    return dest, slot, received.reshape(groups * CAP)


def add_kernel(address_ref, incoming, base, out):
    out[...] = base[...]
    for i in range(incoming.shape[0]):
        to = address_ref[i]

        @pl.when(to >= 0)
        def _(i=i, to=to):
            at = pl.ds(pl.multiple_of(to * RB, RB), RB)
            out[at, :] = out[at, :] + incoming[i].astype(jnp.float32)


def add_blocks(address, incoming, parent_base):
    groups, cap, rows, width = incoming.shape
    return pl.pallas_call(
        add_kernel,
        name="add_blocks",
        out_shape=jax.ShapeDtypeStruct(parent_base.shape, parent_base.dtype),
        in_specs=[SMEM, VMEM, VMEM],
        out_specs=VMEM,
    )(address, incoming.reshape(groups * cap, rows, width), parent_base)


def local(front, parent_group, row_block, parent_base):
    order, width = front.shape
    member = lax.axis_index("blk")
    holder = member.reshape(1).astype(jnp.int32)
    p, top = P_SIZE, TICKS * width
    tail_n = NB * RB
    tail_at = order - tail_n
    pivot_ranges = [(t * width, p) for t in range(TICKS)]
    tail_ranges = [(tail_at, tail_n)]
    middle_ranges = [(t * width + p, width - p) for t in range(TICKS)]
    if tail_at > top:
        middle_ranges.append((top, tail_at - top))
    middle, at = [], 0
    for start, count in middle_ranges:
        middle.append((start, at, count))
        at += count
    (own_p,) = pack(front, [pivot_ranges])
    if lax.axis_size("blk") == 8:
        own_t, e_high, own_m = pack(front, [tail_ranges, pivot_ranges[TICKS - 1 :] + tail_ranges, middle_ranges])
        sets = relay((own_p, own_t, own_m, own_p[: (TICKS - 1) * p], e_high), member)
    else:
        own_t, own_m = pack(front, [tail_ranges, middle_ranges])
        sets = tuple(((lax.all_gather(s, "blk")[:TICKS],),) * 2 for s in (own_p, own_t, own_m))
    dest, slot, address = routes(parent_group, row_block)
    out, w = pivot_rows(holder, front, sets[0])
    out, outgoing = other_rows(
        holder, dest, slot, w, front, out, sets[1], [(tail_at, 0, tail_n)], TICKS * p, lax.axis_size("front")
    )
    incoming = lax.all_to_all(outgoing, "front", split_axis=0, concat_axis=0, tiled=True)
    (factored,) = other_rows(holder, dest, slot, w, front, out, sets[2], middle, 0)
    assembled = add_blocks(address, incoming, parent_base)
    return (factored, assembled)


def solution(mesh):
    placed = (
        P("front", "blk"),
        P("front", "blk", None, None),
        P("front", "blk", None),
        P("front", "blk"),
    )
    return jax.shard_map(
        local,
        mesh=mesh,
        in_specs=placed,
        out_specs=(P("front", "blk"), P("front", "blk")),
        check_vma=False,
    )
```

```python
import functools

import jax
import jax.numpy as jnp
from jax import lax
from jax.experimental import pallas as pl
from jax.experimental.pallas import tpu as pltpu
from jax.sharding import PartitionSpec as P


P_SIZE = 256
TICKS = 5
NEWTON = 2
RB = 128
NB = 6
CAP = 2
ANY = pl.BlockSpec(memory_space=pl.ANY)
SMEM = pl.BlockSpec(memory_space=pltpu.SMEM)
VMEM = pl.BlockSpec(memory_space=pltpu.VMEM)


def permute(value, pairs):
    return lax.ppermute(value, "blk", pairs)


def relay(parts, member):
    across = [(m, m ^ 1) for m in range(8)]
    near = [(m, m ^ 2) for m in range(8)]
    distant = [(m, m + 4) for m in range(4)]
    beside, back, mid, up = [(4, 5)], [(4, 0), (5, 1)], [(4, 2), (5, 3)], [(4, 6), (5, 7)]
    level = member // 2
    a, b, c, e_halves, n_halves = parts

    def slabs(own):
        cur = jnp.where(member < 4, own, permute(own, distant))
        far = permute(cur, near)
        over = permute(cur, across)
        return cur, far, over, permute(far, across)

    def halves(low, high):
        half = jnp.where(member == 5, permute(high, beside), low)
        to_up = permute(half, up)
        to_back = permute(half, back)
        to_mid = permute(half, mid)
        half = jnp.where(level == 2, half, jnp.where(level == 3, to_up, jnp.where(level == 0, to_back, to_mid)))
        return half, permute(half, across)

    early, late = halves(*e_halves), halves(*n_halves)
    return (slabs(a), early), (slabs(b), late), (slabs(c), late)


def placed_slabs(member, refs):
    x = lax.rem(member, 2)
    even = lax.rem(lax.div(member, 2), 2) == 0
    near, far = jnp.where(even, x, 2 + x), jnp.where(even, 2 + x, x)
    over, overfar = jnp.where(even, 1 - x, 3 - x), jnp.where(even, 3 - x, 1 - x)
    return tuple(zip(refs, (near, far, over, overfar)))


def start_first(member, refs, target, sems):
    if len(refs) == 1:
        copies = [pltpu.make_async_copy(refs[0].at[pl.ds(0, TICKS - 1)], target.at[pl.ds(0, TICKS - 1)], sems.at[0])]
    else:
        copies = [
            pltpu.make_async_copy(ref, target.at[slab], sems.at[i])
            for i, (ref, slab) in enumerate(placed_slabs(member, refs))
        ]
    for copy in copies:
        copy.start()
    return copies


def start_last(member, refs, target, sems, first_row, rows):
    if len(refs) == 1:
        copies = [pltpu.make_async_copy(refs[0].at[TICKS - 1], target, sems.at[0])]
        copies[0].start()
        return copies
    half, overhalf = refs
    x = lax.rem(member, 2)
    split = half.shape[0]
    low = max(0, min(rows, split - first_row))
    pieces = []
    if low:
        pieces.append((0, first_row, 0, low))
    if rows - low:
        pieces.append((1, first_row + low - split, low, rows - low))

    def copy(ref, number):
        _, source, to, count = pieces[number]
        return pltpu.make_async_copy(
            ref.at[pl.ds(source, count)], target.at[pl.ds(to, count)], sems.at[number]
        )

    for which in (0, 1):

        @pl.when(x == which)
        def _(which=which):
            for number, piece in enumerate(pieces):
                copy(half if piece[0] == which else overhalf, number).start()

    return [copy(half, number) for number in range(len(pieces))]


def wait_all(copies):
    for copy in copies:
        copy.wait()


def cut(ranges):
    left = sum(n for _, n in ranges) // 2
    low, high = [], []
    for start, n in ranges:
        take = min(left, n)
        if take:
            low.append((start, take))
        if n - take:
            high.append((start + take, n - take))
        left -= take
    return low, high


def pack_kernel(pieces, front, *rest):
    outs, (held, sems) = rest[: len(pieces)], rest[len(pieces) :]
    copies, at = [], 0
    for ranges in pieces:
        for start, count in ranges:
            copies.append(
                pltpu.make_async_copy(
                    front.at[pl.ds(start, count), pl.ds(0, P_SIZE)], held.at[pl.ds(at, count), :], sems.at[len(copies)]
                )
            )
            copies[-1].start()
            at += count
    at, number = 0, 0
    for ranges, out in zip(pieces, outs):
        to = 0
        for _, count in ranges:
            copies[number].wait()
            out[pl.ds(to, count), :] = held[pl.ds(at, count), :].astype(jnp.bfloat16)
            at, to, number = at + count, to + count, number + 1


def pack(front, pieces):
    sizes = [sum(n for _, n in ranges) for ranges in pieces]
    return pl.pallas_call(
        functools.partial(pack_kernel, pieces),
        out_shape=tuple(jax.ShapeDtypeStruct((n, P_SIZE), jnp.bfloat16) for n in sizes),
        in_specs=[ANY],
        out_specs=(VMEM,) * len(sizes),
        scratch_shapes=[
            pltpu.VMEM((sum(sizes), P_SIZE), jnp.float32),
            pltpu.SemaphoreType.DMA((sum(len(r) for r in pieces),)),
        ],
    )(front)


def split(value):
    high = value.astype(jnp.bfloat16)
    return high, (value - high.astype(jnp.float32)).astype(jnp.bfloat16)


def dot3(left, right):
    (left_high, left_low), (right_high, right_low) = left, right
    dot = functools.partial(jnp.dot, preferred_element_type=jnp.float32)
    return dot(left_high, right_high) + (dot(left_low, right_high) + dot(left_high, right_low))


def dot2(left, right):
    dot = functools.partial(jnp.dot, preferred_element_type=jnp.float32)
    return dot(left, right[0]) + dot(left, right[1])


def diagonal_inverse(block):
    size = block.shape[0]
    row = lax.broadcasted_iota(jnp.int32, (size, size), 0)
    col = lax.broadcasted_iota(jnp.int32, (size, size), 1)
    on = row == col
    kept = jnp.where(on, block, 0.0)
    down = 1.0 / jnp.sum(kept, axis=1, keepdims=True)
    right = 1.0 / jnp.sum(kept, axis=0, keepdims=True)
    twice = jnp.where(on, 2.0, 0.0)
    parts = split(down * (twice - block * right))
    block_parts = split(block)
    for _ in range(NEWTON - 1):
        parts = split(dot3(parts, split(twice - dot3(block_parts, parts))))
    return parts


def minus_dot(value, left, right):
    return value - jnp.dot(left, right, preferred_element_type=jnp.float32)


def minus_dot(value, left, right):
    return value - jnp.dot(left, right, preferred_element_type=jnp.float32)


def pivot_kernel(counts, width, member_ref, front, *rest):
    firsts, lasts = rest[: counts[0]], rest[counts[0] : sum(counts)]
    out, w_out, raw, mat, own, inv, sems, last_sems, own_sems = rest[sum(counts) :]
    member = member_ref[0]
    p, rows = P_SIZE, TICKS * P_SIZE
    copies = start_first(member, firsts, raw, sems)
    copies += start_last(member, lasts, raw.at[TICKS - 1], last_sems, 0, rows)
    loads = [
        pltpu.make_async_copy(
            front.at[pl.ds(t * width, p), :], own.at[pl.ds(t * p, p), :], own_sems.at[t]
        )
        for t in range(TICKS)
    ]
    for load in loads:
        load.start()
    wait_all(copies)
    x = diagonal_inverse(raw[0, :p, :].astype(jnp.float32))
    wait_all(loads)
    for t in range(TICKS):
        lo, below = t * p, (t + 1) * p
        inv[0, t], inv[1, t] = x
        if below == rows:
            break
        column = mat[t, below:, :] if t else raw[t, below:, :]
        mult = dot3(split(column), x) if t else dot2(column, x)
        panel = mult.astype(jnp.bfloat16)
        for s in range(t + 1, TICKS):
            if t:
                urows = mat[s, lo:below, :].astype(jnp.bfloat16)
                raw[s, lo:below, :] = urows
                rest_rows = mat[s, below:, :]
            else:
                urows = raw[s, lo:below, :]
                rest_rows = raw[s, below:, :].astype(jnp.float32)
            mat[s, below:, :] = minus_dot(rest_rows, panel, urows)
            if s == t + 1:
                x = diagonal_inverse(mat[s, below : below + p, :])
        urows = own[lo:below, :].astype(jnp.bfloat16)
        own[below:, p:] = minus_dot(own[below:, p:], panel, urows[:, p:])
        left = own[below:, :p]
        live = (member >= TICKS) | (member > t)
        changed = jnp.where(live, minus_dot(left, panel, urows[:, :p]), left)
        own[below:, :p] = jnp.where(member == t, mult, changed)

    stores = [
        pltpu.make_async_copy(
            own.at[pl.ds(t * p, p), :], out.at[pl.ds(t * width, p), :], own_sems.at[t]
        )
        for t in range(TICKS)
    ]
    for store in stores:
        store.start()
    row = lax.broadcasted_iota(jnp.int32, (p, width), 0)
    col = lax.broadcasted_iota(jnp.int32, (p, width), 1)
    owner = (member < TICKS) & (col < p)
    for t in reversed(range(TICKS)):
        lo, hi = t * p, (t + 1) * p
        unit = jnp.where((row == col) & (member == t), -1.0, 0.0)
        side = jnp.where(owner, unit, own[lo:hi, :])
        for s in range(t + 1, TICKS):
            side = minus_dot(side, raw[s, lo:hi, :], w_out[s * p : (s + 1) * p, :])
        w_out[lo:hi, :] = dot3((inv[0, t], inv[1, t]), split(side)).astype(jnp.bfloat16)
    wait_all(stores)


def pivot_rows(member, front, bufs):
    order, width = front.shape
    p, rows = P_SIZE, TICKS * P_SIZE
    counts = tuple(len(b) for b in bufs)
    return pl.pallas_call(
        functools.partial(pivot_kernel, counts, width),
        name="pivot_rows",
        out_shape=(
            jax.ShapeDtypeStruct((order, width), jnp.float32),
            jax.ShapeDtypeStruct((rows, width), jnp.bfloat16),
        ),
        in_specs=[SMEM, ANY] + [ANY] * sum(counts),
        out_specs=(ANY, VMEM),
        scratch_shapes=[
            pltpu.VMEM((TICKS, rows, p), jnp.bfloat16),
            pltpu.VMEM((TICKS, rows, p), jnp.float32),
            pltpu.VMEM((rows, width), jnp.float32),
            pltpu.VMEM((2, TICKS, p, p), jnp.bfloat16),
            pltpu.SemaphoreType.DMA((4,)),
            pltpu.SemaphoreType.DMA((2,)),
            pltpu.SemaphoreType.DMA((TICKS,)),
        ],
    )(member, front, *bufs[0], *bufs[1])


def other_kernel(counts, ranges, first_row, tail, member_ref, dest_ref, slot_ref, w, front, out_in, *rest):
    firsts, lasts = rest[: counts[0]], rest[counts[0] : sum(counts)]
    if tail:
        out, outgoing, raw, base, sems, last_sems, base_sems = rest[sum(counts) :]
    else:
        out, raw, base, sems, last_sems, base_sems = rest[sum(counts) :]
    member = member_ref[0]
    rows, width = base.shape
    copies = start_first(member, firsts, raw, sems)
    copies += start_last(member, lasts, raw.at[TICKS - 1], last_sems, first_row, rows)
    loads = [
        pltpu.make_async_copy(front.at[pl.ds(src, n), :], base.at[pl.ds(dst, n), :], base_sems.at[i])
        for i, (src, dst, n) in enumerate(ranges)
    ]
    for load in loads:
        load.start()
    wait_all(copies)
    wait_all(loads)
    keep = (member >= TICKS) | (lax.broadcasted_iota(jnp.int32, (RB, width), 1) >= P_SIZE)

    def tile(src, dst, sem, i, carry):
        at = pl.ds(pl.multiple_of(dst + i * RB, RB), RB)
        total = jnp.where(keep, base[at, :], 0.0)
        for s in range(TICKS):
            total = minus_dot(total, raw[s, at, :], w[s * P_SIZE : (s + 1) * P_SIZE, :])
        base[at, :] = total
        if tail:
            outgoing[dest_ref[i], slot_ref[i]] = jnp.where(keep, total, 0.0).astype(jnp.bfloat16)
        pltpu.make_async_copy(
            base.at[at, :], out.at[pl.ds(pl.multiple_of(src + i * RB, RB), RB), :], sem
        ).start()
        return carry

    for number, (src, dst, n) in enumerate(ranges):
        lax.fori_loop(0, n // RB, functools.partial(tile, src, dst, base_sems.at[number]), 0)
    for number, (src, dst, n) in enumerate(ranges):
        pltpu.make_async_copy(
            base.at[pl.ds(dst, n), :], out.at[pl.ds(src, n), :], base_sems.at[number]
        ).wait()


def other_rows(member, dest, slot, w, front, out, bufs, ranges, first_row, groups=0):
    order, width = front.shape
    rows = sum(n for _, _, n in ranges)
    shapes = [jax.ShapeDtypeStruct((order, width), jnp.float32)]
    specs = [ANY]
    if groups:
        shapes.append(jax.ShapeDtypeStruct((groups, CAP, RB, width), jnp.bfloat16))
        specs.append(VMEM)
    counts = tuple(len(b) for b in bufs)
    return pl.pallas_call(
        functools.partial(other_kernel, counts, ranges, first_row, bool(groups)),
        name="tail_rows" if groups else "middle_rows",
        out_shape=tuple(shapes),
        in_specs=[SMEM, SMEM, SMEM, VMEM, ANY, ANY] + [ANY] * sum(counts),
        out_specs=tuple(specs),
        input_output_aliases={5: 0},
        scratch_shapes=[
            pltpu.VMEM((TICKS, rows, P_SIZE), jnp.bfloat16),
            pltpu.VMEM((rows, width), jnp.float32),
            pltpu.SemaphoreType.DMA((4,)),
            pltpu.SemaphoreType.DMA((2,)),
            pltpu.SemaphoreType.DMA((len(ranges),)),
        ],
    )(member, dest, slot, w, front, out, *bufs[0], *bufs[1])


def routes(parent_group, row_block):
    groups = lax.axis_size("front")
    dest = parent_group.reshape(NB)
    target = row_block.reshape(NB)
    number = jnp.arange(NB)
    earlier = (dest[None, :] == dest[:, None]) & (number[None, :] < number[:, None])
    slot = jnp.sum(earlier.astype(jnp.int32), axis=1)
    pick = (dest[None, None, :] == jnp.arange(groups, dtype=jnp.int32)[:, None, None]) & (
        slot[None, None, :] == jnp.arange(CAP, dtype=jnp.int32)[None, :, None]
    )
    address = jnp.sum(jnp.where(pick, target[None, None, :] + 1, 0), axis=2) - 1
    received = lax.all_to_all(address, "front", split_axis=0, concat_axis=0, tiled=True)
    return dest, slot, received.reshape(groups * CAP)


def add_kernel(address_ref, incoming, base, out):
    out[...] = base[...]
    for i in range(incoming.shape[0]):
        to = address_ref[i]

        @pl.when(to >= 0)
        def _(i=i, to=to):
            at = pl.ds(pl.multiple_of(to * RB, RB), RB)
            out[at, :] = out[at, :] + incoming[i].astype(jnp.float32)


def add_blocks(address, incoming, parent_base):
    groups, cap, rows, width = incoming.shape
    return pl.pallas_call(
        add_kernel,
        name="add_blocks",
        out_shape=jax.ShapeDtypeStruct(parent_base.shape, parent_base.dtype),
        in_specs=[SMEM, VMEM, VMEM],
        out_specs=VMEM,
    )(address, incoming.reshape(groups * cap, rows, width), parent_base)


def local(front, parent_group, row_block, parent_base):
    order, width = front.shape
    member = lax.axis_index("blk")
    holder = member.reshape(1).astype(jnp.int32)
    p, top = P_SIZE, TICKS * width
    tail_n = NB * RB
    tail_at = order - tail_n
    pivot_ranges = [(t * width, p) for t in range(TICKS)]
    tail_ranges = [(tail_at, tail_n)]
    middle_ranges = [(t * width + p, width - p) for t in range(TICKS)]
    if tail_at > top:
        middle_ranges.append((top, tail_at - top))
    middle, at = [], 0
    for start, count in middle_ranges:
        middle.append((start, at, count))
        at += count
    if lax.axis_size("blk") == 8:
        own_p, *e_halves = pack(front, [pivot_ranges, *cut(pivot_ranges)])
        own_t, own_m, *n_halves = pack(front, [tail_ranges, middle_ranges, *cut(tail_ranges + middle_ranges)])
        sets = relay((own_p, own_t, own_m, e_halves, n_halves), member)
    else:
        own_p, own_t, own_m = pack(front, [pivot_ranges, tail_ranges, middle_ranges])
        sets = tuple(((lax.all_gather(s, "blk")[:TICKS],),) * 2 for s in (own_p, own_t, own_m))
    dest, slot, address = routes(parent_group, row_block)
    out, w = pivot_rows(holder, front, sets[0])
    out, outgoing = other_rows(
        holder, dest, slot, w, front, out, sets[1], [(tail_at, 0, tail_n)], 0, lax.axis_size("front")
    )
    incoming = lax.all_to_all(outgoing, "front", split_axis=0, concat_axis=0, tiled=True)
    (factored,) = other_rows(holder, dest, slot, w, front, out, sets[2], middle, tail_n)
    assembled = add_blocks(address, incoming, parent_base)
    return (factored, assembled)


def solution(mesh):
    placed = (
        P("front", "blk"),
        P("front", "blk", None, None),
        P("front", "blk", None),
        P("front", "blk"),
    )
    return jax.shard_map(
        local,
        mesh=mesh,
        in_specs=placed,
        out_specs=(P("front", "blk"), P("front", "blk")),
        check_vma=False,
    )
```

```python
import functools

import jax
import jax.numpy as jnp
from jax import lax
from jax.experimental import pallas as pl
from jax.experimental.pallas import tpu as pltpu
from jax.sharding import PartitionSpec as P


P_SIZE = 256
TICKS = 5
NEWTON = 2
RB = 128
NB = 6
CAP = 2
ANY = pl.BlockSpec(memory_space=pl.ANY)
SMEM = pl.BlockSpec(memory_space=pltpu.SMEM)
VMEM = pl.BlockSpec(memory_space=pltpu.VMEM)


def permute(value, pairs):
    return lax.ppermute(value, "blk", pairs)


def relay(parts, member):
    across = [(m, m ^ 1) for m in range(8)]
    near = [(m, m ^ 2) for m in range(8)]
    distant = [(m, m + 4) for m in range(4)]
    beside, back, mid, up = [(4, 5)], [(4, 0), (5, 1)], [(4, 2), (5, 3)], [(4, 6), (5, 7)]
    level = member // 2
    a, b, c, e_halves, n = parts

    def slabs(own):
        cur = jnp.where(member < 4, own, permute(own, distant))
        far = permute(cur, near)
        over = permute(cur, across)
        return cur, far, over, permute(far, across)

    def halves(low, high):
        half = jnp.where(member == 5, permute(high, beside), low)
        to_up = permute(half, up)
        to_back = permute(half, back)
        to_mid = permute(half, mid)
        half = jnp.where(level == 2, half, jnp.where(level == 3, to_up, jnp.where(level == 0, to_back, to_mid)))
        return half, permute(half, across)

    def whole(own):
        rows = jnp.where(member == 5, permute(own, beside), own)
        to_up = permute(rows, up)
        to_back = permute(rows, back)
        to_mid = permute(rows, mid)
        return (
            jnp.where(level == 2, rows, jnp.where(level == 3, to_up, jnp.where(level == 0, to_back, to_mid))),
        )

    early, late = halves(*e_halves), whole(n)
    return (slabs(a), early), (slabs(b), late), (slabs(c), late)


def placed_slabs(member, refs):
    x = lax.rem(member, 2)
    even = lax.rem(lax.div(member, 2), 2) == 0
    near, far = jnp.where(even, x, 2 + x), jnp.where(even, 2 + x, x)
    over, overfar = jnp.where(even, 1 - x, 3 - x), jnp.where(even, 3 - x, 1 - x)
    return tuple(zip(refs, (near, far, over, overfar)))


def start_first(member, refs, target, sems):
    if len(refs) == 1:
        copies = [pltpu.make_async_copy(refs[0].at[pl.ds(0, TICKS - 1)], target.at[pl.ds(0, TICKS - 1)], sems.at[0])]
    else:
        copies = [
            pltpu.make_async_copy(ref, target.at[slab], sems.at[i])
            for i, (ref, slab) in enumerate(placed_slabs(member, refs))
        ]
    for copy in copies:
        copy.start()
    return copies


def start_last(member, refs, target, sems, first_row, rows):
    if len(refs) == 1 and len(refs[0].shape) == 3:
        copies = [pltpu.make_async_copy(refs[0].at[TICKS - 1], target, sems.at[0])]
        copies[0].start()
        return copies
    if len(refs) == 1:
        copies = [pltpu.make_async_copy(refs[0].at[pl.ds(first_row, rows)], target, sems.at[0])]
        copies[0].start()
        return copies
    half, overhalf = refs
    x = lax.rem(member, 2)
    split = half.shape[0]
    low = max(0, min(rows, split - first_row))
    pieces = []
    if low:
        pieces.append((0, first_row, 0, low))
    if rows - low:
        pieces.append((1, first_row + low - split, low, rows - low))

    def copy(ref, number):
        _, source, to, count = pieces[number]
        return pltpu.make_async_copy(
            ref.at[pl.ds(source, count)], target.at[pl.ds(to, count)], sems.at[number]
        )

    for which in (0, 1):

        @pl.when(x == which)
        def _(which=which):
            for number, piece in enumerate(pieces):
                copy(half if piece[0] == which else overhalf, number).start()

    return [copy(half, number) for number in range(len(pieces))]


def wait_all(copies):
    for copy in copies:
        copy.wait()


def cut(ranges):
    left = sum(n for _, n in ranges) // 2
    low, high = [], []
    for start, n in ranges:
        take = min(left, n)
        if take:
            low.append((start, take))
        if n - take:
            high.append((start + take, n - take))
        left -= take
    return low, high


def pack_kernel(pieces, front, *rest):
    outs, (held, sems) = rest[: len(pieces)], rest[len(pieces) :]
    copies, at = [], 0
    for ranges in pieces:
        for start, count in ranges:
            copies.append(
                pltpu.make_async_copy(
                    front.at[pl.ds(start, count), pl.ds(0, P_SIZE)], held.at[pl.ds(at, count), :], sems.at[len(copies)]
                )
            )
            copies[-1].start()
            at += count
    at, number = 0, 0
    for ranges, out in zip(pieces, outs):
        to = 0
        for _, count in ranges:
            copies[number].wait()
            out[pl.ds(to, count), :] = held[pl.ds(at, count), :].astype(jnp.bfloat16)
            at, to, number = at + count, to + count, number + 1


def pack(front, pieces):
    sizes = [sum(n for _, n in ranges) for ranges in pieces]
    return pl.pallas_call(
        functools.partial(pack_kernel, pieces),
        out_shape=tuple(jax.ShapeDtypeStruct((n, P_SIZE), jnp.bfloat16) for n in sizes),
        in_specs=[ANY],
        out_specs=(VMEM,) * len(sizes),
        scratch_shapes=[
            pltpu.VMEM((sum(sizes), P_SIZE), jnp.float32),
            pltpu.SemaphoreType.DMA((sum(len(r) for r in pieces),)),
        ],
    )(front)


def split(value):
    high = value.astype(jnp.bfloat16)
    return high, (value - high.astype(jnp.float32)).astype(jnp.bfloat16)


def dot3(left, right):
    (left_high, left_low), (right_high, right_low) = left, right
    dot = functools.partial(jnp.dot, preferred_element_type=jnp.float32)
    return dot(left_high, right_high) + (dot(left_low, right_high) + dot(left_high, right_low))


def dot2(left, right):
    dot = functools.partial(jnp.dot, preferred_element_type=jnp.float32)
    return dot(left, right[0]) + dot(left, right[1])


def diagonal_inverse(block):
    size = block.shape[0]
    row = lax.broadcasted_iota(jnp.int32, (size, size), 0)
    col = lax.broadcasted_iota(jnp.int32, (size, size), 1)
    on = row == col
    kept = jnp.where(on, block, 0.0)
    down = 1.0 / jnp.sum(kept, axis=1, keepdims=True)
    right = 1.0 / jnp.sum(kept, axis=0, keepdims=True)
    twice = jnp.where(on, 2.0, 0.0)
    parts = split(down * (twice - block * right))
    block_parts = split(block)
    for _ in range(NEWTON - 1):
        parts = split(dot3(parts, split(twice - dot3(block_parts, parts))))
    return parts


def minus_dot(value, left, right):
    return value - jnp.dot(left, right, preferred_element_type=jnp.float32)


def minus_dot(value, left, right):
    return value - jnp.dot(left, right, preferred_element_type=jnp.float32)


def pivot_kernel(counts, width, member_ref, front, *rest):
    firsts, lasts = rest[: counts[0]], rest[counts[0] : sum(counts)]
    out, w_out, raw, mat, own, inv, sems, last_sems, own_sems = rest[sum(counts) :]
    member = member_ref[0]
    p, rows = P_SIZE, TICKS * P_SIZE
    copies = start_first(member, firsts, raw, sems)
    copies += start_last(member, lasts, raw.at[TICKS - 1], last_sems, 0, rows)
    loads = [
        pltpu.make_async_copy(
            front.at[pl.ds(t * width, p), :], own.at[pl.ds(t * p, p), :], own_sems.at[t]
        )
        for t in range(TICKS)
    ]
    for load in loads:
        load.start()
    wait_all(copies)
    x = diagonal_inverse(raw[0, :p, :].astype(jnp.float32))
    wait_all(loads)
    for t in range(TICKS):
        lo, below = t * p, (t + 1) * p
        inv[0, t], inv[1, t] = x
        if below == rows:
            break
        column = mat[t, below:, :] if t else raw[t, below:, :]
        mult = dot3(split(column), x) if t else dot2(column, x)
        panel = mult.astype(jnp.bfloat16)
        for s in range(t + 1, TICKS):
            if t:
                urows = mat[s, lo:below, :].astype(jnp.bfloat16)
                raw[s, lo:below, :] = urows
                rest_rows = mat[s, below:, :]
            else:
                urows = raw[s, lo:below, :]
                rest_rows = raw[s, below:, :].astype(jnp.float32)
            mat[s, below:, :] = minus_dot(rest_rows, panel, urows)
            if s == t + 1:
                x = diagonal_inverse(mat[s, below : below + p, :])
        urows = own[lo:below, :].astype(jnp.bfloat16)
        own[below:, p:] = minus_dot(own[below:, p:], panel, urows[:, p:])
        left = own[below:, :p]
        live = (member >= TICKS) | (member > t)
        changed = jnp.where(live, minus_dot(left, panel, urows[:, :p]), left)
        own[below:, :p] = jnp.where(member == t, mult, changed)

    stores = [
        pltpu.make_async_copy(
            own.at[pl.ds(t * p, p), :], out.at[pl.ds(t * width, p), :], own_sems.at[t]
        )
        for t in range(TICKS)
    ]
    for store in stores:
        store.start()
    row = lax.broadcasted_iota(jnp.int32, (p, width), 0)
    col = lax.broadcasted_iota(jnp.int32, (p, width), 1)
    owner = (member < TICKS) & (col < p)
    for t in reversed(range(TICKS)):
        lo, hi = t * p, (t + 1) * p
        unit = jnp.where((row == col) & (member == t), -1.0, 0.0)
        side = jnp.where(owner, unit, own[lo:hi, :])
        for s in range(t + 1, TICKS):
            side = minus_dot(side, raw[s, lo:hi, :], w_out[s * p : (s + 1) * p, :])
        w_out[lo:hi, :] = dot3((inv[0, t], inv[1, t]), split(side)).astype(jnp.bfloat16)
    wait_all(stores)


def pivot_rows(member, front, bufs):
    order, width = front.shape
    p, rows = P_SIZE, TICKS * P_SIZE
    counts = tuple(len(b) for b in bufs)
    return pl.pallas_call(
        functools.partial(pivot_kernel, counts, width),
        name="pivot_rows",
        out_shape=(
            jax.ShapeDtypeStruct((order, width), jnp.float32),
            jax.ShapeDtypeStruct((rows, width), jnp.bfloat16),
        ),
        in_specs=[SMEM, ANY] + [ANY] * sum(counts),
        out_specs=(ANY, VMEM),
        scratch_shapes=[
            pltpu.VMEM((TICKS, rows, p), jnp.bfloat16),
            pltpu.VMEM((TICKS, rows, p), jnp.float32),
            pltpu.VMEM((rows, width), jnp.float32),
            pltpu.VMEM((2, TICKS, p, p), jnp.bfloat16),
            pltpu.SemaphoreType.DMA((4,)),
            pltpu.SemaphoreType.DMA((2,)),
            pltpu.SemaphoreType.DMA((TICKS,)),
        ],
    )(member, front, *bufs[0], *bufs[1])


def other_kernel(counts, ranges, first_row, tail, member_ref, dest_ref, slot_ref, w, front, out_in, *rest):
    firsts, lasts = rest[: counts[0]], rest[counts[0] : sum(counts)]
    if tail:
        out, outgoing, raw, base, sems, last_sems, base_sems = rest[sum(counts) :]
    else:
        out, raw, base, sems, last_sems, base_sems = rest[sum(counts) :]
    member = member_ref[0]
    rows, width = base.shape
    copies = start_first(member, firsts, raw, sems)
    copies += start_last(member, lasts, raw.at[TICKS - 1], last_sems, first_row, rows)
    loads = [
        pltpu.make_async_copy(front.at[pl.ds(src, n), :], base.at[pl.ds(dst, n), :], base_sems.at[i])
        for i, (src, dst, n) in enumerate(ranges)
    ]
    for load in loads:
        load.start()
    wait_all(copies)
    wait_all(loads)
    keep = (member >= TICKS) | (lax.broadcasted_iota(jnp.int32, (RB, width), 1) >= P_SIZE)

    def tile(src, dst, sem, i, carry):
        at = pl.ds(pl.multiple_of(dst + i * RB, RB), RB)
        total = jnp.where(keep, base[at, :], 0.0)
        for s in range(TICKS):
            total = minus_dot(total, raw[s, at, :], w[s * P_SIZE : (s + 1) * P_SIZE, :])
        base[at, :] = total
        if tail:
            outgoing[dest_ref[i], slot_ref[i]] = jnp.where(keep, total, 0.0).astype(jnp.bfloat16)
        pltpu.make_async_copy(
            base.at[at, :], out.at[pl.ds(pl.multiple_of(src + i * RB, RB), RB), :], sem
        ).start()
        return carry

    for number, (src, dst, n) in enumerate(ranges):
        lax.fori_loop(0, n // RB, functools.partial(tile, src, dst, base_sems.at[number]), 0)
    for number, (src, dst, n) in enumerate(ranges):
        pltpu.make_async_copy(
            base.at[pl.ds(dst, n), :], out.at[pl.ds(src, n), :], base_sems.at[number]
        ).wait()


def other_rows(member, dest, slot, w, front, out, bufs, ranges, first_row, groups=0):
    order, width = front.shape
    rows = sum(n for _, _, n in ranges)
    shapes = [jax.ShapeDtypeStruct((order, width), jnp.float32)]
    specs = [ANY]
    if groups:
        shapes.append(jax.ShapeDtypeStruct((groups, CAP, RB, width), jnp.bfloat16))
        specs.append(VMEM)
    counts = tuple(len(b) for b in bufs)
    return pl.pallas_call(
        functools.partial(other_kernel, counts, ranges, first_row, bool(groups)),
        name="tail_rows" if groups else "middle_rows",
        out_shape=tuple(shapes),
        in_specs=[SMEM, SMEM, SMEM, VMEM, ANY, ANY] + [ANY] * sum(counts),
        out_specs=tuple(specs),
        input_output_aliases={5: 0},
        scratch_shapes=[
            pltpu.VMEM((TICKS, rows, P_SIZE), jnp.bfloat16),
            pltpu.VMEM((rows, width), jnp.float32),
            pltpu.SemaphoreType.DMA((4,)),
            pltpu.SemaphoreType.DMA((2,)),
            pltpu.SemaphoreType.DMA((len(ranges),)),
        ],
    )(member, dest, slot, w, front, out, *bufs[0], *bufs[1])


def routes(parent_group, row_block):
    groups = lax.axis_size("front")
    dest = parent_group.reshape(NB)
    target = row_block.reshape(NB)
    number = jnp.arange(NB)
    earlier = (dest[None, :] == dest[:, None]) & (number[None, :] < number[:, None])
    slot = jnp.sum(earlier.astype(jnp.int32), axis=1)
    pick = (dest[None, None, :] == jnp.arange(groups, dtype=jnp.int32)[:, None, None]) & (
        slot[None, None, :] == jnp.arange(CAP, dtype=jnp.int32)[None, :, None]
    )
    address = jnp.sum(jnp.where(pick, target[None, None, :] + 1, 0), axis=2) - 1
    received = lax.all_to_all(address, "front", split_axis=0, concat_axis=0, tiled=True)
    return dest, slot, received.reshape(groups * CAP)


def add_kernel(address_ref, incoming, base, out):
    out[...] = base[...]
    for i in range(incoming.shape[0]):
        to = address_ref[i]

        @pl.when(to >= 0)
        def _(i=i, to=to):
            at = pl.ds(pl.multiple_of(to * RB, RB), RB)
            out[at, :] = out[at, :] + incoming[i].astype(jnp.float32)


def add_blocks(address, incoming, parent_base):
    groups, cap, rows, width = incoming.shape
    return pl.pallas_call(
        add_kernel,
        name="add_blocks",
        out_shape=jax.ShapeDtypeStruct(parent_base.shape, parent_base.dtype),
        in_specs=[SMEM, VMEM, VMEM],
        out_specs=VMEM,
    )(address, incoming.reshape(groups * cap, rows, width), parent_base)


def local(front, parent_group, row_block, parent_base):
    order, width = front.shape
    member = lax.axis_index("blk")
    holder = member.reshape(1).astype(jnp.int32)
    p, top = P_SIZE, TICKS * width
    tail_n = NB * RB
    tail_at = order - tail_n
    pivot_ranges = [(t * width, p) for t in range(TICKS)]
    tail_ranges = [(tail_at, tail_n)]
    middle_ranges = [(t * width + p, width - p) for t in range(TICKS)]
    if tail_at > top:
        middle_ranges.append((top, tail_at - top))
    middle, at = [], 0
    for start, count in middle_ranges:
        middle.append((start, at, count))
        at += count
    if lax.axis_size("blk") == 8:
        own_p, *e_halves = pack(front, [pivot_ranges, *cut(pivot_ranges)])
        own_t, own_m, own_n = pack(front, [tail_ranges, middle_ranges, tail_ranges + middle_ranges])
        sets = relay((own_p, own_t, own_m, e_halves, own_n), member)
    else:
        own_p, own_t, own_m = pack(front, [pivot_ranges, tail_ranges, middle_ranges])
        sets = tuple(((lax.all_gather(s, "blk")[:TICKS],),) * 2 for s in (own_p, own_t, own_m))
    dest, slot, address = routes(parent_group, row_block)
    out, w = pivot_rows(holder, front, sets[0])
    out, outgoing = other_rows(
        holder, dest, slot, w, front, out, sets[1], [(tail_at, 0, tail_n)], 0, lax.axis_size("front")
    )
    incoming = lax.all_to_all(outgoing, "front", split_axis=0, concat_axis=0, tiled=True)
    (factored,) = other_rows(holder, dest, slot, w, front, out, sets[2], middle, tail_n)
    assembled = add_blocks(address, incoming, parent_base)
    return (factored, assembled)


def solution(mesh):
    placed = (
        P("front", "blk"),
        P("front", "blk", None, None),
        P("front", "blk", None),
        P("front", "blk"),
    )
    return jax.shard_map(
        local,
        mesh=mesh,
        in_specs=placed,
        out_specs=(P("front", "blk"), P("front", "blk")),
        check_vma=False,
    )
```

```python
import functools

import jax
import jax.numpy as jnp
from jax import lax
from jax.experimental import pallas as pl
from jax.experimental.pallas import tpu as pltpu
from jax.sharding import PartitionSpec as P


P_SIZE = 256
TICKS = 5
NEWTON = 2
RB = 128
NB = 6
CAP = 2
ANY = pl.BlockSpec(memory_space=pl.ANY)
SMEM = pl.BlockSpec(memory_space=pltpu.SMEM)
VMEM = pl.BlockSpec(memory_space=pltpu.VMEM)


def permute(value, pairs):
    return lax.ppermute(value, "blk", pairs)


def relay(parts, member):
    across = [(m, m ^ 1) for m in range(8)]
    near = [(m, m ^ 2) for m in range(8)]
    distant = [(m, m + 4) for m in range(4)]
    beside, back, mid, up = [(4, 5)], [(4, 0), (5, 1)], [(4, 2), (5, 3)], [(4, 6), (5, 7)]
    level = member // 2
    a, b, c, e_halves = parts

    def slabs(own):
        cur = jnp.where(member < 4, own, permute(own, distant))
        far = permute(cur, near)
        over = permute(cur, across)
        return cur, far, over, permute(far, across)

    def halves(low, high):
        half = jnp.where(member == 5, permute(high, beside), low)
        to_up = permute(half, up)
        to_back = permute(half, back)
        to_mid = permute(half, mid)
        half = jnp.where(level == 2, half, jnp.where(level == 3, to_up, jnp.where(level == 0, to_back, to_mid)))
        return half, permute(half, across)

    def whole(own):
        own = lax.optimization_barrier(own)
        rows = jnp.where(member == 5, permute(own, beside), own)
        to_up = permute(rows, up)
        to_back = permute(rows, back)
        to_mid = permute(rows, mid)
        return (
            jnp.where(level == 2, rows, jnp.where(level == 3, to_up, jnp.where(level == 0, to_back, to_mid))),
        )

    return ((slabs(a), halves(*e_halves)), (slabs(b), whole(b)), (slabs(c), whole(c)))


def placed_slabs(member, refs):
    x = lax.rem(member, 2)
    even = lax.rem(lax.div(member, 2), 2) == 0
    near, far = jnp.where(even, x, 2 + x), jnp.where(even, 2 + x, x)
    over, overfar = jnp.where(even, 1 - x, 3 - x), jnp.where(even, 3 - x, 1 - x)
    return tuple(zip(refs, (near, far, over, overfar)))


def start_first(member, refs, target, sems):
    if len(refs) == 1:
        copies = [pltpu.make_async_copy(refs[0].at[pl.ds(0, TICKS - 1)], target.at[pl.ds(0, TICKS - 1)], sems.at[0])]
    else:
        copies = [
            pltpu.make_async_copy(ref, target.at[slab], sems.at[i])
            for i, (ref, slab) in enumerate(placed_slabs(member, refs))
        ]
    for copy in copies:
        copy.start()
    return copies


def start_last(member, refs, target, sems, first_row, rows):
    if len(refs) == 1 and len(refs[0].shape) == 3:
        copies = [pltpu.make_async_copy(refs[0].at[TICKS - 1], target, sems.at[0])]
        copies[0].start()
        return copies
    if len(refs) == 1:
        copies = [pltpu.make_async_copy(refs[0].at[pl.ds(first_row, rows)], target, sems.at[0])]
        copies[0].start()
        return copies
    half, overhalf = refs
    x = lax.rem(member, 2)
    split = half.shape[0]
    low = max(0, min(rows, split - first_row))
    pieces = []
    if low:
        pieces.append((0, first_row, 0, low))
    if rows - low:
        pieces.append((1, first_row + low - split, low, rows - low))

    def copy(ref, number):
        _, source, to, count = pieces[number]
        return pltpu.make_async_copy(
            ref.at[pl.ds(source, count)], target.at[pl.ds(to, count)], sems.at[number]
        )

    for which in (0, 1):

        @pl.when(x == which)
        def _(which=which):
            for number, piece in enumerate(pieces):
                copy(half if piece[0] == which else overhalf, number).start()

    return [copy(half, number) for number in range(len(pieces))]


def wait_all(copies):
    for copy in copies:
        copy.wait()


def cut(ranges):
    left = sum(n for _, n in ranges) // 2
    low, high = [], []
    for start, n in ranges:
        take = min(left, n)
        if take:
            low.append((start, take))
        if n - take:
            high.append((start + take, n - take))
        left -= take
    return low, high


def pack_kernel(pieces, front, *rest):
    outs, (held, sems) = rest[: len(pieces)], rest[len(pieces) :]
    copies, at = [], 0
    for ranges in pieces:
        for start, count in ranges:
            copies.append(
                pltpu.make_async_copy(
                    front.at[pl.ds(start, count), pl.ds(0, P_SIZE)], held.at[pl.ds(at, count), :], sems.at[len(copies)]
                )
            )
            copies[-1].start()
            at += count
    at, number = 0, 0
    for ranges, out in zip(pieces, outs):
        to = 0
        for _, count in ranges:
            copies[number].wait()
            out[pl.ds(to, count), :] = held[pl.ds(at, count), :].astype(jnp.bfloat16)
            at, to, number = at + count, to + count, number + 1


def pack(front, pieces):
    sizes = [sum(n for _, n in ranges) for ranges in pieces]
    return pl.pallas_call(
        functools.partial(pack_kernel, pieces),
        out_shape=tuple(jax.ShapeDtypeStruct((n, P_SIZE), jnp.bfloat16) for n in sizes),
        in_specs=[ANY],
        out_specs=(VMEM,) * len(sizes),
        scratch_shapes=[
            pltpu.VMEM((sum(sizes), P_SIZE), jnp.float32),
            pltpu.SemaphoreType.DMA((sum(len(r) for r in pieces),)),
        ],
    )(front)


def split(value):
    high = value.astype(jnp.bfloat16)
    return high, (value - high.astype(jnp.float32)).astype(jnp.bfloat16)


def dot3(left, right):
    (left_high, left_low), (right_high, right_low) = left, right
    dot = functools.partial(jnp.dot, preferred_element_type=jnp.float32)
    return dot(left_high, right_high) + (dot(left_low, right_high) + dot(left_high, right_low))


def dot2(left, right):
    dot = functools.partial(jnp.dot, preferred_element_type=jnp.float32)
    return dot(left, right[0]) + dot(left, right[1])


def diagonal_inverse(block):
    size = block.shape[0]
    row = lax.broadcasted_iota(jnp.int32, (size, size), 0)
    col = lax.broadcasted_iota(jnp.int32, (size, size), 1)
    on = row == col
    kept = jnp.where(on, block, 0.0)
    down = 1.0 / jnp.sum(kept, axis=1, keepdims=True)
    right = 1.0 / jnp.sum(kept, axis=0, keepdims=True)
    twice = jnp.where(on, 2.0, 0.0)
    parts = split(down * (twice - block * right))
    block_parts = split(block)
    for _ in range(NEWTON - 1):
        parts = split(dot3(parts, split(twice - dot3(block_parts, parts))))
    return parts


def minus_dot(value, left, right):
    return value - jnp.dot(left, right, preferred_element_type=jnp.float32)


def minus_dot(value, left, right):
    return value - jnp.dot(left, right, preferred_element_type=jnp.float32)


def pivot_kernel(counts, width, member_ref, front, *rest):
    firsts, lasts = rest[: counts[0]], rest[counts[0] : sum(counts)]
    out, w_out, raw, mat, own, inv, sems, last_sems, own_sems = rest[sum(counts) :]
    member = member_ref[0]
    p, rows = P_SIZE, TICKS * P_SIZE
    copies = start_first(member, firsts, raw, sems)
    copies += start_last(member, lasts, raw.at[TICKS - 1], last_sems, 0, rows)
    loads = [
        pltpu.make_async_copy(
            front.at[pl.ds(t * width, p), :], own.at[pl.ds(t * p, p), :], own_sems.at[t]
        )
        for t in range(TICKS)
    ]
    for load in loads:
        load.start()
    wait_all(copies)
    x = diagonal_inverse(raw[0, :p, :].astype(jnp.float32))
    wait_all(loads)
    for t in range(TICKS):
        lo, below = t * p, (t + 1) * p
        inv[0, t], inv[1, t] = x
        if below == rows:
            break
        column = mat[t, below:, :] if t else raw[t, below:, :]
        mult = dot3(split(column), x) if t else dot2(column, x)
        panel = mult.astype(jnp.bfloat16)
        for s in range(t + 1, TICKS):
            if t:
                urows = mat[s, lo:below, :].astype(jnp.bfloat16)
                raw[s, lo:below, :] = urows
                rest_rows = mat[s, below:, :]
            else:
                urows = raw[s, lo:below, :]
                rest_rows = raw[s, below:, :].astype(jnp.float32)
            mat[s, below:, :] = minus_dot(rest_rows, panel, urows)
            if s == t + 1:
                x = diagonal_inverse(mat[s, below : below + p, :])
        urows = own[lo:below, :].astype(jnp.bfloat16)
        own[below:, p:] = minus_dot(own[below:, p:], panel, urows[:, p:])
        left = own[below:, :p]
        live = (member >= TICKS) | (member > t)
        changed = jnp.where(live, minus_dot(left, panel, urows[:, :p]), left)
        own[below:, :p] = jnp.where(member == t, mult, changed)

    stores = [
        pltpu.make_async_copy(
            own.at[pl.ds(t * p, p), :], out.at[pl.ds(t * width, p), :], own_sems.at[t]
        )
        for t in range(TICKS)
    ]
    for store in stores:
        store.start()
    row = lax.broadcasted_iota(jnp.int32, (p, width), 0)
    col = lax.broadcasted_iota(jnp.int32, (p, width), 1)
    owner = (member < TICKS) & (col < p)
    for t in reversed(range(TICKS)):
        lo, hi = t * p, (t + 1) * p
        unit = jnp.where((row == col) & (member == t), -1.0, 0.0)
        side = jnp.where(owner, unit, own[lo:hi, :])
        for s in range(t + 1, TICKS):
            side = minus_dot(side, raw[s, lo:hi, :], w_out[s * p : (s + 1) * p, :])
        w_out[lo:hi, :] = dot3((inv[0, t], inv[1, t]), split(side)).astype(jnp.bfloat16)
    wait_all(stores)


def pivot_rows(member, front, bufs):
    order, width = front.shape
    p, rows = P_SIZE, TICKS * P_SIZE
    counts = tuple(len(b) for b in bufs)
    return pl.pallas_call(
        functools.partial(pivot_kernel, counts, width),
        name="pivot_rows",
        out_shape=(
            jax.ShapeDtypeStruct((order, width), jnp.float32),
            jax.ShapeDtypeStruct((rows, width), jnp.bfloat16),
        ),
        in_specs=[SMEM, ANY] + [ANY] * sum(counts),
        out_specs=(ANY, VMEM),
        scratch_shapes=[
            pltpu.VMEM((TICKS, rows, p), jnp.bfloat16),
            pltpu.VMEM((TICKS, rows, p), jnp.float32),
            pltpu.VMEM((rows, width), jnp.float32),
            pltpu.VMEM((2, TICKS, p, p), jnp.bfloat16),
            pltpu.SemaphoreType.DMA((4,)),
            pltpu.SemaphoreType.DMA((2,)),
            pltpu.SemaphoreType.DMA((TICKS,)),
        ],
    )(member, front, *bufs[0], *bufs[1])


def other_kernel(counts, ranges, first_row, tail, member_ref, dest_ref, slot_ref, w, front, out_in, *rest):
    firsts, lasts = rest[: counts[0]], rest[counts[0] : sum(counts)]
    if tail:
        out, outgoing, raw, base, sems, last_sems, base_sems = rest[sum(counts) :]
    else:
        out, raw, base, sems, last_sems, base_sems = rest[sum(counts) :]
    member = member_ref[0]
    rows, width = base.shape
    copies = start_first(member, firsts, raw, sems)
    copies += start_last(member, lasts, raw.at[TICKS - 1], last_sems, first_row, rows)
    loads = [
        pltpu.make_async_copy(front.at[pl.ds(src, n), :], base.at[pl.ds(dst, n), :], base_sems.at[i])
        for i, (src, dst, n) in enumerate(ranges)
    ]
    for load in loads:
        load.start()
    wait_all(copies)
    wait_all(loads)
    keep = (member >= TICKS) | (lax.broadcasted_iota(jnp.int32, (RB, width), 1) >= P_SIZE)

    def tile(src, dst, sem, i, carry):
        at = pl.ds(pl.multiple_of(dst + i * RB, RB), RB)
        total = jnp.where(keep, base[at, :], 0.0)
        for s in range(TICKS):
            total = minus_dot(total, raw[s, at, :], w[s * P_SIZE : (s + 1) * P_SIZE, :])
        base[at, :] = total
        if tail:
            outgoing[dest_ref[i], slot_ref[i]] = jnp.where(keep, total, 0.0).astype(jnp.bfloat16)
        pltpu.make_async_copy(
            base.at[at, :], out.at[pl.ds(pl.multiple_of(src + i * RB, RB), RB), :], sem
        ).start()
        return carry

    for number, (src, dst, n) in enumerate(ranges):
        lax.fori_loop(0, n // RB, functools.partial(tile, src, dst, base_sems.at[number]), 0)
    for number, (src, dst, n) in enumerate(ranges):
        pltpu.make_async_copy(
            base.at[pl.ds(dst, n), :], out.at[pl.ds(src, n), :], base_sems.at[number]
        ).wait()


def other_rows(member, dest, slot, w, front, out, bufs, ranges, first_row, groups=0):
    order, width = front.shape
    rows = sum(n for _, _, n in ranges)
    shapes = [jax.ShapeDtypeStruct((order, width), jnp.float32)]
    specs = [ANY]
    if groups:
        shapes.append(jax.ShapeDtypeStruct((groups, CAP, RB, width), jnp.bfloat16))
        specs.append(VMEM)
    counts = tuple(len(b) for b in bufs)
    return pl.pallas_call(
        functools.partial(other_kernel, counts, ranges, first_row, bool(groups)),
        name="tail_rows" if groups else "middle_rows",
        out_shape=tuple(shapes),
        in_specs=[SMEM, SMEM, SMEM, VMEM, ANY, ANY] + [ANY] * sum(counts),
        out_specs=tuple(specs),
        input_output_aliases={5: 0},
        scratch_shapes=[
            pltpu.VMEM((TICKS, rows, P_SIZE), jnp.bfloat16),
            pltpu.VMEM((rows, width), jnp.float32),
            pltpu.SemaphoreType.DMA((4,)),
            pltpu.SemaphoreType.DMA((2,)),
            pltpu.SemaphoreType.DMA((len(ranges),)),
        ],
    )(member, dest, slot, w, front, out, *bufs[0], *bufs[1])


def routes(parent_group, row_block):
    groups = lax.axis_size("front")
    dest = parent_group.reshape(NB)
    target = row_block.reshape(NB)
    number = jnp.arange(NB)
    earlier = (dest[None, :] == dest[:, None]) & (number[None, :] < number[:, None])
    slot = jnp.sum(earlier.astype(jnp.int32), axis=1)
    pick = (dest[None, None, :] == jnp.arange(groups, dtype=jnp.int32)[:, None, None]) & (
        slot[None, None, :] == jnp.arange(CAP, dtype=jnp.int32)[None, :, None]
    )
    address = jnp.sum(jnp.where(pick, target[None, None, :] + 1, 0), axis=2) - 1
    received = lax.all_to_all(address, "front", split_axis=0, concat_axis=0, tiled=True)
    return dest, slot, received.reshape(groups * CAP)


def add_kernel(address_ref, incoming, base, out):
    out[...] = base[...]
    for i in range(incoming.shape[0]):
        to = address_ref[i]

        @pl.when(to >= 0)
        def _(i=i, to=to):
            at = pl.ds(pl.multiple_of(to * RB, RB), RB)
            out[at, :] = out[at, :] + incoming[i].astype(jnp.float32)


def add_blocks(address, incoming, parent_base):
    groups, cap, rows, width = incoming.shape
    return pl.pallas_call(
        add_kernel,
        name="add_blocks",
        out_shape=jax.ShapeDtypeStruct(parent_base.shape, parent_base.dtype),
        in_specs=[SMEM, VMEM, VMEM],
        out_specs=VMEM,
    )(address, incoming.reshape(groups * cap, rows, width), parent_base)


def local(front, parent_group, row_block, parent_base):
    order, width = front.shape
    member = lax.axis_index("blk")
    holder = member.reshape(1).astype(jnp.int32)
    p, top = P_SIZE, TICKS * width
    tail_n = NB * RB
    tail_at = order - tail_n
    pivot_ranges = [(t * width, p) for t in range(TICKS)]
    tail_ranges = [(tail_at, tail_n)]
    middle_ranges = [(t * width + p, width - p) for t in range(TICKS)]
    if tail_at > top:
        middle_ranges.append((top, tail_at - top))
    middle, at = [], 0
    for start, count in middle_ranges:
        middle.append((start, at, count))
        at += count
    if lax.axis_size("blk") == 8:
        own_p, *e_halves = pack(front, [pivot_ranges, *cut(pivot_ranges)])
        own_t, own_m = pack(front, [tail_ranges, middle_ranges])
        sets = relay((own_p, own_t, own_m, e_halves), member)
    else:
        own_p, own_t, own_m = pack(front, [pivot_ranges, tail_ranges, middle_ranges])
        sets = tuple(((lax.all_gather(s, "blk")[:TICKS],),) * 2 for s in (own_p, own_t, own_m))
    dest, slot, address = routes(parent_group, row_block)
    out, w = pivot_rows(holder, front, sets[0])
    out, outgoing = other_rows(
        holder, dest, slot, w, front, out, sets[1], [(tail_at, 0, tail_n)], 0, lax.axis_size("front")
    )
    incoming = lax.all_to_all(outgoing, "front", split_axis=0, concat_axis=0, tiled=True)
    (factored,) = other_rows(holder, dest, slot, w, front, out, sets[2], middle, 0)
    assembled = add_blocks(address, incoming, parent_base)
    return (factored, assembled)


def solution(mesh):
    placed = (
        P("front", "blk"),
        P("front", "blk", None, None),
        P("front", "blk", None),
        P("front", "blk"),
    )
    return jax.shard_map(
        local,
        mesh=mesh,
        in_specs=placed,
        out_specs=(P("front", "blk"), P("front", "blk")),
        check_vma=False,
    )
```

```python
import functools

import jax
import jax.numpy as jnp
from jax import lax
from jax.experimental import pallas as pl
from jax.experimental.pallas import tpu as pltpu
from jax.sharding import PartitionSpec as P


P_SIZE = 256
TICKS = 5
NEWTON = 2
RB = 128
NB = 6
CAP = 2
ANY = pl.BlockSpec(memory_space=pl.ANY)
SMEM = pl.BlockSpec(memory_space=pltpu.SMEM)
VMEM = pl.BlockSpec(memory_space=pltpu.VMEM)


def permute(value, pairs):
    return lax.ppermute(value, "blk", pairs)


def relay(parts, member):
    across = [(m, m ^ 1) for m in range(8)]
    near = [(m, m ^ 2) for m in range(8)]
    distant = [(m, m + 4) for m in range(4)]
    beside, back, mid, up = [(4, 5)], [(4, 0), (5, 1)], [(4, 2), (5, 3)], [(4, 6), (5, 7)]
    level = member // 2
    a, b, c, e_halves = parts

    def slabs(own):
        cur = jnp.where(member < 4, own, permute(own, distant))
        far = permute(cur, near)
        over = permute(cur, across)
        return cur, far, over, permute(far, across)

    def halves(low, high):
        half = jnp.where(member == 5, permute(high, beside), low)
        to_up = permute(half, up)
        to_back = permute(half, back)
        to_mid = permute(half, mid)
        half = jnp.where(level == 2, half, jnp.where(level == 3, to_up, jnp.where(level == 0, to_back, to_mid)))
        return half, permute(half, across)

    def whole(own):
        own = lax.optimization_barrier(own)
        rows = jnp.where(member == 5, permute(own, beside), own)
        to_up = permute(rows, up)
        to_back = permute(rows, back)
        to_mid = permute(rows, mid)
        return to_back, to_mid, rows, to_up

    return ((slabs(a), halves(*e_halves)), (slabs(b), whole(b)), (slabs(c), whole(c)))


def placed_slabs(member, refs):
    x = lax.rem(member, 2)
    even = lax.rem(lax.div(member, 2), 2) == 0
    near, far = jnp.where(even, x, 2 + x), jnp.where(even, 2 + x, x)
    over, overfar = jnp.where(even, 1 - x, 3 - x), jnp.where(even, 3 - x, 1 - x)
    return tuple(zip(refs, (near, far, over, overfar)))


def start_first(member, refs, target, sems):
    if len(refs) == 1:
        copies = [pltpu.make_async_copy(refs[0].at[pl.ds(0, TICKS - 1)], target.at[pl.ds(0, TICKS - 1)], sems.at[0])]
    else:
        copies = [
            pltpu.make_async_copy(ref, target.at[slab], sems.at[i])
            for i, (ref, slab) in enumerate(placed_slabs(member, refs))
        ]
    for copy in copies:
        copy.start()
    return copies


def start_last(member, refs, target, sems, first_row, rows):
    if len(refs) == 1 and len(refs[0].shape) == 3:
        copies = [pltpu.make_async_copy(refs[0].at[TICKS - 1], target, sems.at[0])]
        copies[0].start()
        return copies
    if len(refs) == 4:
        copies = [pltpu.make_async_copy(ref.at[pl.ds(0, rows)], target, sems.at[0]) for ref in refs]
        for level, copy in enumerate(copies):
            pl.when(lax.div(member, 2) == level)(copy.start)
        return copies[:1]
    half, overhalf = refs
    x = lax.rem(member, 2)
    split = half.shape[0]
    low = max(0, min(rows, split - first_row))
    pieces = []
    if low:
        pieces.append((0, first_row, 0, low))
    if rows - low:
        pieces.append((1, first_row + low - split, low, rows - low))

    def copy(ref, number):
        _, source, to, count = pieces[number]
        return pltpu.make_async_copy(
            ref.at[pl.ds(source, count)], target.at[pl.ds(to, count)], sems.at[number]
        )

    for which in (0, 1):

        @pl.when(x == which)
        def _(which=which):
            for number, piece in enumerate(pieces):
                copy(half if piece[0] == which else overhalf, number).start()

    return [copy(half, number) for number in range(len(pieces))]


def wait_all(copies):
    for copy in copies:
        copy.wait()


def cut(ranges):
    left = sum(n for _, n in ranges) // 2
    low, high = [], []
    for start, n in ranges:
        take = min(left, n)
        if take:
            low.append((start, take))
        if n - take:
            high.append((start + take, n - take))
        left -= take
    return low, high


def pack_kernel(pieces, front, *rest):
    outs, (held, sems) = rest[: len(pieces)], rest[len(pieces) :]
    copies, at = [], 0
    for ranges in pieces:
        for start, count in ranges:
            copies.append(
                pltpu.make_async_copy(
                    front.at[pl.ds(start, count), pl.ds(0, P_SIZE)], held.at[pl.ds(at, count), :], sems.at[len(copies)]
                )
            )
            copies[-1].start()
            at += count
    at, number = 0, 0
    for ranges, out in zip(pieces, outs):
        to = 0
        for _, count in ranges:
            copies[number].wait()
            out[pl.ds(to, count), :] = held[pl.ds(at, count), :].astype(jnp.bfloat16)
            at, to, number = at + count, to + count, number + 1


def pack(front, pieces):
    sizes = [sum(n for _, n in ranges) for ranges in pieces]
    return pl.pallas_call(
        functools.partial(pack_kernel, pieces),
        out_shape=tuple(jax.ShapeDtypeStruct((n, P_SIZE), jnp.bfloat16) for n in sizes),
        in_specs=[ANY],
        out_specs=(VMEM,) * len(sizes),
        scratch_shapes=[
            pltpu.VMEM((sum(sizes), P_SIZE), jnp.float32),
            pltpu.SemaphoreType.DMA((sum(len(r) for r in pieces),)),
        ],
    )(front)


def split(value):
    high = value.astype(jnp.bfloat16)
    return high, (value - high.astype(jnp.float32)).astype(jnp.bfloat16)


def dot3(left, right):
    (left_high, left_low), (right_high, right_low) = left, right
    dot = functools.partial(jnp.dot, preferred_element_type=jnp.float32)
    return dot(left_high, right_high) + (dot(left_low, right_high) + dot(left_high, right_low))


def dot2(left, right):
    dot = functools.partial(jnp.dot, preferred_element_type=jnp.float32)
    return dot(left, right[0]) + dot(left, right[1])


def diagonal_inverse(block):
    size = block.shape[0]
    row = lax.broadcasted_iota(jnp.int32, (size, size), 0)
    col = lax.broadcasted_iota(jnp.int32, (size, size), 1)
    on = row == col
    kept = jnp.where(on, block, 0.0)
    down = 1.0 / jnp.sum(kept, axis=1, keepdims=True)
    right = 1.0 / jnp.sum(kept, axis=0, keepdims=True)
    twice = jnp.where(on, 2.0, 0.0)
    parts = split(down * (twice - block * right))
    block_parts = split(block)
    for _ in range(NEWTON - 1):
        parts = split(dot3(parts, split(twice - dot3(block_parts, parts))))
    return parts


def minus_dot(value, left, right):
    return value - jnp.dot(left, right, preferred_element_type=jnp.float32)


def minus_dot(value, left, right):
    return value - jnp.dot(left, right, preferred_element_type=jnp.float32)


def pivot_kernel(counts, width, member_ref, front, *rest):
    firsts, lasts = rest[: counts[0]], rest[counts[0] : sum(counts)]
    out, w_out, raw, mat, own, inv, sems, last_sems, own_sems = rest[sum(counts) :]
    member = member_ref[0]
    p, rows = P_SIZE, TICKS * P_SIZE
    copies = start_first(member, firsts, raw, sems)
    copies += start_last(member, lasts, raw.at[TICKS - 1], last_sems, 0, rows)
    loads = [
        pltpu.make_async_copy(
            front.at[pl.ds(t * width, p), :], own.at[pl.ds(t * p, p), :], own_sems.at[t]
        )
        for t in range(TICKS)
    ]
    for load in loads:
        load.start()
    wait_all(copies)
    x = diagonal_inverse(raw[0, :p, :].astype(jnp.float32))
    wait_all(loads)
    for t in range(TICKS):
        lo, below = t * p, (t + 1) * p
        inv[0, t], inv[1, t] = x
        if below == rows:
            break
        column = mat[t, below:, :] if t else raw[t, below:, :]
        mult = dot3(split(column), x) if t else dot2(column, x)
        panel = mult.astype(jnp.bfloat16)
        for s in range(t + 1, TICKS):
            if t:
                urows = mat[s, lo:below, :].astype(jnp.bfloat16)
                raw[s, lo:below, :] = urows
                rest_rows = mat[s, below:, :]
            else:
                urows = raw[s, lo:below, :]
                rest_rows = raw[s, below:, :].astype(jnp.float32)
            mat[s, below:, :] = minus_dot(rest_rows, panel, urows)
            if s == t + 1:
                x = diagonal_inverse(mat[s, below : below + p, :])
        urows = own[lo:below, :].astype(jnp.bfloat16)
        own[below:, p:] = minus_dot(own[below:, p:], panel, urows[:, p:])
        left = own[below:, :p]
        live = (member >= TICKS) | (member > t)
        changed = jnp.where(live, minus_dot(left, panel, urows[:, :p]), left)
        own[below:, :p] = jnp.where(member == t, mult, changed)

    stores = [
        pltpu.make_async_copy(
            own.at[pl.ds(t * p, p), :], out.at[pl.ds(t * width, p), :], own_sems.at[t]
        )
        for t in range(TICKS)
    ]
    for store in stores:
        store.start()
    row = lax.broadcasted_iota(jnp.int32, (p, width), 0)
    col = lax.broadcasted_iota(jnp.int32, (p, width), 1)
    owner = (member < TICKS) & (col < p)
    for t in reversed(range(TICKS)):
        lo, hi = t * p, (t + 1) * p
        unit = jnp.where((row == col) & (member == t), -1.0, 0.0)
        side = jnp.where(owner, unit, own[lo:hi, :])
        for s in range(t + 1, TICKS):
            side = minus_dot(side, raw[s, lo:hi, :], w_out[s * p : (s + 1) * p, :])
        w_out[lo:hi, :] = dot3((inv[0, t], inv[1, t]), split(side)).astype(jnp.bfloat16)
    wait_all(stores)


def pivot_rows(member, front, bufs):
    order, width = front.shape
    p, rows = P_SIZE, TICKS * P_SIZE
    counts = tuple(len(b) for b in bufs)
    return pl.pallas_call(
        functools.partial(pivot_kernel, counts, width),
        name="pivot_rows",
        out_shape=(
            jax.ShapeDtypeStruct((order, width), jnp.float32),
            jax.ShapeDtypeStruct((rows, width), jnp.bfloat16),
        ),
        in_specs=[SMEM, ANY] + [ANY] * sum(counts),
        out_specs=(ANY, VMEM),
        scratch_shapes=[
            pltpu.VMEM((TICKS, rows, p), jnp.bfloat16),
            pltpu.VMEM((TICKS, rows, p), jnp.float32),
            pltpu.VMEM((rows, width), jnp.float32),
            pltpu.VMEM((2, TICKS, p, p), jnp.bfloat16),
            pltpu.SemaphoreType.DMA((4,)),
            pltpu.SemaphoreType.DMA((2,)),
            pltpu.SemaphoreType.DMA((TICKS,)),
        ],
    )(member, front, *bufs[0], *bufs[1])


def other_kernel(counts, ranges, first_row, tail, member_ref, dest_ref, slot_ref, w, front, out_in, *rest):
    firsts, lasts = rest[: counts[0]], rest[counts[0] : sum(counts)]
    if tail:
        out, outgoing, raw, base, sems, last_sems, base_sems = rest[sum(counts) :]
    else:
        out, raw, base, sems, last_sems, base_sems = rest[sum(counts) :]
    member = member_ref[0]
    rows, width = base.shape
    copies = start_first(member, firsts, raw, sems)
    copies += start_last(member, lasts, raw.at[TICKS - 1], last_sems, first_row, rows)
    loads = [
        pltpu.make_async_copy(front.at[pl.ds(src, n), :], base.at[pl.ds(dst, n), :], base_sems.at[i])
        for i, (src, dst, n) in enumerate(ranges)
    ]
    for load in loads:
        load.start()
    wait_all(copies)
    wait_all(loads)
    keep = (member >= TICKS) | (lax.broadcasted_iota(jnp.int32, (RB, width), 1) >= P_SIZE)

    def tile(src, dst, sem, i, carry):
        at = pl.ds(pl.multiple_of(dst + i * RB, RB), RB)
        total = jnp.where(keep, base[at, :], 0.0)
        for s in range(TICKS):
            total = minus_dot(total, raw[s, at, :], w[s * P_SIZE : (s + 1) * P_SIZE, :])
        base[at, :] = total
        if tail:
            outgoing[dest_ref[i], slot_ref[i]] = jnp.where(keep, total, 0.0).astype(jnp.bfloat16)
        pltpu.make_async_copy(
            base.at[at, :], out.at[pl.ds(pl.multiple_of(src + i * RB, RB), RB), :], sem
        ).start()
        return carry

    for number, (src, dst, n) in enumerate(ranges):
        lax.fori_loop(0, n // RB, functools.partial(tile, src, dst, base_sems.at[number]), 0)
    for number, (src, dst, n) in enumerate(ranges):
        pltpu.make_async_copy(
            base.at[pl.ds(dst, n), :], out.at[pl.ds(src, n), :], base_sems.at[number]
        ).wait()


def other_rows(member, dest, slot, w, front, out, bufs, ranges, first_row, groups=0):
    order, width = front.shape
    rows = sum(n for _, _, n in ranges)
    shapes = [jax.ShapeDtypeStruct((order, width), jnp.float32)]
    specs = [ANY]
    if groups:
        shapes.append(jax.ShapeDtypeStruct((groups, CAP, RB, width), jnp.bfloat16))
        specs.append(VMEM)
    counts = tuple(len(b) for b in bufs)
    return pl.pallas_call(
        functools.partial(other_kernel, counts, ranges, first_row, bool(groups)),
        name="tail_rows" if groups else "middle_rows",
        out_shape=tuple(shapes),
        in_specs=[SMEM, SMEM, SMEM, VMEM, ANY, ANY] + [ANY] * sum(counts),
        out_specs=tuple(specs),
        input_output_aliases={5: 0},
        scratch_shapes=[
            pltpu.VMEM((TICKS, rows, P_SIZE), jnp.bfloat16),
            pltpu.VMEM((rows, width), jnp.float32),
            pltpu.SemaphoreType.DMA((4,)),
            pltpu.SemaphoreType.DMA((2,)),
            pltpu.SemaphoreType.DMA((len(ranges),)),
        ],
    )(member, dest, slot, w, front, out, *bufs[0], *bufs[1])


def routes(parent_group, row_block):
    groups = lax.axis_size("front")
    dest = parent_group.reshape(NB)
    target = row_block.reshape(NB)
    number = jnp.arange(NB)
    earlier = (dest[None, :] == dest[:, None]) & (number[None, :] < number[:, None])
    slot = jnp.sum(earlier.astype(jnp.int32), axis=1)
    pick = (dest[None, None, :] == jnp.arange(groups, dtype=jnp.int32)[:, None, None]) & (
        slot[None, None, :] == jnp.arange(CAP, dtype=jnp.int32)[None, :, None]
    )
    address = jnp.sum(jnp.where(pick, target[None, None, :] + 1, 0), axis=2) - 1
    received = lax.all_to_all(address, "front", split_axis=0, concat_axis=0, tiled=True)
    return dest, slot, received.reshape(groups * CAP)


def add_kernel(address_ref, incoming, base, out):
    out[...] = base[...]
    for i in range(incoming.shape[0]):
        to = address_ref[i]

        @pl.when(to >= 0)
        def _(i=i, to=to):
            at = pl.ds(pl.multiple_of(to * RB, RB), RB)
            out[at, :] = out[at, :] + incoming[i].astype(jnp.float32)


def add_blocks(address, incoming, parent_base):
    groups, cap, rows, width = incoming.shape
    return pl.pallas_call(
        add_kernel,
        name="add_blocks",
        out_shape=jax.ShapeDtypeStruct(parent_base.shape, parent_base.dtype),
        in_specs=[SMEM, VMEM, VMEM],
        out_specs=VMEM,
    )(address, incoming.reshape(groups * cap, rows, width), parent_base)


def local(front, parent_group, row_block, parent_base):
    order, width = front.shape
    member = lax.axis_index("blk")
    holder = member.reshape(1).astype(jnp.int32)
    p, top = P_SIZE, TICKS * width
    tail_n = NB * RB
    tail_at = order - tail_n
    pivot_ranges = [(t * width, p) for t in range(TICKS)]
    tail_ranges = [(tail_at, tail_n)]
    middle_ranges = [(t * width + p, width - p) for t in range(TICKS)]
    if tail_at > top:
        middle_ranges.append((top, tail_at - top))
    middle, at = [], 0
    for start, count in middle_ranges:
        middle.append((start, at, count))
        at += count
    if lax.axis_size("blk") == 8:
        (own_p,) = pack(front, [pivot_ranges])
        *e_halves, own_t, own_m = pack(front, [*cut(pivot_ranges), tail_ranges, middle_ranges])
        sets = relay((own_p, own_t, own_m, e_halves), member)
    else:
        own_p, own_t, own_m = pack(front, [pivot_ranges, tail_ranges, middle_ranges])
        sets = tuple(((lax.all_gather(s, "blk")[:TICKS],),) * 2 for s in (own_p, own_t, own_m))
    dest, slot, address = routes(parent_group, row_block)
    out, w = pivot_rows(holder, front, sets[0])
    out, outgoing = other_rows(
        holder, dest, slot, w, front, out, sets[1], [(tail_at, 0, tail_n)], 0, lax.axis_size("front")
    )
    incoming = lax.all_to_all(outgoing, "front", split_axis=0, concat_axis=0, tiled=True)
    (factored,) = other_rows(holder, dest, slot, w, front, out, sets[2], middle, 0)
    assembled = add_blocks(address, incoming, parent_base)
    return (factored, assembled)


def solution(mesh):
    placed = (
        P("front", "blk"),
        P("front", "blk", None, None),
        P("front", "blk", None),
        P("front", "blk"),
    )
    return jax.shard_map(
        local,
        mesh=mesh,
        in_specs=placed,
        out_specs=(P("front", "blk"), P("front", "blk")),
        check_vma=False,
    )
```

```python
import functools

import jax
import jax.numpy as jnp
from jax import lax
from jax.experimental import pallas as pl
from jax.experimental.pallas import tpu as pltpu
from jax.sharding import PartitionSpec as P


P_SIZE = 256
TICKS = 5
NEWTON = 2
RB = 128
NB = 6
CAP = 2
CHUNK = 256
ANY = pl.BlockSpec(memory_space=pl.ANY)
SMEM = pl.BlockSpec(memory_space=pltpu.SMEM)
VMEM = pl.BlockSpec(memory_space=pltpu.VMEM)


def permute(value, pairs):
    return lax.ppermute(value, "blk", pairs)


def relay(parts, member):
    across = [(m, m ^ 1) for m in range(8)]
    near = [(m, m ^ 2) for m in range(8)]
    distant = [(m, m + 4) for m in range(4)]
    beside, back, mid, up = [(4, 5)], [(4, 0), (5, 1)], [(4, 2), (5, 3)], [(4, 6), (5, 7)]
    level = member // 2
    a, b, c, e_halves = parts

    def slabs(own):
        cur = jnp.where(member < 4, own, permute(own, distant))
        far = permute(cur, near)
        over = permute(cur, across)
        return cur, far, over, permute(far, across)

    def halves(low, high):
        half = jnp.where(member == 5, permute(high, beside), low)
        to_up = permute(half, up)
        to_back = permute(half, back)
        to_mid = permute(half, mid)
        half = jnp.where(level == 2, half, jnp.where(level == 3, to_up, jnp.where(level == 0, to_back, to_mid)))
        return half, permute(half, across)

    def whole(own):
        own = lax.optimization_barrier(own)
        rows = jnp.where(member == 5, permute(own, beside), own)
        to_up = permute(rows, up)
        to_back = permute(rows, back)
        to_mid = permute(rows, mid)
        return to_back, to_mid, rows, to_up

    return ((slabs(a), halves(*e_halves)), (slabs(b), whole(b)), (slabs(c), whole(c)))


def placed_slabs(member, refs):
    x = lax.rem(member, 2)
    even = lax.rem(lax.div(member, 2), 2) == 0
    near, far = jnp.where(even, x, 2 + x), jnp.where(even, 2 + x, x)
    over, overfar = jnp.where(even, 1 - x, 3 - x), jnp.where(even, 3 - x, 1 - x)
    return tuple(zip(refs, (near, far, over, overfar)))


def start_first(member, refs, target, sems, lo, n):
    at = pl.ds(lo, n)
    if len(refs) == 1:
        most = pl.ds(0, TICKS - 1)
        copies = [pltpu.make_async_copy(refs[0].at[most, at], target.at[most, at], sems.at[0])]
    else:
        copies = [
            pltpu.make_async_copy(ref.at[at], target.at[slab, at], sems.at[i])
            for i, (ref, slab) in enumerate(placed_slabs(member, refs))
        ]
    for copy in copies:
        copy.start()
    return copies


def start_last(member, refs, target, sem, lo, n):
    at = pl.ds(lo, n)
    if len(refs) == 1:
        copies = [pltpu.make_async_copy(refs[0].at[TICKS - 1, at], target.at[TICKS - 1, at], sem)]
        copies[0].start()
        return copies
    copies = [pltpu.make_async_copy(ref.at[at], target.at[TICKS - 1, at], sem) for ref in refs]
    for level, copy in enumerate(copies):
        pl.when(lax.div(member, 2) == level)(copy.start)
    return copies[:1]


def start_halves(member, refs, target, sems, rows):
    if len(refs) == 1:
        return start_last(member, refs, target, sems.at[0], 0, rows)
    half, overhalf = refs
    x, n = lax.rem(member, 2), rows // 2

    def copy(ref, number):
        return pltpu.make_async_copy(ref, target.at[TICKS - 1, pl.ds(number * n, n)], sems.at[number])

    for which in (0, 1):

        @pl.when(x == which)
        def _(which=which):
            copy(half, which).start()
            copy(overhalf, 1 - which).start()

    return [copy(half, 0), copy(half, 1)]


def wait_all(copies):
    for copy in copies:
        copy.wait()


def cut(ranges):
    left = sum(n for _, n in ranges) // 2
    low, high = [], []
    for start, n in ranges:
        take = min(left, n)
        if take:
            low.append((start, take))
        if n - take:
            high.append((start + take, n - take))
        left -= take
    return low, high


def pack_kernel(pieces, front, *rest):
    outs, (held, sems) = rest[: len(pieces)], rest[len(pieces) :]
    copies, at = [], 0
    for ranges in pieces:
        for start, count in ranges:
            copies.append(
                pltpu.make_async_copy(
                    front.at[pl.ds(start, count), pl.ds(0, P_SIZE)], held.at[pl.ds(at, count), :], sems.at[len(copies)]
                )
            )
            copies[-1].start()
            at += count
    at, number = 0, 0
    for ranges, out in zip(pieces, outs):
        to = 0
        for _, count in ranges:
            copies[number].wait()
            out[pl.ds(to, count), :] = held[pl.ds(at, count), :].astype(jnp.bfloat16)
            at, to, number = at + count, to + count, number + 1


def pack(front, pieces):
    sizes = [sum(n for _, n in ranges) for ranges in pieces]
    return pl.pallas_call(
        functools.partial(pack_kernel, pieces),
        out_shape=tuple(jax.ShapeDtypeStruct((n, P_SIZE), jnp.bfloat16) for n in sizes),
        in_specs=[ANY],
        out_specs=(VMEM,) * len(sizes),
        scratch_shapes=[
            pltpu.VMEM((sum(sizes), P_SIZE), jnp.float32),
            pltpu.SemaphoreType.DMA((sum(len(r) for r in pieces),)),
        ],
    )(front)


def split(value):
    high = value.astype(jnp.bfloat16)
    return high, (value - high.astype(jnp.float32)).astype(jnp.bfloat16)


def dot3(left, right):
    (left_high, left_low), (right_high, right_low) = left, right
    dot = functools.partial(jnp.dot, preferred_element_type=jnp.float32)
    return dot(left_high, right_high) + (dot(left_low, right_high) + dot(left_high, right_low))


def dot2(left, right):
    dot = functools.partial(jnp.dot, preferred_element_type=jnp.float32)
    return dot(left, right[0]) + dot(left, right[1])


def diagonal_inverse(block):
    size = block.shape[0]
    row = lax.broadcasted_iota(jnp.int32, (size, size), 0)
    col = lax.broadcasted_iota(jnp.int32, (size, size), 1)
    on = row == col
    kept = jnp.where(on, block, 0.0)
    down = 1.0 / jnp.sum(kept, axis=1, keepdims=True)
    right = 1.0 / jnp.sum(kept, axis=0, keepdims=True)
    twice = jnp.where(on, 2.0, 0.0)
    parts = split(down * (twice - block * right))
    block_parts = split(block)
    for _ in range(NEWTON - 1):
        parts = split(dot3(parts, split(twice - dot3(block_parts, parts))))
    return parts


def minus_dot(value, left, right):
    return value - jnp.dot(left, right, preferred_element_type=jnp.float32)


def minus_dot(value, left, right):
    return value - jnp.dot(left, right, preferred_element_type=jnp.float32)


def pivot_kernel(counts, width, member_ref, front, *rest):
    firsts, lasts = rest[: counts[0]], rest[counts[0] : sum(counts)]
    out, w_out, raw, mat, own, inv, sems, last_sems, own_sems = rest[sum(counts) :]
    member = member_ref[0]
    p, rows = P_SIZE, TICKS * P_SIZE
    copies = start_first(member, firsts, raw, sems, 0, rows)
    copies += start_halves(member, lasts, raw, last_sems, rows)
    loads = [
        pltpu.make_async_copy(
            front.at[pl.ds(t * width, p), :], own.at[pl.ds(t * p, p), :], own_sems.at[t]
        )
        for t in range(TICKS)
    ]
    for load in loads:
        load.start()
    wait_all(copies)
    x = diagonal_inverse(raw[0, :p, :].astype(jnp.float32))
    wait_all(loads)
    for t in range(TICKS):
        lo, below = t * p, (t + 1) * p
        inv[0, t], inv[1, t] = x
        if below == rows:
            break
        column = mat[t, below:, :] if t else raw[t, below:, :]
        mult = dot3(split(column), x) if t else dot2(column, x)
        panel = mult.astype(jnp.bfloat16)
        for s in range(t + 1, TICKS):
            if t:
                urows = mat[s, lo:below, :].astype(jnp.bfloat16)
                raw[s, lo:below, :] = urows
                rest_rows = mat[s, below:, :]
            else:
                urows = raw[s, lo:below, :]
                rest_rows = raw[s, below:, :].astype(jnp.float32)
            mat[s, below:, :] = minus_dot(rest_rows, panel, urows)
            if s == t + 1:
                x = diagonal_inverse(mat[s, below : below + p, :])
        urows = own[lo:below, :].astype(jnp.bfloat16)
        own[below:, p:] = minus_dot(own[below:, p:], panel, urows[:, p:])
        left = own[below:, :p]
        live = (member >= TICKS) | (member > t)
        changed = jnp.where(live, minus_dot(left, panel, urows[:, :p]), left)
        own[below:, :p] = jnp.where(member == t, mult, changed)

    stores = [
        pltpu.make_async_copy(
            own.at[pl.ds(t * p, p), :], out.at[pl.ds(t * width, p), :], own_sems.at[t]
        )
        for t in range(TICKS)
    ]
    for store in stores:
        store.start()
    row = lax.broadcasted_iota(jnp.int32, (p, width), 0)
    col = lax.broadcasted_iota(jnp.int32, (p, width), 1)
    owner = (member < TICKS) & (col < p)
    for t in reversed(range(TICKS)):
        lo, hi = t * p, (t + 1) * p
        unit = jnp.where((row == col) & (member == t), -1.0, 0.0)
        side = jnp.where(owner, unit, own[lo:hi, :])
        for s in range(t + 1, TICKS):
            side = minus_dot(side, raw[s, lo:hi, :], w_out[s * p : (s + 1) * p, :])
        w_out[lo:hi, :] = dot3((inv[0, t], inv[1, t]), split(side)).astype(jnp.bfloat16)
    wait_all(stores)


def pivot_rows(member, front, bufs):
    order, width = front.shape
    p, rows = P_SIZE, TICKS * P_SIZE
    counts = tuple(len(b) for b in bufs)
    return pl.pallas_call(
        functools.partial(pivot_kernel, counts, width),
        name="pivot_rows",
        out_shape=(
            jax.ShapeDtypeStruct((order, width), jnp.float32),
            jax.ShapeDtypeStruct((rows, width), jnp.bfloat16),
        ),
        in_specs=[SMEM, ANY] + [ANY] * sum(counts),
        out_specs=(ANY, VMEM),
        scratch_shapes=[
            pltpu.VMEM((TICKS, rows, p), jnp.bfloat16),
            pltpu.VMEM((TICKS, rows, p), jnp.float32),
            pltpu.VMEM((rows, width), jnp.float32),
            pltpu.VMEM((2, TICKS, p, p), jnp.bfloat16),
            pltpu.SemaphoreType.DMA((4,)),
            pltpu.SemaphoreType.DMA((2,)),
            pltpu.SemaphoreType.DMA((TICKS,)),
        ],
    )(member, front, *bufs[0], *bufs[1])


def windows(ranges, rows):
    chunks = []
    for lo in range(0, rows, CHUNK):
        n = min(CHUNK, rows - lo)
        pieces = []
        for src, dst, count in ranges:
            first, last = max(lo, dst), min(lo + n, dst + count)
            if first < last:
                pieces.append((src + first - dst, first, last - first))
        chunks.append((lo, n, pieces))
    return chunks


def other_kernel(counts, chunks, tail, member_ref, dest_ref, slot_ref, w, front, out_in, *rest):
    firsts, lasts = rest[: counts[0]], rest[counts[0] : sum(counts)]
    if tail:
        out, outgoing, raw, base, sems, base_sems = rest[sum(counts) :]
    else:
        out, raw, base, sems, base_sems = rest[sum(counts) :]
    member = member_ref[0]
    width = base.shape[1]
    waits = []
    for number, (lo, n, pieces) in enumerate(chunks):
        copies = start_first(member, firsts, raw, sems.at[number], lo, n)
        copies += start_last(member, lasts, raw, sems.at[number, TICKS - 1], lo, n)
        for i, (src, dst, count) in enumerate(pieces):
            copies.append(
                pltpu.make_async_copy(
                    front.at[pl.ds(src, count), :], base.at[pl.ds(dst, count), :], base_sems.at[number, i]
                )
            )
            copies[-1].start()
        waits.append(copies)
    keep = (member >= TICKS) | (lax.broadcasted_iota(jnp.int32, (RB, width), 1) >= P_SIZE)
    stores = []
    for number, (lo, n, pieces) in enumerate(chunks):
        wait_all(waits[number])
        for first in range(lo, lo + n, RB):
            at = pl.ds(first, RB)
            total = jnp.where(keep, base[at, :], 0.0)
            for s in range(TICKS):
                total = minus_dot(total, raw[s, at, :], w[s * P_SIZE : (s + 1) * P_SIZE, :])
            base[at, :] = total
            if tail:
                block = first // RB
                outgoing[dest_ref[block], slot_ref[block]] = jnp.where(keep, total, 0.0).astype(jnp.bfloat16)
        for i, (src, dst, count) in enumerate(pieces):
            stores.append(
                pltpu.make_async_copy(
                    base.at[pl.ds(dst, count), :], out.at[pl.ds(src, count), :], base_sems.at[number, i]
                )
            )
            stores[-1].start()
    wait_all(stores)


def other_rows(member, dest, slot, w, front, out, bufs, ranges, groups=0):
    order, width = front.shape
    rows = sum(n for _, _, n in ranges)
    shapes = [jax.ShapeDtypeStruct((order, width), jnp.float32)]
    specs = [ANY]
    if groups:
        shapes.append(jax.ShapeDtypeStruct((groups, CAP, RB, width), jnp.bfloat16))
        specs.append(VMEM)
    counts = tuple(len(b) for b in bufs)
    chunks = windows(ranges, rows)
    return pl.pallas_call(
        functools.partial(other_kernel, counts, chunks, bool(groups)),
        name="tail_rows" if groups else "middle_rows",
        out_shape=tuple(shapes),
        in_specs=[SMEM, SMEM, SMEM, VMEM, ANY, ANY] + [ANY] * sum(counts),
        out_specs=tuple(specs),
        input_output_aliases={5: 0},
        scratch_shapes=[
            pltpu.VMEM((TICKS, rows, P_SIZE), jnp.bfloat16),
            pltpu.VMEM((rows, width), jnp.float32),
            pltpu.SemaphoreType.DMA((len(chunks), TICKS)),
            pltpu.SemaphoreType.DMA((len(chunks), max(len(c[2]) for c in chunks))),
        ],
    )(member, dest, slot, w, front, out, *bufs[0], *bufs[1])


def routes(parent_group, row_block):
    groups = lax.axis_size("front")
    dest = parent_group.reshape(NB)
    target = row_block.reshape(NB)
    number = jnp.arange(NB)
    earlier = (dest[None, :] == dest[:, None]) & (number[None, :] < number[:, None])
    slot = jnp.sum(earlier.astype(jnp.int32), axis=1)
    pick = (dest[None, None, :] == jnp.arange(groups, dtype=jnp.int32)[:, None, None]) & (
        slot[None, None, :] == jnp.arange(CAP, dtype=jnp.int32)[None, :, None]
    )
    address = jnp.sum(jnp.where(pick, target[None, None, :] + 1, 0), axis=2) - 1
    received = lax.all_to_all(address, "front", split_axis=0, concat_axis=0, tiled=True)
    return dest, slot, received.reshape(groups * CAP)


def add_kernel(address_ref, incoming, base, out):
    out[...] = base[...]
    for i in range(incoming.shape[0]):
        to = address_ref[i]

        @pl.when(to >= 0)
        def _(i=i, to=to):
            at = pl.ds(pl.multiple_of(to * RB, RB), RB)
            out[at, :] = out[at, :] + incoming[i].astype(jnp.float32)


def add_blocks(address, incoming, parent_base):
    groups, cap, rows, width = incoming.shape
    return pl.pallas_call(
        add_kernel,
        name="add_blocks",
        out_shape=jax.ShapeDtypeStruct(parent_base.shape, parent_base.dtype),
        in_specs=[SMEM, VMEM, VMEM],
        out_specs=VMEM,
    )(address, incoming.reshape(groups * cap, rows, width), parent_base)


def local(front, parent_group, row_block, parent_base):
    order, width = front.shape
    member = lax.axis_index("blk")
    holder = member.reshape(1).astype(jnp.int32)
    p, top = P_SIZE, TICKS * width
    tail_n = NB * RB
    tail_at = order - tail_n
    pivot_ranges = [(t * width, p) for t in range(TICKS)]
    tail_ranges = [(tail_at, tail_n)]
    middle_ranges = [(t * width + p, width - p) for t in range(TICKS)]
    if tail_at > top:
        middle_ranges.append((top, tail_at - top))
    middle, at = [], 0
    for start, count in middle_ranges:
        middle.append((start, at, count))
        at += count
    if lax.axis_size("blk") == 8:
        (own_p,) = pack(front, [pivot_ranges])
        *e_halves, own_t, own_m = pack(front, [*cut(pivot_ranges), tail_ranges, middle_ranges])
        sets = relay((own_p, own_t, own_m, e_halves), member)
    else:
        own_p, own_t, own_m = pack(front, [pivot_ranges, tail_ranges, middle_ranges])
        sets = tuple(((lax.all_gather(s, "blk")[:TICKS],),) * 2 for s in (own_p, own_t, own_m))
    dest, slot, address = routes(parent_group, row_block)
    out, w = pivot_rows(holder, front, sets[0])
    out, outgoing = other_rows(
        holder, dest, slot, w, front, out, sets[1], [(tail_at, 0, tail_n)], lax.axis_size("front")
    )
    incoming = lax.all_to_all(outgoing, "front", split_axis=0, concat_axis=0, tiled=True)
    (factored,) = other_rows(holder, dest, slot, w, front, out, sets[2], middle)
    assembled = add_blocks(address, incoming, parent_base)
    return (factored, assembled)


def solution(mesh):
    placed = (
        P("front", "blk"),
        P("front", "blk", None, None),
        P("front", "blk", None),
        P("front", "blk"),
    )
    return jax.shard_map(
        local,
        mesh=mesh,
        in_specs=placed,
        out_specs=(P("front", "blk"), P("front", "blk")),
        check_vma=False,
    )
```

```python
import functools

import jax
import jax.numpy as jnp
from jax import lax
from jax.experimental import pallas as pl
from jax.experimental.pallas import tpu as pltpu
from jax.sharding import PartitionSpec as P


P_SIZE = 256
TICKS = 5
NEWTON = 2
RB = 128
NB = 6
CAP = 2
CHUNK = 256
ANY = pl.BlockSpec(memory_space=pl.ANY)
SMEM = pl.BlockSpec(memory_space=pltpu.SMEM)
VMEM = pl.BlockSpec(memory_space=pltpu.VMEM)


def permute(value, pairs):
    return lax.ppermute(value, "blk", pairs)


def relay(parts, member):
    across = [(m, m ^ 1) for m in range(8)]
    near = [(m, m ^ 2) for m in range(8)]
    distant = [(m, m + 4) for m in range(4)]
    beside, back, mid, up = [(4, 5)], [(4, 0), (5, 1)], [(4, 2), (5, 3)], [(4, 6), (5, 7)]
    level = member // 2
    a, b, c = parts

    def slabs(own):
        cur = jnp.where(member < 4, own, permute(own, distant))
        far = permute(cur, near)
        over = permute(cur, across)
        return cur, far, over, permute(far, across)

    def column(own):
        to_beside = permute(own, beside)
        to_up = permute(own, [(4, 6)])
        to_back = permute(own, [(4, 0)])
        to_mid = permute(own, [(4, 2)])
        cross_up = permute(to_up, [(6, 7)])
        cross_low = permute(jnp.where(level == 0, to_back, to_mid), [(0, 1), (2, 3)])
        return to_back, cross_low, to_mid, cross_low, own, to_beside, to_up, cross_up

    def whole(own):
        own = lax.optimization_barrier(own)
        rows = jnp.where(member == 5, permute(own, beside), own)
        to_up = permute(rows, up)
        to_back = permute(rows, back)
        to_mid = permute(rows, mid)
        return to_back, to_mid, rows, to_up

    return ((slabs(a), column(a)), (slabs(b), whole(b)), (slabs(c), whole(c)))


def placed_slabs(member, refs):
    x = lax.rem(member, 2)
    even = lax.rem(lax.div(member, 2), 2) == 0
    near, far = jnp.where(even, x, 2 + x), jnp.where(even, 2 + x, x)
    over, overfar = jnp.where(even, 1 - x, 3 - x), jnp.where(even, 3 - x, 1 - x)
    return tuple(zip(refs, (near, far, over, overfar)))


def start_first(member, refs, target, sems, lo, n):
    at = pl.ds(lo, n)
    if len(refs) == 1:
        most = pl.ds(0, TICKS - 1)
        copies = [pltpu.make_async_copy(refs[0].at[most, at], target.at[most, at], sems.at[0])]
    else:
        copies = [
            pltpu.make_async_copy(ref.at[at], target.at[slab, at], sems.at[i])
            for i, (ref, slab) in enumerate(placed_slabs(member, refs))
        ]
    for copy in copies:
        copy.start()
    return copies


def start_last(member, refs, target, sem, lo, n):
    at = pl.ds(lo, n)
    if len(refs) == 1:
        copies = [pltpu.make_async_copy(refs[0].at[TICKS - 1, at], target.at[TICKS - 1, at], sem)]
        copies[0].start()
        return copies
    share = 8 // len(refs)
    copies = [pltpu.make_async_copy(ref.at[at], target.at[TICKS - 1, at], sem) for ref in refs]
    for place, copy in enumerate(copies):
        pl.when(lax.div(member, share) == place)(copy.start)
    return copies[:1]


def wait_all(copies):
    for copy in copies:
        copy.wait()


def pack_kernel(pieces, front, *rest):
    outs, (held, sems) = rest[: len(pieces)], rest[len(pieces) :]
    copies, at = [], 0
    for ranges in pieces:
        for start, count in ranges:
            copies.append(
                pltpu.make_async_copy(
                    front.at[pl.ds(start, count), pl.ds(0, P_SIZE)], held.at[pl.ds(at, count), :], sems.at[len(copies)]
                )
            )
            copies[-1].start()
            at += count
    at, number = 0, 0
    for ranges, out in zip(pieces, outs):
        to = 0
        for _, count in ranges:
            copies[number].wait()
            out[pl.ds(to, count), :] = held[pl.ds(at, count), :].astype(jnp.bfloat16)
            at, to, number = at + count, to + count, number + 1


def pack(front, pieces):
    sizes = [sum(n for _, n in ranges) for ranges in pieces]
    return pl.pallas_call(
        functools.partial(pack_kernel, pieces),
        out_shape=tuple(jax.ShapeDtypeStruct((n, P_SIZE), jnp.bfloat16) for n in sizes),
        in_specs=[ANY],
        out_specs=(VMEM,) * len(sizes),
        scratch_shapes=[
            pltpu.VMEM((sum(sizes), P_SIZE), jnp.float32),
            pltpu.SemaphoreType.DMA((sum(len(r) for r in pieces),)),
        ],
    )(front)


def split(value):
    high = value.astype(jnp.bfloat16)
    return high, (value - high.astype(jnp.float32)).astype(jnp.bfloat16)


def dot3(left, right):
    (left_high, left_low), (right_high, right_low) = left, right
    dot = functools.partial(jnp.dot, preferred_element_type=jnp.float32)
    return dot(left_high, right_high) + (dot(left_low, right_high) + dot(left_high, right_low))


def dot2(left, right):
    dot = functools.partial(jnp.dot, preferred_element_type=jnp.float32)
    return dot(left, right[0]) + dot(left, right[1])


def diagonal_inverse(block):
    size = block.shape[0]
    row = lax.broadcasted_iota(jnp.int32, (size, size), 0)
    col = lax.broadcasted_iota(jnp.int32, (size, size), 1)
    on = row == col
    kept = jnp.where(on, block, 0.0)
    down = 1.0 / jnp.sum(kept, axis=1, keepdims=True)
    right = 1.0 / jnp.sum(kept, axis=0, keepdims=True)
    twice = jnp.where(on, 2.0, 0.0)
    parts = split(down * (twice - block * right))
    block_parts = split(block)
    for _ in range(NEWTON - 1):
        parts = split(dot3(parts, split(twice - dot3(block_parts, parts))))
    return parts


def minus_dot(value, left, right):
    return value - jnp.dot(left, right, preferred_element_type=jnp.float32)


def minus_dot(value, left, right):
    return value - jnp.dot(left, right, preferred_element_type=jnp.float32)


def pivot_kernel(counts, width, member_ref, front, *rest):
    firsts, lasts = rest[: counts[0]], rest[counts[0] : sum(counts)]
    out, w_out, raw, mat, own, inv, sems, last_sems, own_sems = rest[sum(counts) :]
    member = member_ref[0]
    p, rows = P_SIZE, TICKS * P_SIZE
    copies = start_first(member, firsts, raw, sems, 0, rows)
    copies += start_last(member, lasts, raw, last_sems.at[0], 0, rows)
    loads = [
        pltpu.make_async_copy(
            front.at[pl.ds(t * width, p), :], own.at[pl.ds(t * p, p), :], own_sems.at[t]
        )
        for t in range(TICKS)
    ]
    for load in loads:
        load.start()
    wait_all(copies)
    x = diagonal_inverse(raw[0, :p, :].astype(jnp.float32))
    wait_all(loads)
    for t in range(TICKS):
        lo, below = t * p, (t + 1) * p
        inv[0, t], inv[1, t] = x
        if below == rows:
            break
        column = mat[t, below:, :] if t else raw[t, below:, :]
        mult = dot3(split(column), x) if t else dot2(column, x)
        panel = mult.astype(jnp.bfloat16)
        for s in range(t + 1, TICKS):
            if t:
                urows = mat[s, lo:below, :].astype(jnp.bfloat16)
                raw[s, lo:below, :] = urows
                rest_rows = mat[s, below:, :]
            else:
                urows = raw[s, lo:below, :]
                rest_rows = raw[s, below:, :].astype(jnp.float32)
            mat[s, below:, :] = minus_dot(rest_rows, panel, urows)
            if s == t + 1:
                x = diagonal_inverse(mat[s, below : below + p, :])
        urows = own[lo:below, :].astype(jnp.bfloat16)
        own[below:, p:] = minus_dot(own[below:, p:], panel, urows[:, p:])
        left = own[below:, :p]
        live = (member >= TICKS) | (member > t)
        changed = jnp.where(live, minus_dot(left, panel, urows[:, :p]), left)
        own[below:, :p] = jnp.where(member == t, mult, changed)

    stores = [
        pltpu.make_async_copy(
            own.at[pl.ds(t * p, p), :], out.at[pl.ds(t * width, p), :], own_sems.at[t]
        )
        for t in range(TICKS)
    ]
    for store in stores:
        store.start()
    row = lax.broadcasted_iota(jnp.int32, (p, width), 0)
    col = lax.broadcasted_iota(jnp.int32, (p, width), 1)
    owner = (member < TICKS) & (col < p)
    for t in reversed(range(TICKS)):
        lo, hi = t * p, (t + 1) * p
        unit = jnp.where((row == col) & (member == t), -1.0, 0.0)
        side = jnp.where(owner, unit, own[lo:hi, :])
        for s in range(t + 1, TICKS):
            side = minus_dot(side, raw[s, lo:hi, :], w_out[s * p : (s + 1) * p, :])
        w_out[lo:hi, :] = dot3((inv[0, t], inv[1, t]), split(side)).astype(jnp.bfloat16)
    wait_all(stores)


def pivot_rows(member, front, bufs):
    order, width = front.shape
    p, rows = P_SIZE, TICKS * P_SIZE
    counts = tuple(len(b) for b in bufs)
    return pl.pallas_call(
        functools.partial(pivot_kernel, counts, width),
        name="pivot_rows",
        out_shape=(
            jax.ShapeDtypeStruct((order, width), jnp.float32),
            jax.ShapeDtypeStruct((rows, width), jnp.bfloat16),
        ),
        in_specs=[SMEM, ANY] + [ANY] * sum(counts),
        out_specs=(ANY, VMEM),
        scratch_shapes=[
            pltpu.VMEM((TICKS, rows, p), jnp.bfloat16),
            pltpu.VMEM((TICKS, rows, p), jnp.float32),
            pltpu.VMEM((rows, width), jnp.float32),
            pltpu.VMEM((2, TICKS, p, p), jnp.bfloat16),
            pltpu.SemaphoreType.DMA((4,)),
            pltpu.SemaphoreType.DMA((1,)),
            pltpu.SemaphoreType.DMA((TICKS,)),
        ],
    )(member, front, *bufs[0], *bufs[1])


def windows(ranges, rows):
    chunks = []
    for lo in range(0, rows, CHUNK):
        n = min(CHUNK, rows - lo)
        pieces = []
        for src, dst, count in ranges:
            first, last = max(lo, dst), min(lo + n, dst + count)
            if first < last:
                pieces.append((src + first - dst, first, last - first))
        chunks.append((lo, n, pieces))
    return chunks


def other_kernel(counts, chunks, tail, member_ref, dest_ref, slot_ref, w, front, out_in, *rest):
    firsts, lasts = rest[: counts[0]], rest[counts[0] : sum(counts)]
    if tail:
        out, outgoing, raw, base, sems, base_sems = rest[sum(counts) :]
    else:
        out, raw, base, sems, base_sems = rest[sum(counts) :]
    member = member_ref[0]
    width = base.shape[1]
    waits = []
    for number, (lo, n, pieces) in enumerate(chunks):
        copies = start_first(member, firsts, raw, sems.at[number], lo, n)
        copies += start_last(member, lasts, raw, sems.at[number, TICKS - 1], lo, n)
        for i, (src, dst, count) in enumerate(pieces):
            copies.append(
                pltpu.make_async_copy(
                    front.at[pl.ds(src, count), :], base.at[pl.ds(dst, count), :], base_sems.at[number, i]
                )
            )
            copies[-1].start()
        waits.append(copies)
    keep = (member >= TICKS) | (lax.broadcasted_iota(jnp.int32, (CHUNK, width), 1) >= P_SIZE)
    stores = []
    for number, (lo, n, pieces) in enumerate(chunks):
        wait_all(waits[number])
        at = pl.ds(lo, n)
        total = jnp.where(keep[:n], base[at, :], 0.0)
        for s in range(TICKS):
            total = minus_dot(total, raw[s, at, :], w[s * P_SIZE : (s + 1) * P_SIZE, :])
        base[at, :] = total
        if tail:
            cont = jnp.where(keep[:n], total, 0.0).astype(jnp.bfloat16)
            for first in range(0, n, RB):
                block = (lo + first) // RB
                outgoing[dest_ref[block], slot_ref[block]] = cont[first : first + RB]
        for i, (src, dst, count) in enumerate(pieces):
            stores.append(
                pltpu.make_async_copy(
                    base.at[pl.ds(dst, count), :], out.at[pl.ds(src, count), :], base_sems.at[number, i]
                )
            )
            stores[-1].start()
    wait_all(stores)


def other_rows(member, dest, slot, w, front, out, bufs, ranges, groups=0):
    order, width = front.shape
    rows = sum(n for _, _, n in ranges)
    shapes = [jax.ShapeDtypeStruct((order, width), jnp.float32)]
    specs = [ANY]
    if groups:
        shapes.append(jax.ShapeDtypeStruct((groups, CAP, RB, width), jnp.bfloat16))
        specs.append(VMEM)
    counts = tuple(len(b) for b in bufs)
    chunks = windows(ranges, rows)
    return pl.pallas_call(
        functools.partial(other_kernel, counts, chunks, bool(groups)),
        name="tail_rows" if groups else "middle_rows",
        out_shape=tuple(shapes),
        in_specs=[SMEM, SMEM, SMEM, VMEM, ANY, ANY] + [ANY] * sum(counts),
        out_specs=tuple(specs),
        input_output_aliases={5: 0},
        scratch_shapes=[
            pltpu.VMEM((TICKS, rows, P_SIZE), jnp.bfloat16),
            pltpu.VMEM((rows, width), jnp.float32),
            pltpu.SemaphoreType.DMA((len(chunks), TICKS)),
            pltpu.SemaphoreType.DMA((len(chunks), max(len(c[2]) for c in chunks))),
        ],
    )(member, dest, slot, w, front, out, *bufs[0], *bufs[1])


def routes(parent_group, row_block):
    groups = lax.axis_size("front")
    dest = parent_group.reshape(NB)
    target = row_block.reshape(NB)
    number = jnp.arange(NB)
    earlier = (dest[None, :] == dest[:, None]) & (number[None, :] < number[:, None])
    slot = jnp.sum(earlier.astype(jnp.int32), axis=1)
    pick = (dest[None, None, :] == jnp.arange(groups, dtype=jnp.int32)[:, None, None]) & (
        slot[None, None, :] == jnp.arange(CAP, dtype=jnp.int32)[None, :, None]
    )
    address = jnp.sum(jnp.where(pick, target[None, None, :] + 1, 0), axis=2) - 1
    received = lax.all_to_all(address, "front", split_axis=0, concat_axis=0, tiled=True)
    return dest, slot, received.reshape(groups * CAP)


def add_kernel(address_ref, incoming, base, out):
    out[...] = base[...]
    for i in range(incoming.shape[0]):
        to = address_ref[i]

        @pl.when(to >= 0)
        def _(i=i, to=to):
            at = pl.ds(pl.multiple_of(to * RB, RB), RB)
            out[at, :] = out[at, :] + incoming[i].astype(jnp.float32)


def add_blocks(address, incoming, parent_base):
    groups, cap, rows, width = incoming.shape
    return pl.pallas_call(
        add_kernel,
        name="add_blocks",
        out_shape=jax.ShapeDtypeStruct(parent_base.shape, parent_base.dtype),
        in_specs=[SMEM, VMEM, VMEM],
        out_specs=VMEM,
    )(address, incoming.reshape(groups * cap, rows, width), parent_base)


def local(front, parent_group, row_block, parent_base):
    order, width = front.shape
    member = lax.axis_index("blk")
    holder = member.reshape(1).astype(jnp.int32)
    p, top = P_SIZE, TICKS * width
    tail_n = NB * RB
    tail_at = order - tail_n
    pivot_ranges = [(t * width, p) for t in range(TICKS)]
    tail_ranges = [(tail_at, tail_n)]
    middle_ranges = [(t * width + p, width - p) for t in range(TICKS)]
    if tail_at > top:
        middle_ranges.append((top, tail_at - top))
    middle, at = [], 0
    for start, count in middle_ranges:
        middle.append((start, at, count))
        at += count
    if lax.axis_size("blk") == 8:
        (own_p,) = pack(front, [pivot_ranges])
        own_t, own_m = pack(front, [tail_ranges, middle_ranges])
        sets = relay((own_p, own_t, own_m), member)
    else:
        own_p, own_t, own_m = pack(front, [pivot_ranges, tail_ranges, middle_ranges])
        sets = tuple(((lax.all_gather(s, "blk")[:TICKS],),) * 2 for s in (own_p, own_t, own_m))
    dest, slot, address = routes(parent_group, row_block)
    out, w = pivot_rows(holder, front, sets[0])
    out, outgoing = other_rows(
        holder, dest, slot, w, front, out, sets[1], [(tail_at, 0, tail_n)], lax.axis_size("front")
    )
    incoming = lax.all_to_all(outgoing, "front", split_axis=0, concat_axis=0, tiled=True)
    (factored,) = other_rows(holder, dest, slot, w, front, out, sets[2], middle)
    assembled = add_blocks(address, incoming, parent_base)
    return (factored, assembled)


def solution(mesh):
    placed = (
        P("front", "blk"),
        P("front", "blk", None, None),
        P("front", "blk", None),
        P("front", "blk"),
    )
    return jax.shard_map(
        local,
        mesh=mesh,
        in_specs=placed,
        out_specs=(P("front", "blk"), P("front", "blk")),
        check_vma=False,
    )
```

```python
import functools

import jax
import jax.numpy as jnp
from jax import lax
from jax.experimental import pallas as pl
from jax.experimental.pallas import tpu as pltpu
from jax.sharding import PartitionSpec as P


P_SIZE = 256
TICKS = 5
NEWTON = 2
RB = 128
NB = 6
CAP = 2
CHUNK = 256
ANY = pl.BlockSpec(memory_space=pl.ANY)
SMEM = pl.BlockSpec(memory_space=pltpu.SMEM)
VMEM = pl.BlockSpec(memory_space=pltpu.VMEM)


def permute(value, pairs):
    return lax.ppermute(value, "blk", pairs)


def relay(parts, member):
    across = [(m, m ^ 1) for m in range(8)]
    near = [(m, m ^ 2) for m in range(8)]
    distant = [(m, m + 4) for m in range(4)]
    beside, back, mid, up = [(4, 5)], [(4, 0), (5, 1)], [(4, 2), (5, 3)], [(4, 6), (5, 7)]
    level = member // 2
    a, b, c, e_halves = parts

    def slabs(own):
        cur = jnp.where(member < 4, own, permute(own, distant))
        far = permute(cur, near)
        over = permute(cur, across)
        return cur, far, over, permute(far, across)

    def halves(low, high):
        half = jnp.where(member == 5, permute(high, beside), low)
        to_up = permute(half, up)
        to_back = permute(half, back)
        to_mid = permute(half, mid)
        half = jnp.where(level == 2, half, jnp.where(level == 3, to_up, jnp.where(level == 0, to_back, to_mid)))
        return half, permute(half, across)

    def whole(own):
        own = lax.optimization_barrier(own)
        rows = jnp.where(member == 5, permute(own, beside), own)
        to_up = permute(rows, up)
        to_back = permute(rows, back)
        to_mid = permute(rows, mid)
        return to_back, to_mid, rows, to_up

    return ((slabs(a), halves(*e_halves)), (slabs(b), whole(b)), (slabs(c), whole(c)))


def placed_slabs(member, refs):
    x = lax.rem(member, 2)
    even = lax.rem(lax.div(member, 2), 2) == 0
    near, far = jnp.where(even, x, 2 + x), jnp.where(even, 2 + x, x)
    over, overfar = jnp.where(even, 1 - x, 3 - x), jnp.where(even, 3 - x, 1 - x)
    return tuple(zip(refs, (near, far, over, overfar)))


def start_first(member, refs, target, sems, lo, n):
    at = pl.ds(lo, n)
    if len(refs) == 1:
        most = pl.ds(0, TICKS - 1)
        copies = [pltpu.make_async_copy(refs[0].at[most, at], target.at[most, at], sems.at[0])]
    else:
        copies = [
            pltpu.make_async_copy(ref.at[at], target.at[slab, at], sems.at[i])
            for i, (ref, slab) in enumerate(placed_slabs(member, refs))
        ]
    for copy in copies:
        copy.start()
    return copies


def start_last(member, refs, target, sem, lo, n):
    at = pl.ds(lo, n)
    if len(refs) == 1:
        copies = [pltpu.make_async_copy(refs[0].at[TICKS - 1, at], target.at[TICKS - 1, at], sem)]
        copies[0].start()
        return copies
    copies = [pltpu.make_async_copy(ref.at[at], target.at[TICKS - 1, at], sem) for ref in refs]
    for level, copy in enumerate(copies):
        pl.when(lax.div(member, 2) == level)(copy.start)
    return copies[:1]


def start_halves(member, refs, target, sems, rows):
    if len(refs) == 1:
        return start_last(member, refs, target, sems.at[0], 0, rows)
    half, overhalf = refs
    x, n = lax.rem(member, 2), rows // 2

    def copy(ref, number):
        return pltpu.make_async_copy(ref, target.at[TICKS - 1, pl.ds(number * n, n)], sems.at[number])

    for which in (0, 1):

        @pl.when(x == which)
        def _(which=which):
            copy(half, which).start()
            copy(overhalf, 1 - which).start()

    return [copy(half, 0), copy(half, 1)]


def wait_all(copies):
    for copy in copies:
        copy.wait()


def pack_kernel(pieces, front, *rest):
    outs, (held, sems) = rest[: len(pieces)], rest[len(pieces) :]
    copies, at = [], 0
    for ranges in pieces:
        for start, count in ranges:
            copies.append(
                pltpu.make_async_copy(
                    front.at[pl.ds(start, count), pl.ds(0, P_SIZE)], held.at[pl.ds(at, count), :], sems.at[len(copies)]
                )
            )
            copies[-1].start()
            at += count
    at, number = 0, 0
    for ranges, out in zip(pieces, outs):
        to = 0
        for _, count in ranges:
            copies[number].wait()
            out[pl.ds(to, count), :] = held[pl.ds(at, count), :].astype(jnp.bfloat16)
            at, to, number = at + count, to + count, number + 1


def pack(front, pieces):
    sizes = [sum(n for _, n in ranges) for ranges in pieces]
    return pl.pallas_call(
        functools.partial(pack_kernel, pieces),
        out_shape=tuple(jax.ShapeDtypeStruct((n, P_SIZE), jnp.bfloat16) for n in sizes),
        in_specs=[ANY],
        out_specs=(VMEM,) * len(sizes),
        scratch_shapes=[
            pltpu.VMEM((sum(sizes), P_SIZE), jnp.float32),
            pltpu.SemaphoreType.DMA((sum(len(r) for r in pieces),)),
        ],
    )(front)


def split(value):
    high = value.astype(jnp.bfloat16)
    return high, (value - high.astype(jnp.float32)).astype(jnp.bfloat16)


def dot3(left, right):
    (left_high, left_low), (right_high, right_low) = left, right
    dot = functools.partial(jnp.dot, preferred_element_type=jnp.float32)
    return dot(left_high, right_high) + (dot(left_low, right_high) + dot(left_high, right_low))


def dot2(left, right):
    dot = functools.partial(jnp.dot, preferred_element_type=jnp.float32)
    return dot(left, right[0]) + dot(left, right[1])


def diagonal_inverse(block):
    size = block.shape[0]
    row = lax.broadcasted_iota(jnp.int32, (size, size), 0)
    col = lax.broadcasted_iota(jnp.int32, (size, size), 1)
    on = row == col
    kept = jnp.where(on, block, 0.0)
    down = 1.0 / jnp.sum(kept, axis=1, keepdims=True)
    right = 1.0 / jnp.sum(kept, axis=0, keepdims=True)
    twice = jnp.where(on, 2.0, 0.0)
    parts = split(down * (twice - block * right))
    block_parts = split(block)
    for _ in range(NEWTON - 1):
        parts = split(dot3(parts, split(twice - dot3(block_parts, parts))))
    return parts


def minus_dot(value, left, right):
    return value - jnp.dot(left, right, preferred_element_type=jnp.float32)


def minus_dot(value, left, right):
    return value - jnp.dot(left, right, preferred_element_type=jnp.float32)


def pivot_kernel(counts, width, member_ref, front, *rest):
    firsts, lasts = rest[: counts[0]], rest[counts[0] : sum(counts)]
    out, w_out, raw, mat, own, inv, sems, last_sems, own_sems = rest[sum(counts) :]
    member = member_ref[0]
    p, rows = P_SIZE, TICKS * P_SIZE
    copies = start_first(member, firsts, raw, sems, 0, rows)
    copies += start_halves(member, lasts, raw, last_sems, rows)
    loads = [
        pltpu.make_async_copy(
            front.at[pl.ds(t * width, p), :], own.at[pl.ds(t * p, p), :], own_sems.at[t]
        )
        for t in range(TICKS)
    ]
    for load in loads:
        load.start()
    wait_all(copies)
    x = diagonal_inverse(raw[0, :p, :].astype(jnp.float32))
    wait_all(loads)
    for t in range(TICKS):
        lo, below = t * p, (t + 1) * p
        inv[0, t], inv[1, t] = x
        if below == rows:
            break
        column = mat[t, below:, :] if t else raw[t, below:, :]
        mult = dot3(split(column), x) if t else dot2(column, x)
        panel = mult.astype(jnp.bfloat16)
        for s in range(t + 1, TICKS):
            if t:
                urows = mat[s, lo:below, :].astype(jnp.bfloat16)
                raw[s, lo:below, :] = urows
                rest_rows = mat[s, below:, :]
            else:
                urows = raw[s, lo:below, :]
                rest_rows = raw[s, below:, :].astype(jnp.float32)
            mat[s, below:, :] = minus_dot(rest_rows, panel, urows)
            if s == t + 1:
                x = diagonal_inverse(mat[s, below : below + p, :])
        urows = own[lo:below, :].astype(jnp.bfloat16)
        own[below:, p:] = minus_dot(own[below:, p:], panel, urows[:, p:])
        left = own[below:, :p]
        live = (member >= TICKS) | (member > t)
        changed = jnp.where(live, minus_dot(left, panel, urows[:, :p]), left)
        own[below:, :p] = jnp.where(member == t, mult, changed)

    stores = [
        pltpu.make_async_copy(
            own.at[pl.ds(t * p, p), :], out.at[pl.ds(t * width, p), :], own_sems.at[t]
        )
        for t in range(TICKS)
    ]
    for store in stores:
        store.start()
    row = lax.broadcasted_iota(jnp.int32, (p, width), 0)
    col = lax.broadcasted_iota(jnp.int32, (p, width), 1)
    owner = (member < TICKS) & (col < p)
    for t in reversed(range(TICKS)):
        lo, hi = t * p, (t + 1) * p
        unit = jnp.where((row == col) & (member == t), -1.0, 0.0)
        side = jnp.where(owner, unit, own[lo:hi, :])
        for s in range(t + 1, TICKS):
            side = minus_dot(side, raw[s, lo:hi, :], w_out[s * p : (s + 1) * p, :])
        w_out[lo:hi, :] = dot3((inv[0, t], inv[1, t]), split(side)).astype(jnp.bfloat16)
    wait_all(stores)


def pivot_rows(member, front, bufs):
    order, width = front.shape
    p, rows = P_SIZE, TICKS * P_SIZE
    counts = tuple(len(b) for b in bufs)
    return pl.pallas_call(
        functools.partial(pivot_kernel, counts, width),
        name="pivot_rows",
        out_shape=(
            jax.ShapeDtypeStruct((order, width), jnp.float32),
            jax.ShapeDtypeStruct((rows, width), jnp.bfloat16),
        ),
        in_specs=[SMEM, ANY] + [ANY] * sum(counts),
        out_specs=(ANY, VMEM),
        scratch_shapes=[
            pltpu.VMEM((TICKS, rows, p), jnp.bfloat16),
            pltpu.VMEM((TICKS, rows, p), jnp.float32),
            pltpu.VMEM((rows, width), jnp.float32),
            pltpu.VMEM((2, TICKS, p, p), jnp.bfloat16),
            pltpu.SemaphoreType.DMA((4,)),
            pltpu.SemaphoreType.DMA((2,)),
            pltpu.SemaphoreType.DMA((TICKS,)),
        ],
    )(member, front, *bufs[0], *bufs[1])


def windows(ranges, rows):
    chunks = []
    for lo in range(0, rows, CHUNK):
        n = min(CHUNK, rows - lo)
        pieces = []
        for src, dst, count in ranges:
            first, last = max(lo, dst), min(lo + n, dst + count)
            if first < last:
                pieces.append((src + first - dst, first, last - first))
        chunks.append((lo, n, pieces))
    return chunks


def other_kernel(counts, chunks, tail, member_ref, dest_ref, slot_ref, w, front, out_in, *rest):
    firsts, lasts = rest[: counts[0]], rest[counts[0] : sum(counts)]
    if tail:
        out, outgoing, raw, base, sems, base_sems = rest[sum(counts) :]
    else:
        out, raw, base, sems, base_sems = rest[sum(counts) :]
    member = member_ref[0]
    width = base.shape[1]
    waits = []
    for number, (lo, n, pieces) in enumerate(chunks):
        copies = start_first(member, firsts, raw, sems.at[number], lo, n)
        copies += start_last(member, lasts, raw, sems.at[number, TICKS - 1], lo, n)
        for i, (src, dst, count) in enumerate(pieces):
            copies.append(
                pltpu.make_async_copy(
                    front.at[pl.ds(src, count), :], base.at[pl.ds(dst, count), :], base_sems.at[number, i]
                )
            )
            copies[-1].start()
        waits.append(copies)
    keep = (member >= TICKS) | (lax.broadcasted_iota(jnp.int32, (CHUNK, width), 1) >= P_SIZE)
    stores = []
    for number, (lo, n, pieces) in enumerate(chunks):
        wait_all(waits[number])
        at = pl.ds(lo, n)
        total = jnp.where(keep[:n], base[at, :], 0.0)
        for s in range(TICKS):
            total = minus_dot(total, raw[s, at, :], w[s * P_SIZE : (s + 1) * P_SIZE, :])
        base[at, :] = total
        if tail:
            cont = jnp.where(keep[:n], total, 0.0).astype(jnp.bfloat16)
            for first in range(0, n, RB):
                block = (lo + first) // RB
                outgoing[dest_ref[block], slot_ref[block]] = cont[first : first + RB]
        for i, (src, dst, count) in enumerate(pieces):
            stores.append(
                pltpu.make_async_copy(
                    base.at[pl.ds(dst, count), :], out.at[pl.ds(src, count), :], base_sems.at[number, i]
                )
            )
            stores[-1].start()
    wait_all(stores)


def other_rows(member, dest, slot, w, front, out, bufs, ranges, groups=0):
    order, width = front.shape
    rows = sum(n for _, _, n in ranges)
    shapes = [jax.ShapeDtypeStruct((order, width), jnp.float32)]
    specs = [ANY]
    if groups:
        shapes.append(jax.ShapeDtypeStruct((groups, CAP, RB, width), jnp.bfloat16))
        specs.append(VMEM)
    counts = tuple(len(b) for b in bufs)
    chunks = windows(ranges, rows)
    return pl.pallas_call(
        functools.partial(other_kernel, counts, chunks, bool(groups)),
        name="tail_rows" if groups else "middle_rows",
        out_shape=tuple(shapes),
        in_specs=[SMEM, SMEM, SMEM, VMEM, ANY, ANY] + [ANY] * sum(counts),
        out_specs=tuple(specs),
        input_output_aliases={5: 0},
        scratch_shapes=[
            pltpu.VMEM((TICKS, rows, P_SIZE), jnp.bfloat16),
            pltpu.VMEM((rows, width), jnp.float32),
            pltpu.SemaphoreType.DMA((len(chunks), TICKS)),
            pltpu.SemaphoreType.DMA((len(chunks), max(len(c[2]) for c in chunks))),
        ],
    )(member, dest, slot, w, front, out, *bufs[0], *bufs[1])


def routes(parent_group, row_block):
    groups = lax.axis_size("front")
    dest = parent_group.reshape(NB)
    target = row_block.reshape(NB)
    number = jnp.arange(NB)
    earlier = (dest[None, :] == dest[:, None]) & (number[None, :] < number[:, None])
    slot = jnp.sum(earlier.astype(jnp.int32), axis=1)
    pick = (dest[None, None, :] == jnp.arange(groups, dtype=jnp.int32)[:, None, None]) & (
        slot[None, None, :] == jnp.arange(CAP, dtype=jnp.int32)[None, :, None]
    )
    address = jnp.sum(jnp.where(pick, target[None, None, :] + 1, 0), axis=2) - 1
    received = lax.all_to_all(address, "front", split_axis=0, concat_axis=0, tiled=True)
    return dest, slot, received.reshape(groups * CAP)


def add_kernel(address_ref, incoming, base, out):
    out[...] = base[...]
    for i in range(incoming.shape[0]):
        to = address_ref[i]

        @pl.when(to >= 0)
        def _(i=i, to=to):
            at = pl.ds(pl.multiple_of(to * RB, RB), RB)
            out[at, :] = out[at, :] + incoming[i].astype(jnp.float32)


def add_blocks(address, incoming, parent_base):
    groups, cap, rows, width = incoming.shape
    return pl.pallas_call(
        add_kernel,
        name="add_blocks",
        out_shape=jax.ShapeDtypeStruct(parent_base.shape, parent_base.dtype),
        in_specs=[SMEM, VMEM, VMEM],
        out_specs=VMEM,
    )(address, incoming.reshape(groups * cap, rows, width), parent_base)


def local(front, parent_group, row_block, parent_base):
    order, width = front.shape
    member = lax.axis_index("blk")
    holder = member.reshape(1).astype(jnp.int32)
    p, top = P_SIZE, TICKS * width
    tail_n = NB * RB
    tail_at = order - tail_n
    pivot_ranges = [(t * width, p) for t in range(TICKS)]
    tail_ranges = [(tail_at, tail_n)]
    middle_ranges = [(t * width + p, width - p) for t in range(TICKS)]
    if tail_at > top:
        middle_ranges.append((top, tail_at - top))
    middle, at = [], 0
    for start, count in middle_ranges:
        middle.append((start, at, count))
        at += count
    if lax.axis_size("blk") == 8:
        (own_p,) = pack(front, [pivot_ranges])
        own_t, own_m = pack(front, [tail_ranges, middle_ranges])
        half = own_p.shape[0] // 2
        sets = relay((own_p, own_t, own_m, (own_p[:half], own_p[half:])), member)
    else:
        own_p, own_t, own_m = pack(front, [pivot_ranges, tail_ranges, middle_ranges])
        sets = tuple(((lax.all_gather(s, "blk")[:TICKS],),) * 2 for s in (own_p, own_t, own_m))
    dest, slot, address = routes(parent_group, row_block)
    out, w = pivot_rows(holder, front, sets[0])
    out, outgoing = other_rows(
        holder, dest, slot, w, front, out, sets[1], [(tail_at, 0, tail_n)], lax.axis_size("front")
    )
    incoming = lax.all_to_all(outgoing, "front", split_axis=0, concat_axis=0, tiled=True)
    (factored,) = other_rows(holder, dest, slot, w, front, out, sets[2], middle)
    assembled = add_blocks(address, incoming, parent_base)
    return (factored, assembled)


def solution(mesh):
    placed = (
        P("front", "blk"),
        P("front", "blk", None, None),
        P("front", "blk", None),
        P("front", "blk"),
    )
    return jax.shard_map(
        local,
        mesh=mesh,
        in_specs=placed,
        out_specs=(P("front", "blk"), P("front", "blk")),
        check_vma=False,
    )
```

```python
import functools

import jax
import jax.numpy as jnp
from jax import lax
from jax.experimental import pallas as pl
from jax.experimental.pallas import tpu as pltpu
from jax.sharding import PartitionSpec as P


P_SIZE = 256
TICKS = 5
NEWTON = 2
RB = 128
NB = 6
CAP = 2
CHUNK = 256
ANY = pl.BlockSpec(memory_space=pl.ANY)
SMEM = pl.BlockSpec(memory_space=pltpu.SMEM)
VMEM = pl.BlockSpec(memory_space=pltpu.VMEM)


def permute(value, pairs):
    return lax.ppermute(value, "blk", pairs)


def relay(parts, member):
    across = [(m, m ^ 1) for m in range(8)]
    near = [(m, m ^ 2) for m in range(8)]
    distant = [(m, m + 4) for m in range(4)]
    beside, back, mid, up = [(4, 5)], [(4, 0), (5, 1)], [(4, 2), (5, 3)], [(4, 6), (5, 7)]
    level = member // 2
    a, b, c, e_halves = parts

    def slabs(own):
        cur = jnp.where(member < 4, own, permute(own, distant))
        far = permute(cur, near)
        over = permute(cur, across)
        return cur, far, over, permute(far, across)

    def halves(low, high):
        half = jnp.where(member == 5, permute(high, beside), low)
        to_up = permute(half, up)
        to_back = permute(half, back)
        to_mid = permute(half, mid)
        half = jnp.where(level == 2, half, jnp.where(level == 3, to_up, jnp.where(level == 0, to_back, to_mid)))
        return half, permute(half, across)

    def whole(own):
        own = lax.optimization_barrier(own)
        rows = jnp.where(member == 5, permute(own, beside), own)
        to_up = permute(rows, up)
        to_back = permute(rows, back)
        to_mid = permute(rows, mid)
        return to_back, to_mid, rows, to_up

    return ((slabs(a), halves(*e_halves)), (slabs(b), whole(b)), (slabs(c), whole(c)))


def places(member):
    x = lax.rem(member, 2)
    even = lax.rem(lax.div(member, 2), 2) == 0
    near, far = jnp.where(even, x, 2 + x), jnp.where(even, 2 + x, x)
    over, overfar = jnp.where(even, 1 - x, 3 - x), jnp.where(even, 3 - x, 1 - x)
    return near, far, over, overfar


def placed_slabs(member, refs):
    return tuple(zip(refs, places(member)))


def start_first(member, refs, target, sems, lo, n):
    at = pl.ds(lo, n)
    if len(refs) == 1:
        most = pl.ds(0, TICKS - 1)
        copies = [pltpu.make_async_copy(refs[0].at[most, at], target.at[most, at], sems.at[0])]
    else:
        copies = [
            pltpu.make_async_copy(ref.at[at], target.at[slab, at], sems.at[i])
            for i, (ref, slab) in enumerate(placed_slabs(member, refs))
        ]
    for copy in copies:
        copy.start()
    return copies


def start_last(member, refs, target, sem, lo, n):
    at = pl.ds(lo, n)
    if len(refs) == 1:
        copies = [pltpu.make_async_copy(refs[0].at[TICKS - 1, at], target.at[TICKS - 1, at], sem)]
        copies[0].start()
        return copies
    copies = [pltpu.make_async_copy(ref.at[at], target.at[TICKS - 1, at], sem) for ref in refs]
    for level, copy in enumerate(copies):
        pl.when(lax.div(member, 2) == level)(copy.start)
    return copies[:1]


def start_halves(member, refs, target, sems, rows):
    if len(refs) == 1:
        return start_last(member, refs, target, sems.at[0], 0, rows)
    half, overhalf = refs
    x, n = lax.rem(member, 2), rows // 2

    def copy(ref, number):
        return pltpu.make_async_copy(ref, target.at[TICKS - 1, pl.ds(number * n, n)], sems.at[number])

    for which in (0, 1):

        @pl.when(x == which)
        def _(which=which):
            copy(half, which).start()
            copy(overhalf, 1 - which).start()

    return [copy(half, 0), copy(half, 1)]


def wait_all(copies):
    for copy in copies:
        copy.wait()


def pack_kernel(pieces, front, *rest):
    outs, (held, sems) = rest[: len(pieces)], rest[len(pieces) :]
    copies, at = [], 0
    for ranges in pieces:
        for start, count in ranges:
            copies.append(
                pltpu.make_async_copy(
                    front.at[pl.ds(start, count), pl.ds(0, P_SIZE)], held.at[pl.ds(at, count), :], sems.at[len(copies)]
                )
            )
            copies[-1].start()
            at += count
    at, number = 0, 0
    for ranges, out in zip(pieces, outs):
        to = 0
        for _, count in ranges:
            copies[number].wait()
            out[pl.ds(to, count), :] = held[pl.ds(at, count), :].astype(jnp.bfloat16)
            at, to, number = at + count, to + count, number + 1


def pack(front, pieces):
    sizes = [sum(n for _, n in ranges) for ranges in pieces]
    return pl.pallas_call(
        functools.partial(pack_kernel, pieces),
        out_shape=tuple(jax.ShapeDtypeStruct((n, P_SIZE), jnp.bfloat16) for n in sizes),
        in_specs=[ANY],
        out_specs=(VMEM,) * len(sizes),
        scratch_shapes=[
            pltpu.VMEM((sum(sizes), P_SIZE), jnp.float32),
            pltpu.SemaphoreType.DMA((sum(len(r) for r in pieces),)),
        ],
    )(front)


def split(value):
    high = value.astype(jnp.bfloat16)
    return high, (value - high.astype(jnp.float32)).astype(jnp.bfloat16)


def dot3(left, right):
    (left_high, left_low), (right_high, right_low) = left, right
    dot = functools.partial(jnp.dot, preferred_element_type=jnp.float32)
    return dot(left_high, right_high) + (dot(left_low, right_high) + dot(left_high, right_low))


def dot2(left, right):
    dot = functools.partial(jnp.dot, preferred_element_type=jnp.float32)
    return dot(left, right[0]) + dot(left, right[1])


def diagonal_inverse(block):
    size = block.shape[0]
    row = lax.broadcasted_iota(jnp.int32, (size, size), 0)
    col = lax.broadcasted_iota(jnp.int32, (size, size), 1)
    on = row == col
    kept = jnp.where(on, block, 0.0)
    down = 1.0 / jnp.sum(kept, axis=1, keepdims=True)
    right = 1.0 / jnp.sum(kept, axis=0, keepdims=True)
    twice = jnp.where(on, 2.0, 0.0)
    parts = split(down * (twice - block * right))
    block_parts = split(block)
    for _ in range(NEWTON - 1):
        parts = split(dot3(parts, split(twice - dot3(block_parts, parts))))
    return parts


def minus_dot(value, left, right):
    return value - jnp.dot(left, right, preferred_element_type=jnp.float32)


def minus_dot(value, left, right):
    return value - jnp.dot(left, right, preferred_element_type=jnp.float32)


def pivot_kernel(counts, width, member_ref, front, *rest):
    firsts, lasts = rest[: counts[0]], rest[counts[0] : sum(counts)]
    out, w_out, raw, mat, own, inv, sems, last_sems, own_sems = rest[sum(counts) :]
    member = member_ref[0]
    p, rows = P_SIZE, TICKS * P_SIZE
    copies = start_first(member, firsts, raw, sems, 0, rows)
    copies += start_halves(member, lasts, raw, last_sems, rows)
    loads = [
        pltpu.make_async_copy(
            front.at[pl.ds(t * width, p), :], own.at[pl.ds(t * p, p), :], own_sems.at[t]
        )
        for t in range(TICKS)
    ]
    for load in loads:
        load.start()
    wait_all(copies)
    x = diagonal_inverse(raw[0, :p, :].astype(jnp.float32))
    wait_all(loads)
    for t in range(TICKS):
        lo, below = t * p, (t + 1) * p
        inv[0, t], inv[1, t] = x
        if below == rows:
            break
        column = mat[t, below:, :] if t else raw[t, below:, :]
        mult = dot3(split(column), x) if t else dot2(column, x)
        panel = mult.astype(jnp.bfloat16)
        for s in range(t + 1, TICKS):
            if t:
                urows = mat[s, lo:below, :].astype(jnp.bfloat16)
                raw[s, lo:below, :] = urows
                rest_rows = mat[s, below:, :]
            else:
                urows = raw[s, lo:below, :]
                rest_rows = raw[s, below:, :].astype(jnp.float32)
            mat[s, below:, :] = minus_dot(rest_rows, panel, urows)
            if s == t + 1:
                x = diagonal_inverse(mat[s, below : below + p, :])
        urows = own[lo:below, :].astype(jnp.bfloat16)
        own[below:, p:] = minus_dot(own[below:, p:], panel, urows[:, p:])
        left = own[below:, :p]
        live = (member >= TICKS) | (member > t)
        changed = jnp.where(live, minus_dot(left, panel, urows[:, :p]), left)
        own[below:, :p] = jnp.where(member == t, mult, changed)

    stores = [
        pltpu.make_async_copy(
            own.at[pl.ds(t * p, p), :], out.at[pl.ds(t * width, p), :], own_sems.at[t]
        )
        for t in range(TICKS)
    ]
    for store in stores:
        store.start()
    row = lax.broadcasted_iota(jnp.int32, (p, width), 0)
    col = lax.broadcasted_iota(jnp.int32, (p, width), 1)
    owner = (member < TICKS) & (col < p)
    for t in reversed(range(TICKS)):
        lo, hi = t * p, (t + 1) * p
        unit = jnp.where((row == col) & (member == t), -1.0, 0.0)
        side = jnp.where(owner, unit, own[lo:hi, :])
        for s in range(t + 1, TICKS):
            side = minus_dot(side, raw[s, lo:hi, :], w_out[s * p : (s + 1) * p, :])
        w_out[lo:hi, :] = dot3((inv[0, t], inv[1, t]), split(side)).astype(jnp.bfloat16)
    wait_all(stores)


def pivot_rows(member, front, bufs):
    order, width = front.shape
    p, rows = P_SIZE, TICKS * P_SIZE
    counts = tuple(len(b) for b in bufs)
    return pl.pallas_call(
        functools.partial(pivot_kernel, counts, width),
        name="pivot_rows",
        out_shape=(
            jax.ShapeDtypeStruct((order, width), jnp.float32),
            jax.ShapeDtypeStruct((rows, width), jnp.bfloat16),
        ),
        in_specs=[SMEM, ANY] + [ANY] * sum(counts),
        out_specs=(ANY, VMEM),
        scratch_shapes=[
            pltpu.VMEM((TICKS, rows, p), jnp.bfloat16),
            pltpu.VMEM((TICKS, rows, p), jnp.float32),
            pltpu.VMEM((rows, width), jnp.float32),
            pltpu.VMEM((2, TICKS, p, p), jnp.bfloat16),
            pltpu.SemaphoreType.DMA((4,)),
            pltpu.SemaphoreType.DMA((2,)),
            pltpu.SemaphoreType.DMA((TICKS,)),
        ],
    )(member, front, *bufs[0], *bufs[1])


def windows(ranges, rows):
    chunks = []
    for lo in range(0, rows, CHUNK):
        n = min(CHUNK, rows - lo)
        pieces = []
        for src, dst, count in ranges:
            first, last = max(lo, dst), min(lo + n, dst + count)
            if first < last:
                pieces.append((src + first - dst, first, last - first))
        chunks.append((lo, n, pieces))
    return chunks


def other_kernel(counts, chunks, tail, member_ref, dest_ref, slot_ref, w, front, out_in, *rest):
    firsts, lasts = rest[: counts[0]], rest[counts[0] : sum(counts)]
    if tail:
        out, outgoing, raw, base, sems, base_sems = rest[sum(counts) :]
    else:
        out, raw, base, sems, base_sems = rest[sum(counts) :]
    member = member_ref[0]
    width = base.shape[1]
    waits = []
    for number, (lo, n, pieces) in enumerate(chunks):
        copies = start_first(member, firsts, raw, sems.at[number], lo, n)
        copies += start_last(member, lasts, raw, sems.at[number, TICKS - 1], lo, n)
        for i, (src, dst, count) in enumerate(pieces):
            copies.append(
                pltpu.make_async_copy(
                    front.at[pl.ds(src, count), :], base.at[pl.ds(dst, count), :], base_sems.at[number, i]
                )
            )
            copies[-1].start()
        waits.append(copies)
    keep = (member >= TICKS) | (lax.broadcasted_iota(jnp.int32, (CHUNK, width), 1) >= P_SIZE)
    stores = []
    for number, (lo, n, pieces) in enumerate(chunks):
        wait_all(waits[number])
        at = pl.ds(lo, n)
        total = jnp.where(keep[:n], base[at, :], 0.0)
        for s in range(TICKS):
            total = minus_dot(total, raw[s, at, :], w[s * P_SIZE : (s + 1) * P_SIZE, :])
        base[at, :] = total
        if tail:
            cont = jnp.where(keep[:n], total, 0.0).astype(jnp.bfloat16)
            for first in range(0, n, RB):
                block = (lo + first) // RB
                outgoing[dest_ref[block], slot_ref[block]] = cont[first : first + RB]
        for i, (src, dst, count) in enumerate(pieces):
            stores.append(
                pltpu.make_async_copy(
                    base.at[pl.ds(dst, count), :], out.at[pl.ds(src, count), :], base_sems.at[number, i]
                )
            )
            stores[-1].start()
    wait_all(stores)


def other_rows(member, dest, slot, w, front, out, bufs, ranges, groups=0):
    order, width = front.shape
    rows = sum(n for _, _, n in ranges)
    shapes = [jax.ShapeDtypeStruct((order, width), jnp.float32)]
    specs = [ANY]
    if groups:
        shapes.append(jax.ShapeDtypeStruct((groups, CAP, RB, width), jnp.bfloat16))
        specs.append(VMEM)
    counts = tuple(len(b) for b in bufs)
    chunks = windows(ranges, rows)
    return pl.pallas_call(
        functools.partial(other_kernel, counts, chunks, bool(groups)),
        name="tail_rows" if groups else "middle_rows",
        out_shape=tuple(shapes),
        in_specs=[SMEM, SMEM, SMEM, VMEM, ANY, ANY] + [ANY] * sum(counts),
        out_specs=tuple(specs),
        input_output_aliases={5: 0},
        scratch_shapes=[
            pltpu.VMEM((TICKS, rows, P_SIZE), jnp.bfloat16),
            pltpu.VMEM((rows, width), jnp.float32),
            pltpu.SemaphoreType.DMA((len(chunks), TICKS)),
            pltpu.SemaphoreType.DMA((len(chunks), max(len(c[2]) for c in chunks))),
        ],
    )(member, dest, slot, w, front, out, *bufs[0], *bufs[1])


def rows_of(slab):
    return pl.ds(pl.multiple_of(slab * P_SIZE, P_SIZE), P_SIZE)


def partial_kernel(n_bufs, chunks, member_ref, w, front, *rest):
    bufs = rest[:n_bufs]
    base, raw, sems, base_sems = rest[n_bufs:]
    member = member_ref[0]
    width = base.shape[1]
    keep = (member >= TICKS) | (lax.broadcasted_iota(jnp.int32, (CHUNK, width), 1) >= P_SIZE)
    waits = []
    for number, (lo, n, pieces) in enumerate(chunks):
        at = pl.ds(lo, n)
        if n_bufs == 1:
            slabs = tuple(range(TICKS - 2))
            sources = [(bufs[0].at[slab], slab) for slab in slabs]
        else:
            sources = placed_slabs(member, bufs)
            slabs = tuple(slab for _, slab in sources)
        copies = [
            pltpu.make_async_copy(ref.at[at], raw.at[slab, at], sems.at[number, i])
            for i, (ref, slab) in enumerate(sources)
        ]
        copies += [
            pltpu.make_async_copy(
                front.at[pl.ds(src, count), :], base.at[pl.ds(dst, count), :], base_sems.at[number, i]
            )
            for i, (src, dst, count) in enumerate(pieces)
        ]
        for copy in copies:
            copy.start()
        waits.append(copies)
    for number, (lo, n, pieces) in enumerate(chunks):
        wait_all(waits[number])
        at = pl.ds(lo, n)
        total = jnp.where(keep[:n], base[at, :], 0.0)
        for slab in slabs:
            total = minus_dot(total, raw[slab, at, :], w[rows_of(slab), :])
        base[at, :] = total


def final_kernel(counts, chunks, gathered, member_ref, w, base, out_in, *rest):
    firsts, lasts = rest[: counts[0]], rest[counts[0] : sum(counts)]
    out, raw, held, sems, store_sems = rest[sum(counts) :]
    member = member_ref[0]
    waits = []
    for number, (lo, n, pieces) in enumerate(chunks):
        at = pl.ds(lo, n)
        if gathered:
            ref, slab = firsts[0].at[TICKS - 2], TICKS - 2
        else:
            ref, slab = firsts[0], places(member)[-1]
        copy = pltpu.make_async_copy(ref.at[at], raw.at[slab, at], sems.at[number, 0])
        copy.start()
        waits.append([copy] + start_last(member, lasts, raw, sems.at[number, 1], lo, n))
    stores = []
    for number, (lo, n, pieces) in enumerate(chunks):
        wait_all(waits[number])
        at = pl.ds(lo, n)
        total = base[at, :]
        for s in (slab, TICKS - 1):
            total = minus_dot(total, raw[s, at, :], w[rows_of(s), :])
        held[at, :] = total
        for i, (src, dst, count) in enumerate(pieces):
            stores.append(
                pltpu.make_async_copy(
                    held.at[pl.ds(dst, count), :], out.at[pl.ds(src, count), :], store_sems.at[number, i]
                )
            )
            stores[-1].start()
    wait_all(stores)


def middle_rows(member, w, front, out, bufs, ranges):
    order, width = front.shape
    rows = sum(n for _, _, n in ranges)
    chunks = windows(ranges, rows)
    pieces = max(len(c[2]) for c in chunks)
    counts = tuple(len(b) for b in bufs)
    early = bufs[0] if counts[0] == 1 else bufs[0][:-1]
    base = pl.pallas_call(
        functools.partial(partial_kernel, len(early), chunks),
        name="partial_rows",
        out_shape=jax.ShapeDtypeStruct((rows, width), jnp.float32),
        in_specs=[SMEM, VMEM, ANY] + [ANY] * len(early),
        out_specs=VMEM,
        scratch_shapes=[
            pltpu.VMEM((TICKS, rows, P_SIZE), jnp.bfloat16),
            pltpu.SemaphoreType.DMA((len(chunks), TICKS)),
            pltpu.SemaphoreType.DMA((len(chunks), pieces)),
        ],
    )(member, w, front, *early)
    late = bufs[0] if counts[0] == 1 else bufs[0][-1:]
    return pl.pallas_call(
        functools.partial(final_kernel, (len(late), counts[1]), chunks, counts[0] == 1),
        name="middle_rows",
        out_shape=jax.ShapeDtypeStruct((order, width), jnp.float32),
        in_specs=[SMEM, VMEM, VMEM, ANY] + [ANY] * (len(late) + counts[1]),
        out_specs=ANY,
        input_output_aliases={3: 0},
        scratch_shapes=[
            pltpu.VMEM((TICKS, rows, P_SIZE), jnp.bfloat16),
            pltpu.VMEM((rows, width), jnp.float32),
            pltpu.SemaphoreType.DMA((len(chunks), 2)),
            pltpu.SemaphoreType.DMA((len(chunks), pieces)),
        ],
    )(member, w, base, out, *late, *bufs[1])


def routes(parent_group, row_block):
    groups = lax.axis_size("front")
    dest = parent_group.reshape(NB)
    target = row_block.reshape(NB)
    number = jnp.arange(NB)
    earlier = (dest[None, :] == dest[:, None]) & (number[None, :] < number[:, None])
    slot = jnp.sum(earlier.astype(jnp.int32), axis=1)
    pick = (dest[None, None, :] == jnp.arange(groups, dtype=jnp.int32)[:, None, None]) & (
        slot[None, None, :] == jnp.arange(CAP, dtype=jnp.int32)[None, :, None]
    )
    address = jnp.sum(jnp.where(pick, target[None, None, :] + 1, 0), axis=2) - 1
    received = lax.all_to_all(address, "front", split_axis=0, concat_axis=0, tiled=True)
    return dest, slot, received.reshape(groups * CAP)


def add_kernel(address_ref, incoming, base, out):
    out[...] = base[...]
    for i in range(incoming.shape[0]):
        to = address_ref[i]

        @pl.when(to >= 0)
        def _(i=i, to=to):
            at = pl.ds(pl.multiple_of(to * RB, RB), RB)
            out[at, :] = out[at, :] + incoming[i].astype(jnp.float32)


def add_blocks(address, incoming, parent_base):
    groups, cap, rows, width = incoming.shape
    return pl.pallas_call(
        add_kernel,
        name="add_blocks",
        out_shape=jax.ShapeDtypeStruct(parent_base.shape, parent_base.dtype),
        in_specs=[SMEM, VMEM, VMEM],
        out_specs=VMEM,
    )(address, incoming.reshape(groups * cap, rows, width), parent_base)


def local(front, parent_group, row_block, parent_base):
    order, width = front.shape
    member = lax.axis_index("blk")
    holder = member.reshape(1).astype(jnp.int32)
    p, top = P_SIZE, TICKS * width
    tail_n = NB * RB
    tail_at = order - tail_n
    pivot_ranges = [(t * width, p) for t in range(TICKS)]
    tail_ranges = [(tail_at, tail_n)]
    middle_ranges = [(t * width + p, width - p) for t in range(TICKS)]
    if tail_at > top:
        middle_ranges.append((top, tail_at - top))
    middle, at = [], 0
    for start, count in middle_ranges:
        middle.append((start, at, count))
        at += count
    if lax.axis_size("blk") == 8:
        (own_p,) = pack(front, [pivot_ranges])
        own_t, own_m = pack(front, [tail_ranges, middle_ranges])
        half = own_p.shape[0] // 2
        sets = relay((own_p, own_t, own_m, (own_p[:half], own_p[half:])), member)
    else:
        own_p, own_t, own_m = pack(front, [pivot_ranges, tail_ranges, middle_ranges])
        sets = tuple(((lax.all_gather(s, "blk")[:TICKS],),) * 2 for s in (own_p, own_t, own_m))
    dest, slot, address = routes(parent_group, row_block)
    out, w = pivot_rows(holder, front, sets[0])
    out, outgoing = other_rows(
        holder, dest, slot, w, front, out, sets[1], [(tail_at, 0, tail_n)], lax.axis_size("front")
    )
    incoming = lax.all_to_all(outgoing, "front", split_axis=0, concat_axis=0, tiled=True)
    factored = middle_rows(holder, w, front, out, sets[2], middle)
    assembled = add_blocks(address, incoming, parent_base)
    return (factored, assembled)


def solution(mesh):
    placed = (
        P("front", "blk"),
        P("front", "blk", None, None),
        P("front", "blk", None),
        P("front", "blk"),
    )
    return jax.shard_map(
        local,
        mesh=mesh,
        in_specs=placed,
        out_specs=(P("front", "blk"), P("front", "blk")),
        check_vma=False,
    )
```

```python
import functools

import jax
import jax.numpy as jnp
from jax import lax
from jax.experimental import pallas as pl
from jax.experimental.pallas import tpu as pltpu
from jax.sharding import PartitionSpec as P


P_SIZE = 256
TICKS = 5
NEWTON = 2
RB = 128
NB = 6
CAP = 2
CHUNK = 256
ANY = pl.BlockSpec(memory_space=pl.ANY)
SMEM = pl.BlockSpec(memory_space=pltpu.SMEM)
VMEM = pl.BlockSpec(memory_space=pltpu.VMEM)


def permute(value, pairs):
    return lax.ppermute(value, "blk", pairs)


def relay(parts, member):
    across = [(m, m ^ 1) for m in range(8)]
    near = [(m, m ^ 2) for m in range(8)]
    distant = [(m, m + 4) for m in range(4)]
    beside, back, mid, up = [(4, 5)], [(4, 0), (5, 1)], [(4, 2), (5, 3)], [(4, 6), (5, 7)]
    level = member // 2
    a, b, c, e_halves = parts

    def slabs(own):
        cur = jnp.where(member < 4, own, permute(own, distant))
        far = permute(cur, near)
        over = permute(cur, across)
        return cur, far, over, permute(far, across)

    def halves(low, high):
        half = jnp.where(member == 5, permute(high, beside), low)
        to_up = permute(half, up)
        to_back = permute(half, back)
        to_mid = permute(half, mid)
        half = jnp.where(level == 2, half, jnp.where(level == 3, to_up, jnp.where(level == 0, to_back, to_mid)))
        return half, permute(half, across)

    def whole(own):
        own = lax.optimization_barrier(own)
        rows = jnp.where(member == 5, permute(own, beside), own)
        to_up = permute(rows, up)
        to_back = permute(rows, back)
        to_mid = permute(rows, mid)
        return to_back, to_mid, rows, to_up

    return ((slabs(a), halves(*e_halves)), (slabs(b), whole(b)), (slabs(c), whole(c)))


def places(member):
    x = lax.rem(member, 2)
    even = lax.rem(lax.div(member, 2), 2) == 0
    near, far = jnp.where(even, x, 2 + x), jnp.where(even, 2 + x, x)
    over, overfar = jnp.where(even, 1 - x, 3 - x), jnp.where(even, 3 - x, 1 - x)
    return near, far, over, overfar


def placed_slabs(member, refs):
    return tuple(zip(refs, places(member)))


def start_first(member, refs, target, sems, lo, n):
    at = pl.ds(lo, n)
    if len(refs) == 1:
        most = pl.ds(0, TICKS - 1)
        copies = [pltpu.make_async_copy(refs[0].at[most, at], target.at[most, at], sems.at[0])]
    else:
        copies = [
            pltpu.make_async_copy(ref.at[at], target.at[slab, at], sems.at[i])
            for i, (ref, slab) in enumerate(placed_slabs(member, refs))
        ]
    for copy in copies:
        copy.start()
    return copies


def start_last(member, refs, target, sem, lo, n):
    at = pl.ds(lo, n)
    if len(refs) == 1:
        copies = [pltpu.make_async_copy(refs[0].at[TICKS - 1, at], target.at[TICKS - 1, at], sem)]
        copies[0].start()
        return copies
    copies = [pltpu.make_async_copy(ref.at[at], target.at[TICKS - 1, at], sem) for ref in refs]
    for level, copy in enumerate(copies):
        pl.when(lax.div(member, 2) == level)(copy.start)
    return copies[:1]


def start_halves(member, refs, target, sems, rows):
    if len(refs) == 1:
        return start_last(member, refs, target, sems.at[0], 0, rows)
    half, overhalf = refs
    x, n = lax.rem(member, 2), rows // 2

    def copy(ref, number):
        return pltpu.make_async_copy(ref, target.at[TICKS - 1, pl.ds(number * n, n)], sems.at[number])

    for which in (0, 1):

        @pl.when(x == which)
        def _(which=which):
            copy(half, which).start()
            copy(overhalf, 1 - which).start()

    return [copy(half, 0), copy(half, 1)]


def wait_all(copies):
    for copy in copies:
        copy.wait()


def pack_kernel(pieces, front, *rest):
    outs, (held, sems) = rest[: len(pieces)], rest[len(pieces) :]
    copies, at = [], 0
    for ranges in pieces:
        for start, count in ranges:
            copies.append(
                pltpu.make_async_copy(
                    front.at[pl.ds(start, count), pl.ds(0, P_SIZE)], held.at[pl.ds(at, count), :], sems.at[len(copies)]
                )
            )
            copies[-1].start()
            at += count
    at, number = 0, 0
    for ranges, out in zip(pieces, outs):
        to = 0
        for _, count in ranges:
            copies[number].wait()
            out[pl.ds(to, count), :] = held[pl.ds(at, count), :].astype(jnp.bfloat16)
            at, to, number = at + count, to + count, number + 1


def pack(front, pieces):
    sizes = [sum(n for _, n in ranges) for ranges in pieces]
    return pl.pallas_call(
        functools.partial(pack_kernel, pieces),
        out_shape=tuple(jax.ShapeDtypeStruct((n, P_SIZE), jnp.bfloat16) for n in sizes),
        in_specs=[ANY],
        out_specs=(VMEM,) * len(sizes),
        scratch_shapes=[
            pltpu.VMEM((sum(sizes), P_SIZE), jnp.float32),
            pltpu.SemaphoreType.DMA((sum(len(r) for r in pieces),)),
        ],
    )(front)


def split(value):
    high = value.astype(jnp.bfloat16)
    return high, (value - high.astype(jnp.float32)).astype(jnp.bfloat16)


def dot3(left, right):
    (left_high, left_low), (right_high, right_low) = left, right
    dot = functools.partial(jnp.dot, preferred_element_type=jnp.float32)
    return dot(left_high, right_high) + (dot(left_low, right_high) + dot(left_high, right_low))


def dot2(left, right):
    dot = functools.partial(jnp.dot, preferred_element_type=jnp.float32)
    return dot(left, right[0]) + dot(left, right[1])


def diagonal_inverse(block):
    size = block.shape[0]
    row = lax.broadcasted_iota(jnp.int32, (size, size), 0)
    col = lax.broadcasted_iota(jnp.int32, (size, size), 1)
    on = row == col
    kept = jnp.where(on, block, 0.0)
    down = 1.0 / jnp.sum(kept, axis=1, keepdims=True)
    right = 1.0 / jnp.sum(kept, axis=0, keepdims=True)
    twice = jnp.where(on, 2.0, 0.0)
    parts = split(down * (twice - block * right))
    block_parts = split(block)
    for _ in range(NEWTON - 1):
        parts = split(dot3(parts, split(twice - dot3(block_parts, parts))))
    return parts


def minus_dot(value, left, right):
    return value - jnp.dot(left, right, preferred_element_type=jnp.float32)


def minus_dot(value, left, right):
    return value - jnp.dot(left, right, preferred_element_type=jnp.float32)


def pivot_kernel(counts, width, member_ref, front, *rest):
    firsts, lasts = rest[: counts[0]], rest[counts[0] : sum(counts)]
    out, w_out, raw, mat, own, inv, sems, last_sems, own_sems = rest[sum(counts) :]
    member = member_ref[0]
    p, rows = P_SIZE, TICKS * P_SIZE
    copies = start_first(member, firsts, raw, sems, 0, rows)
    copies += start_halves(member, lasts, raw, last_sems, rows)
    loads = [
        pltpu.make_async_copy(
            front.at[pl.ds(t * width, p), :], own.at[pl.ds(t * p, p), :], own_sems.at[t]
        )
        for t in range(TICKS)
    ]
    for load in loads:
        load.start()
    wait_all(copies)
    x = diagonal_inverse(raw[0, :p, :].astype(jnp.float32))
    wait_all(loads)
    for t in range(TICKS):
        lo, below = t * p, (t + 1) * p
        inv[0, t], inv[1, t] = x
        if below == rows:
            break
        column = mat[t, below:, :] if t else raw[t, below:, :]
        mult = dot3(split(column), x) if t else dot2(column, x)
        panel = mult.astype(jnp.bfloat16)
        for s in range(t + 1, TICKS):
            if t:
                urows = mat[s, lo:below, :].astype(jnp.bfloat16)
                raw[s, lo:below, :] = urows
                rest_rows = mat[s, below:, :]
            else:
                urows = raw[s, lo:below, :]
                rest_rows = raw[s, below:, :].astype(jnp.float32)
            mat[s, below:, :] = minus_dot(rest_rows, panel, urows)
            if s == t + 1:
                x = diagonal_inverse(mat[s, below : below + p, :])
        urows = own[lo:below, :].astype(jnp.bfloat16)
        own[below:, p:] = minus_dot(own[below:, p:], panel, urows[:, p:])
        left = own[below:, :p]
        live = (member >= TICKS) | (member > t)
        changed = jnp.where(live, minus_dot(left, panel, urows[:, :p]), left)
        own[below:, :p] = jnp.where(member == t, mult, changed)

    stores = [
        pltpu.make_async_copy(
            own.at[pl.ds(t * p, p), :], out.at[pl.ds(t * width, p), :], own_sems.at[t]
        )
        for t in range(TICKS)
    ]
    for store in stores:
        store.start()
    row = lax.broadcasted_iota(jnp.int32, (p, width), 0)
    col = lax.broadcasted_iota(jnp.int32, (p, width), 1)
    owner = (member < TICKS) & (col < p)
    for t in reversed(range(TICKS)):
        lo, hi = t * p, (t + 1) * p
        unit = jnp.where((row == col) & (member == t), -1.0, 0.0)
        side = jnp.where(owner, unit, own[lo:hi, :])
        for s in range(t + 1, TICKS):
            side = minus_dot(side, raw[s, lo:hi, :], w_out[s * p : (s + 1) * p, :])
        w_out[lo:hi, :] = dot3((inv[0, t], inv[1, t]), split(side)).astype(jnp.bfloat16)
    wait_all(stores)


def pivot_rows(member, front, bufs):
    order, width = front.shape
    p, rows = P_SIZE, TICKS * P_SIZE
    counts = tuple(len(b) for b in bufs)
    return pl.pallas_call(
        functools.partial(pivot_kernel, counts, width),
        name="pivot_rows",
        out_shape=(
            jax.ShapeDtypeStruct((order, width), jnp.float32),
            jax.ShapeDtypeStruct((rows, width), jnp.bfloat16),
        ),
        in_specs=[SMEM, ANY] + [ANY] * sum(counts),
        out_specs=(ANY, VMEM),
        scratch_shapes=[
            pltpu.VMEM((TICKS, rows, p), jnp.bfloat16),
            pltpu.VMEM((TICKS, rows, p), jnp.float32),
            pltpu.VMEM((rows, width), jnp.float32),
            pltpu.VMEM((2, TICKS, p, p), jnp.bfloat16),
            pltpu.SemaphoreType.DMA((4,)),
            pltpu.SemaphoreType.DMA((2,)),
            pltpu.SemaphoreType.DMA((TICKS,)),
        ],
    )(member, front, *bufs[0], *bufs[1])


def windows(ranges, rows):
    chunks = []
    for lo in range(0, rows, CHUNK):
        n = min(CHUNK, rows - lo)
        pieces = []
        for src, dst, count in ranges:
            first, last = max(lo, dst), min(lo + n, dst + count)
            if first < last:
                pieces.append((src + first - dst, first, last - first))
        chunks.append((lo, n, pieces))
    return chunks


def other_kernel(counts, chunks, tail, member_ref, dest_ref, slot_ref, w, front, out_in, *rest):
    firsts, lasts = rest[: counts[0]], rest[counts[0] : sum(counts)]
    if tail:
        out, outgoing, raw, base, sems, base_sems = rest[sum(counts) :]
    else:
        out, raw, base, sems, base_sems = rest[sum(counts) :]
    member = member_ref[0]
    width = base.shape[1]
    waits = []
    for number, (lo, n, pieces) in enumerate(chunks):
        copies = start_first(member, firsts, raw, sems.at[number], lo, n)
        copies += start_last(member, lasts, raw, sems.at[number, TICKS - 1], lo, n)
        for i, (src, dst, count) in enumerate(pieces):
            copies.append(
                pltpu.make_async_copy(
                    front.at[pl.ds(src, count), :], base.at[pl.ds(dst, count), :], base_sems.at[number, i]
                )
            )
            copies[-1].start()
        waits.append(copies)
    keep = (member >= TICKS) | (lax.broadcasted_iota(jnp.int32, (CHUNK, width), 1) >= P_SIZE)
    stores = []
    for number, (lo, n, pieces) in enumerate(chunks):
        wait_all(waits[number])
        at = pl.ds(lo, n)
        total = jnp.where(keep[:n], base[at, :], 0.0)
        for s in range(TICKS):
            total = minus_dot(total, raw[s, at, :], w[s * P_SIZE : (s + 1) * P_SIZE, :])
        base[at, :] = total
        if tail:
            cont = jnp.where(keep[:n], total, 0.0).astype(jnp.bfloat16)
            for first in range(0, n, RB):
                block = (lo + first) // RB
                outgoing[dest_ref[block], slot_ref[block]] = cont[first : first + RB]
        for i, (src, dst, count) in enumerate(pieces):
            stores.append(
                pltpu.make_async_copy(
                    base.at[pl.ds(dst, count), :], out.at[pl.ds(src, count), :], base_sems.at[number, i]
                )
            )
            stores[-1].start()
    wait_all(stores)


def other_rows(member, dest, slot, w, front, out, bufs, ranges, groups=0):
    order, width = front.shape
    rows = sum(n for _, _, n in ranges)
    shapes = [jax.ShapeDtypeStruct((order, width), jnp.float32)]
    specs = [ANY]
    if groups:
        shapes.append(jax.ShapeDtypeStruct((groups, CAP, RB, width), jnp.bfloat16))
        specs.append(VMEM)
    counts = tuple(len(b) for b in bufs)
    chunks = windows(ranges, rows)
    return pl.pallas_call(
        functools.partial(other_kernel, counts, chunks, bool(groups)),
        name="tail_rows" if groups else "middle_rows",
        out_shape=tuple(shapes),
        in_specs=[SMEM, SMEM, SMEM, VMEM, ANY, ANY] + [ANY] * sum(counts),
        out_specs=tuple(specs),
        input_output_aliases={5: 0},
        scratch_shapes=[
            pltpu.VMEM((TICKS, rows, P_SIZE), jnp.bfloat16),
            pltpu.VMEM((rows, width), jnp.float32),
            pltpu.SemaphoreType.DMA((len(chunks), TICKS)),
            pltpu.SemaphoreType.DMA((len(chunks), max(len(c[2]) for c in chunks))),
        ],
    )(member, dest, slot, w, front, out, *bufs[0], *bufs[1])


def rows_of(slab):
    return pl.ds(pl.multiple_of(slab * P_SIZE, P_SIZE), P_SIZE)


def partial_kernel(n_bufs, chunks, member_ref, w, front, *rest):
    bufs = rest[:n_bufs]
    base, raw, sems, base_sems = rest[n_bufs:]
    member = member_ref[0]
    width = base.shape[1]
    keep = (member >= TICKS) | (lax.broadcasted_iota(jnp.int32, (CHUNK, width), 1) >= P_SIZE)
    waits = []
    for number, (lo, n, pieces) in enumerate(chunks):
        at = pl.ds(lo, n)
        if n_bufs == 1:
            slabs = tuple(range(TICKS - 2))
            sources = [(bufs[0].at[slab], slab) for slab in slabs]
        else:
            sources = placed_slabs(member, bufs)
            slabs = tuple(slab for _, slab in sources)
        copies = [
            pltpu.make_async_copy(ref.at[at], raw.at[slab, at], sems.at[number, i])
            for i, (ref, slab) in enumerate(sources)
        ]
        copies += [
            pltpu.make_async_copy(
                front.at[pl.ds(src, count), :], base.at[pl.ds(dst, count), :], base_sems.at[number, i]
            )
            for i, (src, dst, count) in enumerate(pieces)
        ]
        for copy in copies:
            copy.start()
        waits.append(copies)
    for number, (lo, n, pieces) in enumerate(chunks):
        wait_all(waits[number])
        at = pl.ds(lo, n)
        total = jnp.where(keep[:n], base[at, :], 0.0)
        for slab in slabs:
            total = minus_dot(total, raw[slab, at, :], w[rows_of(slab), :])
        base[at, :] = total


def final_kernel(counts, chunks, gathered, member_ref, w, base, out_in, *rest):
    firsts, lasts = rest[: counts[0]], rest[counts[0] : sum(counts)]
    out, raw, held, sems, store_sems = rest[sum(counts) :]
    member = member_ref[0]
    waits = []
    for number, (lo, n, pieces) in enumerate(chunks):
        at = pl.ds(lo, n)
        if gathered:
            ref, slab = firsts[0].at[TICKS - 2], TICKS - 2
        else:
            ref, slab = firsts[0], places(member)[-1]
        copy = pltpu.make_async_copy(ref.at[at], raw.at[slab, at], sems.at[number, 0])
        copy.start()
        waits.append([copy] + start_last(member, lasts, raw, sems.at[number, 1], lo, n))
    stores = []
    for number, (lo, n, pieces) in enumerate(chunks):
        wait_all(waits[number])
        at = pl.ds(lo, n)
        total = base[at, :]
        for s in (slab, TICKS - 1):
            total = minus_dot(total, raw[s, at, :], w[rows_of(s), :])
        held[at, :] = total
        for i, (src, dst, count) in enumerate(pieces):
            stores.append(
                pltpu.make_async_copy(
                    held.at[pl.ds(dst, count), :], out.at[pl.ds(src, count), :], store_sems.at[number, i]
                )
            )
            stores[-1].start()
    wait_all(stores)


def middle_rows(member, w, front, out, bufs, ranges):
    order, width = front.shape
    rows = sum(n for _, _, n in ranges)
    chunks = windows(ranges, rows)
    pieces = max(len(c[2]) for c in chunks)
    counts = tuple(len(b) for b in bufs)
    early = bufs[0] if counts[0] == 1 else bufs[0][:-1]
    base = pl.pallas_call(
        functools.partial(partial_kernel, len(early), chunks),
        name="partial_rows",
        out_shape=jax.ShapeDtypeStruct((rows, width), jnp.float32),
        in_specs=[SMEM, VMEM, ANY] + [ANY] * len(early),
        out_specs=VMEM,
        scratch_shapes=[
            pltpu.VMEM((TICKS, rows, P_SIZE), jnp.bfloat16),
            pltpu.SemaphoreType.DMA((len(chunks), TICKS)),
            pltpu.SemaphoreType.DMA((len(chunks), pieces)),
        ],
    )(member, w, front, *early)
    late = bufs[0] if counts[0] == 1 else bufs[0][-1:]
    return pl.pallas_call(
        functools.partial(final_kernel, (len(late), counts[1]), chunks, counts[0] == 1),
        name="middle_rows",
        out_shape=jax.ShapeDtypeStruct((order, width), jnp.float32),
        in_specs=[SMEM, VMEM, VMEM, ANY] + [ANY] * (len(late) + counts[1]),
        out_specs=ANY,
        input_output_aliases={3: 0},
        scratch_shapes=[
            pltpu.VMEM((TICKS, rows, P_SIZE), jnp.bfloat16),
            pltpu.VMEM((rows, width), jnp.float32),
            pltpu.SemaphoreType.DMA((len(chunks), 2)),
            pltpu.SemaphoreType.DMA((len(chunks), pieces)),
        ],
    )(member, w, base, out, *late, *bufs[1])


def routes(parent_group, row_block):
    groups = lax.axis_size("front")
    dest = parent_group.reshape(NB)
    target = row_block.reshape(NB)
    number = jnp.arange(NB)
    earlier = (dest[None, :] == dest[:, None]) & (number[None, :] < number[:, None])
    slot = jnp.sum(earlier.astype(jnp.int32), axis=1)
    pick = (dest[None, None, :] == jnp.arange(groups, dtype=jnp.int32)[:, None, None]) & (
        slot[None, None, :] == jnp.arange(CAP, dtype=jnp.int32)[None, :, None]
    )
    address = jnp.sum(jnp.where(pick, target[None, None, :] + 1, 0), axis=2) - 1
    received = lax.all_to_all(address, "front", split_axis=0, concat_axis=0, tiled=True)
    return dest, slot, received.reshape(groups, CAP)


def add_kernel(address_ref, incoming, base, out, held, sems):
    rows = incoming.shape[1]
    stores = []
    for block in range(base.shape[0] // rows):
        at = pl.ds(block * rows, rows)
        held[at, :] = base[at, :]
        for i in range(incoming.shape[0]):

            @pl.when(address_ref[i // CAP, i % CAP] == block)
            def _(i=i, at=at):
                held[at, :] = held[at, :] + incoming[i].astype(jnp.float32)

        stores.append(pltpu.make_async_copy(held.at[at, :], out.at[at, :], sems.at[block]))
        stores[-1].start()
    wait_all(stores)


def add_blocks(address, incoming, parent_base):
    groups, cap, rows, width = incoming.shape
    return pl.pallas_call(
        add_kernel,
        name="add_blocks",
        out_shape=jax.ShapeDtypeStruct(parent_base.shape, parent_base.dtype),
        in_specs=[SMEM, VMEM, VMEM],
        out_specs=ANY,
        scratch_shapes=[
            pltpu.VMEM(parent_base.shape, jnp.float32),
            pltpu.SemaphoreType.DMA((parent_base.shape[0] // rows,)),
        ],
    )(address, incoming.reshape(groups * cap, rows, width), parent_base)


def local(front, parent_group, row_block, parent_base):
    order, width = front.shape
    member = lax.axis_index("blk")
    holder = member.reshape(1).astype(jnp.int32)
    p, top = P_SIZE, TICKS * width
    tail_n = NB * RB
    tail_at = order - tail_n
    pivot_ranges = [(t * width, p) for t in range(TICKS)]
    tail_ranges = [(tail_at, tail_n)]
    middle_ranges = [(t * width + p, width - p) for t in range(TICKS)]
    if tail_at > top:
        middle_ranges.append((top, tail_at - top))
    middle, at = [], 0
    for start, count in middle_ranges:
        middle.append((start, at, count))
        at += count
    if lax.axis_size("blk") == 8:
        (own_p,) = pack(front, [pivot_ranges])
        own_t, own_m = pack(front, [tail_ranges, middle_ranges])
        half = own_p.shape[0] // 2
        sets = relay((own_p, own_t, own_m, (own_p[:half], own_p[half:])), member)
    else:
        own_p, own_t, own_m = pack(front, [pivot_ranges, tail_ranges, middle_ranges])
        sets = tuple(((lax.all_gather(s, "blk")[:TICKS],),) * 2 for s in (own_p, own_t, own_m))
    dest, slot, address = routes(parent_group, row_block)
    out, w = pivot_rows(holder, front, sets[0])
    out, outgoing = other_rows(
        holder, dest, slot, w, front, out, sets[1], [(tail_at, 0, tail_n)], lax.axis_size("front")
    )
    incoming = lax.all_to_all(outgoing, "front", split_axis=0, concat_axis=0, tiled=True)
    factored = middle_rows(holder, w, front, out, sets[2], middle)
    assembled = add_blocks(address, incoming, parent_base)
    return (factored, assembled)


def solution(mesh):
    placed = (
        P("front", "blk"),
        P("front", "blk", None, None),
        P("front", "blk", None),
        P("front", "blk"),
    )
    return jax.shard_map(
        local,
        mesh=mesh,
        in_specs=placed,
        out_specs=(P("front", "blk"), P("front", "blk")),
        check_vma=False,
    )
```
